128 devices in a mesh: sat: 16 (over x, z), dop: 8 (over y, core).
Axes of the slice: x: 4, y: 4, z: 4, core: 2. Of those that a mesh axis runs over, the one named last changes fastest.
Arguments:
- samples: float32 [2, 8192], P(None, ('sat', 'dop')), may hold values from -6 to 6
- code_chips: int32 [48, 4092], P('sat'), may hold values from -1 to 1, as said below
- centers: int32 [48], P('sat'), may hold values from -20 to 20
- widths: int32 [48], P('sat'), may hold values from 1 to 8
Outputs:
- ratio: float32 [48, 128, 8192], P('sat', None, 'dop')
The draws below stay inside these ranges and needn't reach their ends.
Inputs may be any that keep to these rules, and one draw needn't show every extreme that they name: `code_chips`: every entry is -1 or 1.
All inputs are finite; a program needn't handle non-finite values.
Results may differ from the reference program's by a relative error of at most 0.0003.
Values sent between devices are 32-bit elements; how exact they have to be, the bound alone decides.
A program may use at most 64 MiB of HBM per device.

```python
import math
import jax
import jax.numpy as jnp
from jax import lax

SAMPLES = 8192
CHIPS = 4092
DOP = 128
WMAX = 8
SATS = 48


def draw_code_chips(key, part):
    return 2 * jax.random.randint(key, (SATS, CHIPS), 0, 2, dtype=jnp.int32) - 1


def set_ends(array, rng, low, high):
    shape = array.shape
    spot = [jax.random.randint(jax.random.fold_in(rng, axis), (), 0, shape[axis]) for axis in range(len(shape))]
    array = array.at[tuple(spot)].set(low)
    longest = shape.index(max(shape))
    spot[longest] = (spot[longest] + 1) % shape[longest]
    return array.at[tuple(spot)].set(high)


def steps_of(rng, dims, shards, smallest, top_value):
    def one(dim, shards_of):
        draws = jax.random.uniform(jax.random.fold_in(jax.random.fold_in(rng, 6), dim), (shards_of,), jnp.float32, smallest / len(shards), top_value / len(shards))
        return jnp.repeat(jnp.exp(draws), dims[dim] // shards_of).reshape((-1,) + (1,) * (len(dims) - dim - 1))

    loudness = one(*shards[0])
    for cut in shards[1:]:
        loudness = loudness * one(*cut)
    return loudness


def normal_values(own_key, dims, deviation, most, split=(), kind=jnp.bfloat16):
    result = deviation * jax.random.normal(own_key, dims, jnp.float32)
    if split:
        result = result * steps_of(own_key, dims, split, -0.22, 0.18)
    return jnp.clip(result, -most, most).astype(kind)


def setup_inputs(seed: int = 0) -> dict:
    key_of = jax.random.split(jax.random.key(seed), 5)
    return {
        "samples": normal_values(key_of[0], (2, SAMPLES), 1.0, 6.0, ((1, 128),), jnp.float32),
        "code_chips": draw_code_chips(jax.random.fold_in(key_of[4], 71), 0),
        "centers": set_ends(jax.random.randint(key_of[2], (SATS,), -20, 21), jax.random.fold_in(key_of[2], 1), -20, 20).astype(jnp.int32),
        "widths": set_ends(jax.random.randint(key_of[3], (SATS,), 1, WMAX + 1), jax.random.fold_in(key_of[3], 1), 1, WMAX).astype(jnp.int32),
    }


def make_replica(chips, center):
    index = jnp.arange(SAMPLES, dtype=jnp.int32)
    chip_index = ((index * CHIPS) // SAMPLES).astype(jnp.int32)
    halves = ((2 * index * CHIPS) // SAMPLES) % 2
    values = (jnp.take(chips, chip_index) * (1 - 2 * halves)).astype(jnp.float32)
    phase = ((center * index) % SAMPLES).astype(jnp.float32) * (2.0 * math.pi / SAMPLES)
    return values * jnp.cos(phase), values * jnp.sin(phase)


def reference(samples, code_chips, centers, widths):
    index = jnp.arange(SAMPLES, dtype=jnp.int32)
    bins = jnp.arange(DOP, dtype=jnp.int32) - DOP // 2
    turns = (bins[:, None] * index[None, :]) % (2 * SAMPLES)
    phase = turns.astype(jnp.float32) * (2.0 * math.pi / (2 * SAMPLES))
    cosine = jnp.cos(phase)
    sine = jnp.sin(phase)
    wiped_re = samples[0][None, :] * cosine + samples[1][None, :] * sine
    wiped_im = samples[1][None, :] * cosine - samples[0][None, :] * sine
    signal_spectrum = jnp.fft.fft(wiped_re + 1j * wiped_im, axis=1)
    rows = jnp.arange(DOP, dtype=jnp.int32)
    gap = jnp.abs(rows[:, None] - rows[None, :])

    def one_satellite(packed):
        chips, center, width = packed
        mod_re, mod_im = make_replica(chips, center)
        code_spectrum = jnp.fft.fft(mod_re + 1j * mod_im)
        corr = jnp.fft.ifft(signal_spectrum * jnp.conj(code_spectrum)[None, :], axis=1)
        power = (jnp.real(corr) ** 2 + jnp.imag(corr) ** 2) / SAMPLES
        mean_power = jnp.sum(power) / (DOP * SAMPLES)
        band = ((gap >= 2) & (gap <= 1 + width)).astype(jnp.float32)
        count = jnp.sum(band, axis=1)
        noise = jnp.dot(band, power, precision=lax.Precision.HIGHEST) / count[:, None]
        return power / (noise + 0.25 * mean_power + 1e-6)

    return lax.map(one_satellite, (code_chips, centers, widths))
```

```python
import functools
import math

import jax
import jax.numpy as jnp
import numpy as np
from jax import lax
from jax.experimental import pallas as pl
from jax.experimental.pallas import tpu as pltpu
from jax.sharding import PartitionSpec as P

N = 8192
CHIPS = 4092
DOP = 128
SATS = 3
KLO = 64
KHI = 128
THI = 8
F32 = jnp.float32
BF16 = jnp.bfloat16
MESH = pl.DeviceIdType.MESH


def split_np(table):
    table = np.asarray(table, np.float32)
    high = table.astype(jnp.bfloat16)
    low = (table - high.astype(np.float32)).astype(jnp.bfloat16)
    return high, low


def split(value):
    high = value.astype(BF16)
    low = (value - high.astype(F32)).astype(BF16)
    return high, low


def dot(left, right):
    return jnp.dot(left, right, preferred_element_type=F32)


def phase(turns):
    return np.cos(2 * np.pi * turns), np.sin(2 * np.pi * turns)


def build_tables():
    out = {}
    kappa = np.arange(-32, 96)
    order = np.concatenate([np.arange(0, 64, 2), np.arange(1, 64, 2)])
    cos, sin = phase(-(kappa[:, None] * order[None, :] % 64) / 64)
    high, low = split_np(np.concatenate([cos, sin], 0))
    out["code_first"] = np.concatenate([high, low], 1)
    lanes = np.arange(128)
    out["code_twiddle"] = np.stack(phase(-(kappa[:, None] * lanes[None, :] % N) / N)).astype(np.float32)
    cos, sin = phase((lanes[:, None] * lanes[None, :] % 128) / 128)
    high, low = split_np(np.block([[cos, -sin], [sin, cos]]))
    out["right"] = np.stack([high, low])
    high, low = split_np(np.block([[cos, sin], [-sin, cos]]))
    out["left"] = np.stack([high, low])
    rho = np.arange(-64, 192)
    device = np.arange(128)
    cos, sin = phase(-((device[:, None] // 2) * rho[None, :] % 128) / 128)
    columns = []
    for parity in range(2):
        keep = (device % 2 == parity)[:, None]
        columns += [cos * keep, sin * keep]
    high, low = split_np(np.concatenate(columns, 1))
    out["signal_first"] = np.stack([high, low])
    out["signal_twiddle"] = np.stack(phase(-(lanes[:, None] * rho[None, :] % (2 * N)) / (2 * N))).astype(np.float32)
    out["inverse"] = np.stack(phase((lanes[:, None] * lanes[None, :] % 128) / 128)).astype(np.float32)
    step = phase(np.broadcast_to(lanes[:, None], (128, 128)) / N)
    out["step"] = np.stack(step).astype(np.float32)
    block = np.arange(8)
    low_k = np.arange(KLO)
    turn = phase((block[:, None] * low_k[None, :] % 8) / 8)
    out["block"] = np.stack([np.broadcast_to(t[:, :, None], (8, KLO, 128)) for t in turn], 1).astype(np.float32) / N
    first = np.arange(256)[None, :] - 2 * np.arange(KLO)[:, None]
    out["window"] = ((first >= 0) & (first < 128)).astype(jnp.bfloat16)
    return out


NAMES = ["code_first", "code_twiddle", "right", "left", "signal_first", "signal_twiddle", "inverse", "step", "window"]


def gather_kernel(row_ref, out_ref, own_sem, send_sem, recv_sem):
    sat = lax.axis_index("sat")
    dop = lax.axis_index("dop")
    x, z = sat // 4, sat % 4
    me = sat * 8 + dop
    barrier = pltpu.get_barrier_semaphore()
    peers = []
    for step in range(1, 8):
        peers.append({"sat": sat, "dop": (dop + step) % 8})
    for step in range(1, 4):
        peers.append({"sat": x * 4 + (z + step) % 4, "dop": dop})
    for step in range(1, 4):
        peers.append({"sat": (x + step) % 4 * 4 + z, "dop": dop})
    for peer in peers:
        pl.semaphore_signal(barrier, inc=1, device_id=peer, device_id_type=MESH)
    own = pltpu.make_async_copy(row_ref, out_ref.at[pl.ds(me, 1)], own_sem)
    own.start()
    pl.semaphore_wait(barrier, 13)

    def exchange(first, size, start, targets, source):
        copies = []
        for i, peer in enumerate(targets):
            copies.append(
                pltpu.make_async_remote_copy(
                    src_ref=source,
                    dst_ref=out_ref.at[pl.ds(start, size)],
                    send_sem=send_sem.at[first + i],
                    recv_sem=recv_sem.at[first + i],
                    device_id=peer,
                    device_id_type=MESH,
                )
            )
            copies[-1].start()
        return copies

    first = exchange(0, 1, me, peers[:7], row_ref)
    own.wait()
    for copy in first:
        copy.wait()
    second = exchange(7, 8, sat * 8, peers[7:10], out_ref.at[pl.ds(sat * 8, 8)])
    for copy in second:
        copy.wait()
    third = exchange(10, 32, x * 32, peers[10:13], out_ref.at[pl.ds(x * 32, 32)])
    for copy in third:
        copy.wait()


def gathered(row):
    return pl.pallas_call(
        gather_kernel,
        out_shape=jax.ShapeDtypeStruct((128, 1, 128), F32),
        in_specs=[pl.BlockSpec(memory_space=pltpu.VMEM)],
        out_specs=pl.BlockSpec(memory_space=pltpu.VMEM),
        scratch_shapes=[
            pltpu.SemaphoreType.DMA,
            pltpu.SemaphoreType.DMA((13,)),
            pltpu.SemaphoreType.DMA((13,)),
        ],
        compiler_params=pltpu.CompilerParams(collective_id=0, has_side_effects=True),
        name="gather",
    )(row)


def code_part(centers_ref, chips_ref, block_ref, code_first, code_twiddle, right, chip_rows, spectrum, code):
    chip_rows[...] = jnp.zeros_like(chip_rows)
    for s in range(SATS):
        for a in range(32):
            width = 128 if a < 31 else CHIPS - 31 * 128
            chip_rows[pl.ds(s * 32 + a, 1), 0:width] = chips_ref[s : s + 1, a * 128 : a * 128 + width].astype(F32)
    rows = chip_rows[...]
    lane = lax.broadcasted_iota(jnp.int32, (96, 128), 1)
    index = lax.broadcasted_iota(jnp.int32, (96, 128), 0)
    turned = pltpu.roll(rows, 64, 1)
    above = pltpu.roll(turned, 1, 0)
    odd = jnp.where(lane < 64, above, turned)
    both = jnp.concatenate([odd, rows], 0).astype(BF16)
    sample = lax.broadcasted_iota(jnp.int32, (128, 128), 1)
    chip = lax.broadcasted_iota(jnp.int32, (128, 128), 0)
    kind = lax.broadcasted_iota(jnp.int32, (192, 128), 0) % 32 // 4
    replica = jnp.zeros((192, 128), F32)
    for i in range(8):
        shifted = sample + (7 - i)
        hit = chip == 60 + (shifted >> 1)
        sign = 1.0 - 2.0 * (shifted & 1).astype(F32)
        select = jnp.where(hit, sign, 0.0).astype(BF16)
        replica = jnp.where(kind == i, dot(both, select), replica)
    start = (lax.broadcasted_iota(jnp.int32, (192, 128), 0) < 96) & (
        lax.broadcasted_iota(jnp.int32, (192, 128), 0) % 4 == 0
    ) & (lax.broadcasted_iota(jnp.int32, (192, 128), 1) == 0)
    replica = jnp.where(start, pltpu.roll(replica, 127, 1), replica).astype(BF16)
    for s in range(SATS):
        part = jnp.concatenate([replica[s * 32 : s * 32 + 32], replica[96 + s * 32 : 128 + s * 32]], 0)
        stage = dot(code_first[...], jnp.concatenate([part, part], 0))
        re, im = stage[:128], stage[128:]
        cos, sin = code_twiddle[0], code_twiddle[1]
        turned = jnp.concatenate([re * cos - im * sin, im * cos + re * sin], 1)
        high, low = split(turned)
        spectrum[s] = dot(
            jnp.concatenate([high, low, high], 1),
            jnp.concatenate([right[0], right[0], right[1]], 0),
        )
    cos, sin = block_ref[0], block_ref[1]
    for s in range(SATS):
        shifted = pltpu.roll(spectrum[s], 96 + centers_ref[s], 0)[:KLO]
        re, im = shifted[:, :128], shifted[:, 128:]
        code[s, 0] = re * cos + im * sin
        code[s, 1] = re * sin - im * cos


def table_part(code, inverse, step, left_high, left_low):
    def group(g, _):
        at = pl.multiple_of(g * 16, 16)
        rows = pl.ds(at, 16)
        step_re, step_im = step[0, rows, :], step[1, rows, :]

        def one(k, carry):
            e_re, e_im = carry
            for s in range(SATS):
                c_re = code[s, 0, pl.ds(k, 1), :]
                c_im = code[s, 1, pl.ds(k, 1), :]
                m_re = e_re * c_re - e_im * c_im
                m_im = e_re * c_im + e_im * c_re
                into = pl.ds(pl.multiple_of(s * 128 + at, 16), 16)
                high, low = split(m_re)
                left_high[k, into, 0:128] = high
                left_low[k, into, 0:128] = low
                high, low = split(m_im)
                left_high[k, into, 128:256] = high
                left_low[k, into, 128:256] = low
            return e_re * step_re - e_im * step_im, e_re * step_im + e_im * step_re

        lax.fori_loop(0, KLO, one, (inverse[0, rows, :], inverse[1, rows, :]), unroll=4)
        return 0

    lax.fori_loop(0, 8, group, 0)


def signal_part(rows, left, signal_first, signal_twiddle):
    turned = rows.T
    high, low = split(turned)
    stage = dot(
        jnp.concatenate([high, low, high], 1),
        jnp.concatenate([signal_first[0], signal_first[0], signal_first[1]], 0),
    )
    re, im = [], []
    for parity in range(2):
        cos = stage[:, parity * 512 : parity * 512 + 256]
        sin = stage[:, parity * 512 + 256 : parity * 512 + 512]
        re.append(cos[:64] - sin[64:])
        im.append(sin[:64] + cos[64:])
    re, im = jnp.concatenate(re, 0), jnp.concatenate(im, 0)
    cos, sin = signal_twiddle[0], signal_twiddle[1]
    both = jnp.concatenate([re * cos - im * sin, im * cos + re * sin], 0)
    high, low = split(both)
    return dot(
        jnp.concatenate([left[0], left[1], left[0]], 1),
        jnp.concatenate([high, high, low], 0),
    )


def mean_part(signal, window, code, mean_ref):
    size = signal[0:128, :] * signal[0:128, :] + signal[128:256, :] * signal[128:256, :]
    high, low = split(size)
    under = lax.dot_general(
        jnp.concatenate([window[...], window[...]], 1),
        jnp.concatenate([high, low], 1),
        (((1,), (1,)), ((), ())),
        preferred_element_type=F32,
    )
    for s in range(SATS):
        re, im = code[s, 0], code[s, 1]
        total = jnp.sum(under * (re * re + im * im), axis=(0, 1), keepdims=True)
        mean_ref[s] = jnp.broadcast_to(total * (1.0 / (DOP * N)), (8, 128))


EIGHTH = math.sqrt(0.5)


def dft8(re, im):
    def add(a, b):
        return (a[0] + b[0], a[1] + b[1])

    def sub(a, b):
        return (a[0] - b[0], a[1] - b[1])

    def turn(a):
        return (-a[1], a[0])

    v = list(zip(re, im))

    def dft4(a, b, c, d):
        p, m = add(a, c), sub(a, c)
        q, n = add(b, d), turn(sub(b, d))
        return add(p, q), add(m, n), sub(p, q), sub(m, n)

    e = dft4(v[0], v[2], v[4], v[6])
    o = dft4(v[1], v[3], v[5], v[7])
    w1 = ((o[1][0] - o[1][1]) * EIGHTH, (o[1][0] + o[1][1]) * EIGHTH)
    w2 = turn(o[2])
    w3 = ((-o[3][0] - o[3][1]) * EIGHTH, (o[3][0] - o[3][1]) * EIGHTH)
    w = [o[0], w1, w2, w3]
    return [add(e[i], w[i]) for i in range(4)] + [sub(e[i], w[i]) for i in range(4)]


def main_part(signal, left_high, left_low, stage, total, power_ref):
    lane = lax.broadcasted_iota(jnp.int32, (256, 128), 1)
    for lam in range(8):
        for kap in range(8):
            k = lam + 8 * kap
            if k == 0:
                window = signal[:, 0:128]
            else:
                window = jnp.where(
                    lane < 128 - 2 * k,
                    pltpu.roll(signal[:, 0:128], 128 - 2 * k, 1),
                    pltpu.roll(signal[:, 128:256], 128 - 2 * k, 1),
                )
            high, low = split(window)

            def embedded(part):
                re, im = part[:128], part[128:]
                return jnp.concatenate([jnp.concatenate([re, im], 1), jnp.concatenate([-im, re], 1)], 0)

            high, low = embedded(high), embedded(low)
            m_high, m_low = left_high[k], left_low[k]
            stage[kap] = dot(
                jnp.concatenate([m_high, m_low, m_high], 1), jnp.concatenate([high, high, low], 0)
            )

        def chunk(c, _):
            rows = pl.ds(pl.multiple_of(c * 8, 8), 8)
            re = [stage[kap, rows, 0:128] for kap in range(8)]
            im = [stage[kap, rows, 128:256] for kap in range(8)]
            out = dft8(re, im)
            for t in range(8):
                a, b = out[t]
                angle = 2 * math.pi * (lam * t % 64) / 64
                cos, sin = math.cos(angle), math.sin(angle)
                if lam * t:
                    a, b = a * cos - b * sin, a * sin + b * cos
                if lam:
                    a = a + total[t, rows, 0:128]
                    b = b + total[t, rows, 128:256]
                if lam < 7:
                    total[t, rows, 0:128] = a
                    total[t, rows, 128:256] = b
                else:
                    power_ref[t, rows, :] = (a * a + b * b) * (1.0 / N)
            return 0

        lax.fori_loop(0, SATS * 16, chunk, 0, unroll=2)


def compute_kernel(
    centers_ref, rows_ref, chips_ref, block_ref, code_first, code_twiddle, right, left, signal_first, signal_twiddle,
    inverse, step, window, power_ref, mean_ref, chip_rows, spectrum, code, left_high, left_low, signal, stage, total,
):
    code_part(centers_ref, chips_ref, block_ref, code_first, code_twiddle, right, chip_rows, spectrum, code)
    table_part(code, inverse, step, left_high, left_low)
    signal[...] = signal_part(rows_ref[:, 0, :], left, signal_first, signal_twiddle)
    mean_part(signal, window, code, mean_ref)
    main_part(signal, left_high, left_low, stage, total, power_ref)


def vmem():
    return pl.BlockSpec(memory_space=pltpu.VMEM)


def computed(rows, chips, centers, block, tables):
    return pl.pallas_call(
        compute_kernel,
        out_shape=[
            jax.ShapeDtypeStruct((THI, SATS * 128, DOP), F32),
            jax.ShapeDtypeStruct((SATS, 8, 128), F32),
        ],
        in_specs=[pl.BlockSpec(memory_space=pltpu.SMEM)] + [vmem()] * (3 + len(tables)),
        out_specs=[vmem(), vmem()],
        scratch_shapes=[
            pltpu.VMEM((96, 128), F32),
            pltpu.VMEM((SATS, 128, 256), F32),
            pltpu.VMEM((SATS, 2, KLO, 128), F32),
            pltpu.VMEM((KLO, SATS * 128, 256), BF16),
            pltpu.VMEM((KLO, SATS * 128, 256), BF16),
            pltpu.VMEM((256, 256), F32),
            pltpu.VMEM((8, SATS * 128, 256), F32),
            pltpu.VMEM((THI, SATS * 128, 256), F32),
        ],
        compiler_params=pltpu.CompilerParams(vmem_limit_bytes=60 << 20),
        name="compute",
    )(centers, rows, chips, block, *tables)


def finish_kernel(widths_ref, power_ref, mean_ref, out_ref):
    s = pl.program_id(0)
    width = widths_ref[s]
    r = lax.broadcasted_iota(jnp.int32, (DOP, DOP), 0)
    q = lax.broadcasted_iota(jnp.int32, (DOP, DOP), 1)
    gap = jnp.abs(r - q)
    band = ((gap >= 2) & (gap <= 1 + width)).astype(F32)
    count = jnp.sum(band, axis=0, keepdims=True)
    scale = 1.0 / count
    band = band.astype(BF16)
    band = jnp.concatenate([band, band], 0)
    floor = mean_ref[0, 0:1, :] * 0.25 + 1e-6
    for t in range(THI):
        power = power_ref[t]
        high, low = split(power)
        around = dot(jnp.concatenate([high, low], 1), band)
        ratio = power / (around * scale + floor)
        out_ref[0, :, t * 128 : t * 128 + 128] = ratio.T


def finished(power, mean, widths):
    return pl.pallas_call(
        finish_kernel,
        grid=(SATS,),
        out_shape=jax.ShapeDtypeStruct((SATS, DOP, THI * 128), F32),
        in_specs=[
            pl.BlockSpec(memory_space=pltpu.SMEM),
            pl.BlockSpec((THI, 128, DOP), lambda s: (0, s, 0)),
            pl.BlockSpec((1, 8, 128), lambda s: (s, 0, 0)),
        ],
        out_specs=pl.BlockSpec((1, DOP, THI * 128), lambda s: (s, 0, 0)),
        name="finish",
    )(widths, power, mean)


def on_device(samples, code_chips, centers, widths):
    tables = build_tables()
    rows = gathered(samples.reshape(1, 1, 128))
    block = jnp.asarray(tables["block"])[lax.axis_index("dop")]
    power, mean = computed(rows, code_chips, centers, block, [jnp.asarray(tables[n]) for n in NAMES])
    return finished(power, mean, widths)


def solution(mesh):
    both = ("sat", "dop")
    return jax.shard_map(
        on_device,
        mesh=mesh,
        in_specs=(P(None, both), P("sat", None), P("sat"), P("sat")),
        out_specs=P("sat", None, "dop"),
        check_vma=False,
    )
```

```python
import math

import jax
import jax.numpy as jnp
import numpy as np
from jax import lax
from jax.experimental import pallas as pl
from jax.experimental.pallas import tpu as pltpu
from jax.sharding import PartitionSpec as P

N = 8192
CHIPS = 4092
DOP = 128
SATS = 3
KLO = 64
KHI = 128
THI = 8
F32 = jnp.float32
BF16 = jnp.bfloat16
MESH = pl.DeviceIdType.MESH


def split_np(table):
    table = np.asarray(table, np.float32)
    high = table.astype(jnp.bfloat16)
    low = (table - high.astype(np.float32)).astype(jnp.bfloat16)
    return high, low


def split(value):
    high = value.astype(BF16)
    low = (value - high.astype(F32)).astype(BF16)
    return high, low


def dot(left, right):
    return jnp.dot(left, right, preferred_element_type=F32)


def phase(turns):
    return np.cos(2 * np.pi * turns), np.sin(2 * np.pi * turns)


def build_tables():
    out = {}
    kappa = np.arange(-32, 96)
    order = np.concatenate([np.arange(0, 64, 2), np.arange(1, 64, 2)])
    cos, sin = phase(-(kappa[:, None] * order[None, :] % 64) / 64)
    high, low = split_np(np.concatenate([cos, sin], 0))
    out["code_first"] = np.concatenate([high, low], 1)
    lanes = np.arange(128)
    out["code_twiddle"] = np.stack(phase(-(kappa[:, None] * lanes[None, :] % N) / N)).astype(np.float32)
    cos, sin = phase((lanes[:, None] * lanes[None, :] % 128) / 128)
    high, low = split_np(np.block([[cos, -sin], [sin, cos]]))
    out["right"] = np.stack([high, low])
    high, low = split_np(np.block([[cos, sin], [-sin, cos]]))
    out["left"] = np.stack([high, low])
    rho = np.arange(-64, 192)
    device = np.arange(128)
    cos, sin = phase(-((device[:, None] // 2) * rho[None, :] % 128) / 128)
    columns = []
    for parity in range(2):
        keep = (device % 2 == parity)[:, None]
        columns += [cos * keep, sin * keep]
    high, low = split_np(np.concatenate(columns, 1))
    out["signal_first"] = np.stack([high, low])
    out["signal_twiddle"] = np.stack(phase(-(lanes[:, None] * rho[None, :] % (2 * N)) / (2 * N))).astype(np.float32)
    out["inverse"] = np.stack(phase((lanes[:, None] * lanes[None, :] % 128) / 128)).astype(np.float32)
    step = phase(np.broadcast_to(lanes[:, None], (128, 128)) / N)
    out["step"] = np.stack(step).astype(np.float32)
    first = np.arange(256)[None, :] - 2 * np.arange(KLO)[:, None]
    out["window"] = ((first >= 0) & (first < 128)).astype(jnp.bfloat16)
    return out


NAMES = ["code_first", "code_twiddle", "right", "left", "signal_first", "signal_twiddle", "inverse", "step", "window"]


def eighth_turns(turns):
    half = jnp.where(turns >= 4, -1.0, 1.0)
    part = turns & 3
    cos = jnp.where(part == 0, 1.0, jnp.where(part == 1, EIGHTH, jnp.where(part == 2, 0.0, -EIGHTH)))
    sin = jnp.where(part == 0, 0.0, jnp.where(part == 2, 1.0, EIGHTH))
    return cos * half, sin * half


def code_part(centers_ref, chips_ref, dop, code_first, code_twiddle, right, chip_rows, spectrum, code):
    chip_rows[...] = jnp.zeros_like(chip_rows)
    for s in range(SATS):
        for a in range(32):
            width = 128 if a < 31 else CHIPS - 31 * 128
            chip_rows[pl.ds(s * 32 + a, 1), 0:width] = chips_ref[s : s + 1, a * 128 : a * 128 + width].astype(F32)
    rows = chip_rows[...]
    lane = lax.broadcasted_iota(jnp.int32, (96, 128), 1)
    index = lax.broadcasted_iota(jnp.int32, (96, 128), 0)
    turned = pltpu.roll(rows, 64, 1)
    above = pltpu.roll(turned, 1, 0)
    odd = jnp.where(lane < 64, above, turned)
    both = jnp.concatenate([odd, rows], 0).astype(BF16)
    sample = lax.broadcasted_iota(jnp.int32, (128, 128), 1)
    chip = lax.broadcasted_iota(jnp.int32, (128, 128), 0)
    kind = lax.broadcasted_iota(jnp.int32, (192, 128), 0) % 32 // 4
    replica = jnp.zeros((192, 128), F32)
    for i in range(8):
        shifted = sample + (7 - i)
        hit = chip == 60 + (shifted >> 1)
        sign = 1.0 - 2.0 * (shifted & 1).astype(F32)
        select = jnp.where(hit, sign, 0.0).astype(BF16)
        replica = jnp.where(kind == i, dot(both, select), replica)
    start = (lax.broadcasted_iota(jnp.int32, (192, 128), 0) < 96) & (
        lax.broadcasted_iota(jnp.int32, (192, 128), 0) % 4 == 0
    ) & (lax.broadcasted_iota(jnp.int32, (192, 128), 1) == 0)
    replica = jnp.where(start, pltpu.roll(replica, 127, 1), replica).astype(BF16)
    for s in range(SATS):
        part = jnp.concatenate([replica[s * 32 : s * 32 + 32], replica[96 + s * 32 : 128 + s * 32]], 0)
        stage = dot(code_first[...], jnp.concatenate([part, part], 0))
        re, im = stage[:128], stage[128:]
        cos, sin = code_twiddle[0], code_twiddle[1]
        turned = jnp.concatenate([re * cos - im * sin, im * cos + re * sin], 1)
        high, low = split(turned)
        spectrum[s] = dot(
            jnp.concatenate([high, low, high], 1),
            jnp.concatenate([right[0], right[0], right[1]], 0),
        )
    cos, sin = eighth_turns(lax.broadcasted_iota(jnp.int32, (KLO, 128), 0) * dop & 7)
    cos, sin = cos * (1.0 / N), sin * (1.0 / N)
    for s in range(SATS):
        shifted = pltpu.roll(spectrum[s], 96 + centers_ref[s], 0)[:KLO]
        re, im = shifted[:, :128], shifted[:, 128:]
        code[s, 0] = re * cos + im * sin
        code[s, 1] = re * sin - im * cos


def table_part(code, inverse, step, left_high, left_low, first, last):
    def group(g, _):
        at = pl.multiple_of(g * 16, 16)
        rows = pl.ds(at, 16)
        step_re, step_im = step[0, rows, :], step[1, rows, :]

        def one(k, carry):
            e_re, e_im = carry
            for s in range(SATS):
                c_re = code[s, 0, pl.ds(k, 1), :]
                c_im = code[s, 1, pl.ds(k, 1), :]
                m_re = e_re * c_re - e_im * c_im
                m_im = e_re * c_im + e_im * c_re
                into = pl.ds(pl.multiple_of(s * 128 + at, 16), 16)
                high, low = split(m_re)
                left_high[k, into, 0:128] = high
                left_low[k, into, 0:128] = low
                high, low = split(m_im)
                left_high[k, into, 128:256] = high
                left_low[k, into, 128:256] = low
            return e_re * step_re - e_im * step_im, e_re * step_im + e_im * step_re

        lax.fori_loop(0, KLO, one, (inverse[0, rows, :], inverse[1, rows, :]), unroll=4)
        return 0

    lax.fori_loop(first, last, group, 0)


def signal_part(rows, left, signal_first, signal_twiddle):
    turned = rows.T
    high, low = split(turned)
    stage = dot(
        jnp.concatenate([high, low, high], 1),
        jnp.concatenate([signal_first[0], signal_first[0], signal_first[1]], 0),
    )
    re, im = [], []
    for parity in range(2):
        cos = stage[:, parity * 512 : parity * 512 + 256]
        sin = stage[:, parity * 512 + 256 : parity * 512 + 512]
        re.append(cos[:64] - sin[64:])
        im.append(sin[:64] + cos[64:])
    re, im = jnp.concatenate(re, 0), jnp.concatenate(im, 0)
    cos, sin = signal_twiddle[0], signal_twiddle[1]
    both = jnp.concatenate([re * cos - im * sin, im * cos + re * sin], 0)
    high, low = split(both)
    return dot(
        jnp.concatenate([left[0], left[1], left[0]], 1),
        jnp.concatenate([high, high, low], 0),
    )


def mean_part(signal, window, code, mean_ref):
    size = signal[0:128, :] * signal[0:128, :] + signal[128:256, :] * signal[128:256, :]
    high, low = split(size)
    under = lax.dot_general(
        jnp.concatenate([window[...], window[...]], 1),
        jnp.concatenate([high, low], 1),
        (((1,), (1,)), ((), ())),
        preferred_element_type=F32,
    )
    for s in range(SATS):
        re, im = code[s, 0], code[s, 1]
        total = jnp.sum(under * (re * re + im * im), axis=(0, 1), keepdims=True)
        mean_ref[s] = jnp.broadcast_to(total * (1.0 / (DOP * N)), (8, 128))


EIGHTH = math.sqrt(0.5)


def dft8(re, im):
    def add(a, b):
        return (a[0] + b[0], a[1] + b[1])

    def sub(a, b):
        return (a[0] - b[0], a[1] - b[1])

    def turn(a):
        return (-a[1], a[0])

    v = list(zip(re, im))

    def dft4(a, b, c, d):
        p, m = add(a, c), sub(a, c)
        q, n = add(b, d), turn(sub(b, d))
        return add(p, q), add(m, n), sub(p, q), sub(m, n)

    e = dft4(v[0], v[2], v[4], v[6])
    o = dft4(v[1], v[3], v[5], v[7])
    w1 = ((o[1][0] - o[1][1]) * EIGHTH, (o[1][0] + o[1][1]) * EIGHTH)
    w2 = turn(o[2])
    w3 = ((-o[3][0] - o[3][1]) * EIGHTH, (o[3][0] - o[3][1]) * EIGHTH)
    w = [o[0], w1, w2, w3]
    return [add(e[i], w[i]) for i in range(4)] + [sub(e[i], w[i]) for i in range(4)]


def products(lam, signal, left_high, left_low, stage, kap):
    k = lam + 8 * kap
    lane = lax.broadcasted_iota(jnp.int32, (256, 128), 1)
    shift = 128 - 2 * k
    window = jnp.where(
        lane < shift,
        pltpu.roll(signal[:, 0:128], shift, 1),
        pltpu.roll(signal[:, 128:256], shift, 1),
    )
    high, low = split(window)

    def embedded(part):
        re, im = part[:128], part[128:]
        return jnp.concatenate([jnp.concatenate([re, im], 1), jnp.concatenate([-im, re], 1)], 0)

    high, low = embedded(high), embedded(low)
    m_high, m_low = left_high[k], left_low[k]
    stage[kap] = dot(jnp.concatenate([m_high, m_low, m_high], 1), jnp.concatenate([high, high, low], 0))


def combine(stage, total, row, power_ref=None, first=False):
    rows = pl.ds(row, 8)
    re = [stage[kap, rows, 0:128] for kap in range(8)]
    im = [stage[kap, rows, 128:256] for kap in range(8)]
    out = dft8(re, im)
    for t in range(8):
        a, b = out[t]
        if not first:
            c, d = total[t, rows, 0:128], total[t, rows, 128:256]
            if t:
                cos, sin = math.cos(math.pi * t / 32), math.sin(math.pi * t / 32)
                c, d = c * cos - d * sin, c * sin + d * cos
            a, b = a + c, b + d
        if power_ref is None:
            total[t, rows, 0:128] = a
            total[t, rows, 128:256] = b
        else:
            power_ref[t, rows, :] = (a * a + b * b) * (1.0 / N)


def main_part(signal, left_high, left_low, even, odd, total, power_ref):
    def both(lam, fill, drain, **kind):
        for kap in range(8):
            products(lam, signal, left_high, left_low, fill, kap)
            for g in range(6):
                combine(drain, total, kap * 48 + g * 8, **kind)

    for kap in range(8):
        products(7, signal, left_high, left_low, odd, kap)
    both(6, even, odd, first=True)

    def pair(i, _):
        lam = 5 - 2 * i
        both(lam, odd, even)
        both(lam - 1, even, odd)
        return 0

    lax.fori_loop(0, 3, pair, 0)

    def last(c, _):
        combine(even, total, pl.multiple_of(c * 8, 8), power_ref)
        return 0

    lax.fori_loop(0, SATS * 16, last, 0, unroll=2)


def compute_kernel(centers_ref, samples_ref, chips_hbm, *refs):
    count = len(NAMES)
    hbm = dict(zip(NAMES, refs[:count]))
    power_ref, mean_ref = refs[count : count + 2]
    refs = refs[count + 2 :]
    table = dict(zip(NAMES, refs[:count]))
    (gathered, chips, chip_rows, spectrum, code, left_high, left_low, signal, even, odd, total,
     own_sem, table_sem, send_sem, recv_sem) = refs[count:]
    sat = lax.axis_index("sat")
    dop = lax.axis_index("dop")
    x, z = sat // 4, sat % 4
    me = sat * 8 + dop
    barrier = pltpu.get_barrier_semaphore()
    peers = [{"sat": sat, "dop": (dop + step) % 8} for step in range(1, 8)]
    peers += [{"sat": x * 4 + (z + step) % 4, "dop": dop} for step in range(1, 4)]
    peers += [{"sat": (x + step) % 4 * 4 + z, "dop": dop} for step in range(1, 4)]
    for peer in peers:
        pl.semaphore_signal(barrier, inc=1, device_id=peer, device_id_type=MESH)
    own = pltpu.make_async_copy(samples_ref, gathered.at[me], own_sem)
    own.start()
    loads = {"chips": pltpu.make_async_copy(chips_hbm, chips, table_sem.at[count])}
    loads["chips"].start()
    for i, name in enumerate(NAMES):
        loads[name] = pltpu.make_async_copy(hbm[name], table[name], table_sem.at[i])
        loads[name].start()

    def exchange(first, size, start, targets, source):
        copies = []
        for i, peer in enumerate(targets):
            copies.append(
                pltpu.make_async_remote_copy(
                    src_ref=source,
                    dst_ref=gathered.at[pl.ds(start, size)],
                    send_sem=send_sem.at[first + i],
                    recv_sem=recv_sem.at[first + i],
                    device_id=peer,
                    device_id_type=MESH,
                )
            )
            copies[-1].start()
        return copies

    own.wait()
    pl.semaphore_wait(barrier, 13)
    copies = exchange(0, 1, me, peers[:7], gathered.at[pl.ds(me, 1)])
    for name in ("chips", "code_first", "code_twiddle", "right"):
        loads[name].wait()
    code_part(centers_ref, chips, dop, table["code_first"], table["code_twiddle"], table["right"], chip_rows, spectrum, code)
    for copy in copies:
        copy.wait()
    copies = exchange(7, 8, sat * 8, peers[7:10], gathered.at[pl.ds(sat * 8, 8)])
    for name in ("inverse", "step", "left", "signal_first", "signal_twiddle", "window"):
        loads[name].wait()
    table_part(code, table["inverse"], table["step"], left_high, left_low, 0, 3)
    for copy in copies:
        copy.wait()
    copies = exchange(10, 32, x * 32, peers[10:13], gathered.at[pl.ds(x * 32, 32)])
    table_part(code, table["inverse"], table["step"], left_high, left_low, 3, 8)
    for copy in copies:
        copy.wait()
    rows = jnp.concatenate([gathered[:, 0, :], gathered[:, 1, :]], 1)
    signal[...] = signal_part(rows, table["left"], table["signal_first"], table["signal_twiddle"])
    mean_part(signal, table["window"], code, mean_ref)
    main_part(signal, left_high, left_low, even, odd, total, power_ref)


def vmem():
    return pl.BlockSpec(memory_space=pltpu.VMEM)


def computed(samples, chips, centers, tables):
    return pl.pallas_call(
        compute_kernel,
        out_shape=[
            jax.ShapeDtypeStruct((THI, SATS * 128, DOP), F32),
            jax.ShapeDtypeStruct((SATS, 8, 128), F32),
        ],
        in_specs=[pl.BlockSpec(memory_space=pltpu.SMEM)] + [pl.BlockSpec(memory_space=pl.ANY)] * (2 + len(tables)),
        out_specs=[vmem(), vmem()],
        scratch_shapes=[pltpu.VMEM(t.shape, t.dtype) for t in tables]
        + [
            pltpu.VMEM((128, 2, 64), F32),
            pltpu.VMEM((SATS, CHIPS), jnp.int32),
            pltpu.VMEM((96, 128), F32),
            pltpu.VMEM((SATS, 128, 256), F32),
            pltpu.VMEM((SATS, 2, KLO, 128), F32),
            pltpu.VMEM((KLO, SATS * 128, 256), BF16),
            pltpu.VMEM((KLO, SATS * 128, 256), BF16),
            pltpu.VMEM((256, 256), F32),
            pltpu.VMEM((8, SATS * 128, 256), F32),
            pltpu.VMEM((8, SATS * 128, 256), F32),
            pltpu.VMEM((THI, SATS * 128, 256), F32),
            pltpu.SemaphoreType.DMA,
            pltpu.SemaphoreType.DMA((len(tables) + 1,)),
            pltpu.SemaphoreType.DMA((13,)),
            pltpu.SemaphoreType.DMA((13,)),
        ],
        compiler_params=pltpu.CompilerParams(vmem_limit_bytes=60 << 20, collective_id=0, has_side_effects=True),
        name="compute",
    )(centers, samples, chips, *tables)


def finish_kernel(widths_ref, power_ref, mean_ref, out_ref):
    s = pl.program_id(0)
    width = widths_ref[s]
    r = lax.broadcasted_iota(jnp.int32, (DOP, DOP), 0)
    q = lax.broadcasted_iota(jnp.int32, (DOP, DOP), 1)
    gap = jnp.abs(r - q)
    band = ((gap >= 2) & (gap <= 1 + width)).astype(F32)
    count = jnp.sum(band, axis=0, keepdims=True)
    scale = 1.0 / count
    band = band.astype(BF16)
    band = jnp.concatenate([band, band], 0)
    floor = mean_ref[0, 0:1, :] * 0.25 + 1e-6
    for t in range(THI):
        power = power_ref[t]
        high, low = split(power)
        around = dot(jnp.concatenate([high, low], 1), band)
        ratio = power / (around * scale + floor)
        out_ref[0, :, t * 128 : t * 128 + 128] = ratio.T


def finished(power, mean, widths):
    return pl.pallas_call(
        finish_kernel,
        grid=(SATS,),
        out_shape=jax.ShapeDtypeStruct((SATS, DOP, THI * 128), F32),
        in_specs=[
            pl.BlockSpec(memory_space=pltpu.SMEM),
            pl.BlockSpec((THI, 128, DOP), lambda s: (0, s, 0)),
            pl.BlockSpec((1, 8, 128), lambda s: (s, 0, 0)),
        ],
        out_specs=pl.BlockSpec((1, DOP, THI * 128), lambda s: (s, 0, 0)),
        name="finish",
    )(widths, power, mean)


def on_device(samples, code_chips, centers, widths):
    tables = build_tables()
    power, mean = computed(samples, code_chips, centers, [jnp.asarray(tables[n]) for n in NAMES])
    return finished(power, mean, widths)


def solution(mesh):
    both = ("sat", "dop")
    return jax.shard_map(
        on_device,
        mesh=mesh,
        in_specs=(P(None, both), P("sat", None), P("sat"), P("sat")),
        out_specs=P("sat", None, "dop"),
        check_vma=False,
    )
```

```python
import math

import jax
import jax.numpy as jnp
import numpy as np
from jax import lax
from jax.experimental import pallas as pl
from jax.experimental.pallas import tpu as pltpu
from jax.sharding import PartitionSpec as P

N = 8192
CHIPS = 4092
DOP = 128
SATS = 3
KLO = 64
KHI = 128
THI = 8
F32 = jnp.float32
BF16 = jnp.bfloat16
MESH = pl.DeviceIdType.MESH


def split_np(table):
    table = np.asarray(table, np.float32)
    high = table.astype(jnp.bfloat16)
    low = (table - high.astype(np.float32)).astype(jnp.bfloat16)
    return high, low


def split(value):
    high = value.astype(BF16)
    low = (value - high.astype(F32)).astype(BF16)
    return high, low


def dot(left, right):
    return jnp.dot(left, right, preferred_element_type=F32)


def phase(turns):
    return np.cos(2 * np.pi * turns), np.sin(2 * np.pi * turns)


def build_tables():
    out = {}
    kappa = np.arange(-32, 96)
    order = np.concatenate([np.arange(0, 64, 2), np.arange(1, 64, 2)])
    cos, sin = phase(-(kappa[:, None] * order[None, :] % 64) / 64)
    high, low = split_np(np.concatenate([cos, sin], 0))
    out["code_first"] = np.concatenate([high, low], 1)
    lanes = np.arange(128)
    out["code_twiddle"] = np.stack(phase(-(kappa[:, None] * lanes[None, :] % N) / N)).astype(np.float32)
    cos, sin = phase((lanes[:, None] * lanes[None, :] % 128) / 128)
    high, low = split_np(np.block([[cos, -sin], [sin, cos]]))
    out["right"] = np.stack([high, low])
    high, low = split_np(np.block([[cos, sin], [-sin, cos]]))
    out["left"] = np.stack([high, low])
    rho = np.arange(-64, 192)
    device = np.arange(128)
    cos, sin = phase(-((device[:, None] // 2) * rho[None, :] % 128) / 128)
    columns = []
    for parity in range(2):
        keep = (device % 2 == parity)[:, None]
        columns += [cos * keep, sin * keep]
    high, low = split_np(np.concatenate(columns, 1))
    out["signal_first"] = np.stack([high, low])
    out["signal_twiddle"] = np.stack(phase(-(lanes[:, None] * rho[None, :] % (2 * N)) / (2 * N))).astype(np.float32)
    out["inverse"] = np.stack(phase((lanes[:, None] * lanes[None, :] % 128) / 128)).astype(np.float32)
    step = phase(np.broadcast_to(lanes[:, None], (128, 128)) / N)
    out["step"] = np.stack(step).astype(np.float32)
    first = np.arange(256)[None, :] - 2 * np.arange(KLO)[:, None]
    out["window"] = ((first >= 0) & (first < 128)).astype(jnp.bfloat16)
    return out


NAMES = ["code_first", "code_twiddle", "right", "left", "signal_first", "signal_twiddle", "inverse", "step", "window"]


def eighth_turns(turns):
    half = jnp.where(turns >= 4, -1.0, 1.0)
    part = turns & 3
    cos = jnp.where(part == 0, 1.0, jnp.where(part == 1, EIGHTH, jnp.where(part == 2, 0.0, -EIGHTH)))
    sin = jnp.where(part == 0, 0.0, jnp.where(part == 2, 1.0, EIGHTH))
    return cos * half, sin * half


def code_part(centers_ref, chips_ref, dop, code_first, code_twiddle, right, chip_rows, spectrum, code):
    chip_rows[...] = jnp.zeros_like(chip_rows)
    for s in range(SATS):
        for a in range(32):
            width = 128 if a < 31 else CHIPS - 31 * 128
            chip_rows[pl.ds(s * 32 + a, 1), 0:width] = chips_ref[s : s + 1, a * 128 : a * 128 + width].astype(F32)
    rows = chip_rows[...]
    lane = lax.broadcasted_iota(jnp.int32, (96, 128), 1)
    index = lax.broadcasted_iota(jnp.int32, (96, 128), 0)
    turned = pltpu.roll(rows, 64, 1)
    above = pltpu.roll(turned, 1, 0)
    odd = jnp.where(lane < 64, above, turned)
    both = jnp.concatenate([odd, rows], 0).astype(BF16)
    sample = lax.broadcasted_iota(jnp.int32, (128, 128), 1)
    chip = lax.broadcasted_iota(jnp.int32, (128, 128), 0)
    kind = lax.broadcasted_iota(jnp.int32, (192, 128), 0) % 32 // 4
    replica = jnp.zeros((192, 128), F32)
    for i in range(8):
        shifted = sample + (7 - i)
        hit = chip == 60 + (shifted >> 1)
        sign = 1.0 - 2.0 * (shifted & 1).astype(F32)
        select = jnp.where(hit, sign, 0.0).astype(BF16)
        replica = jnp.where(kind == i, dot(both, select), replica)
    start = (lax.broadcasted_iota(jnp.int32, (192, 128), 0) < 96) & (
        lax.broadcasted_iota(jnp.int32, (192, 128), 0) % 4 == 0
    ) & (lax.broadcasted_iota(jnp.int32, (192, 128), 1) == 0)
    replica = jnp.where(start, pltpu.roll(replica, 127, 1), replica).astype(BF16)
    for s in range(SATS):
        part = jnp.concatenate([replica[s * 32 : s * 32 + 32], replica[96 + s * 32 : 128 + s * 32]], 0)
        stage = dot(code_first[...], jnp.concatenate([part, part], 0))
        re, im = stage[:128], stage[128:]
        cos, sin = code_twiddle[0], code_twiddle[1]
        turned = jnp.concatenate([re * cos - im * sin, im * cos + re * sin], 1)
        high, low = split(turned)
        spectrum[s] = dot(
            jnp.concatenate([high, low, high], 1),
            jnp.concatenate([right[0], right[0], right[1]], 0),
        )
    cos, sin = eighth_turns(lax.broadcasted_iota(jnp.int32, (KLO, 128), 0) * dop & 7)
    cos, sin = cos * (1.0 / N), sin * (1.0 / N)
    for s in range(SATS):
        shifted = pltpu.roll(spectrum[s], 96 + centers_ref[s], 0)[:KLO]
        re, im = shifted[:, :128], shifted[:, 128:]
        code[s, 0] = re * cos + im * sin
        code[s, 1] = re * sin - im * cos


def table_part(code, inverse, step, left_high, left_low, first, last):
    def group(g, _):
        at = pl.multiple_of(g * 16, 16)
        rows = pl.ds(at, 16)
        step_re, step_im = step[0, rows, :], step[1, rows, :]

        def one(k, carry):
            e_re, e_im = carry
            for s in range(SATS):
                c_re = code[s, 0, pl.ds(k, 1), :]
                c_im = code[s, 1, pl.ds(k, 1), :]
                m_re = e_re * c_re - e_im * c_im
                m_im = e_re * c_im + e_im * c_re
                into = pl.ds(pl.multiple_of(s * 128 + at, 16), 16)
                high, low = split(m_re)
                left_high[k, into, 0:128] = high
                left_low[k, into, 0:128] = low
                high, low = split(m_im)
                left_high[k, into, 128:256] = high
                left_low[k, into, 128:256] = low
            return e_re * step_re - e_im * step_im, e_re * step_im + e_im * step_re

        lax.fori_loop(0, KLO, one, (inverse[0, rows, :], inverse[1, rows, :]), unroll=4)
        return 0

    lax.fori_loop(first, last, group, 0)


def signal_part(rows, left, signal_first, signal_twiddle):
    turned = rows.T
    high, low = split(turned)
    stage = dot(
        jnp.concatenate([high, low, high], 1),
        jnp.concatenate([signal_first[0], signal_first[0], signal_first[1]], 0),
    )
    re, im = [], []
    for parity in range(2):
        cos = stage[:, parity * 512 : parity * 512 + 256]
        sin = stage[:, parity * 512 + 256 : parity * 512 + 512]
        re.append(cos[:64] - sin[64:])
        im.append(sin[:64] + cos[64:])
    re, im = jnp.concatenate(re, 0), jnp.concatenate(im, 0)
    cos, sin = signal_twiddle[0], signal_twiddle[1]
    both = jnp.concatenate([re * cos - im * sin, im * cos + re * sin], 0)
    high, low = split(both)
    return dot(
        jnp.concatenate([left[0], left[1], left[0]], 1),
        jnp.concatenate([high, high, low], 0),
    )


def mean_part(signal, window, code, mean_ref):
    size = signal[0:128, :] * signal[0:128, :] + signal[128:256, :] * signal[128:256, :]
    high, low = split(size)
    under = lax.dot_general(
        jnp.concatenate([window[...], window[...]], 1),
        jnp.concatenate([high, low], 1),
        (((1,), (1,)), ((), ())),
        preferred_element_type=F32,
    )
    for s in range(SATS):
        re, im = code[s, 0], code[s, 1]
        total = jnp.sum(under * (re * re + im * im), axis=(0, 1), keepdims=True)
        mean_ref[s] = jnp.broadcast_to(total * (1.0 / (DOP * N)), (8, 128))


EIGHTH = math.sqrt(0.5)


def dft8(re, im):
    def add(a, b):
        return (a[0] + b[0], a[1] + b[1])

    def sub(a, b):
        return (a[0] - b[0], a[1] - b[1])

    def turn(a):
        return (-a[1], a[0])

    v = list(zip(re, im))

    def dft4(a, b, c, d):
        p, m = add(a, c), sub(a, c)
        q, n = add(b, d), turn(sub(b, d))
        return add(p, q), add(m, n), sub(p, q), sub(m, n)

    e = dft4(v[0], v[2], v[4], v[6])
    o = dft4(v[1], v[3], v[5], v[7])
    w1 = ((o[1][0] - o[1][1]) * EIGHTH, (o[1][0] + o[1][1]) * EIGHTH)
    w2 = turn(o[2])
    w3 = ((-o[3][0] - o[3][1]) * EIGHTH, (o[3][0] - o[3][1]) * EIGHTH)
    w = [o[0], w1, w2, w3]
    return [add(e[i], w[i]) for i in range(4)] + [sub(e[i], w[i]) for i in range(4)]


def products(lam, signal, left_high, left_low, stage, kap):
    k = lam + 8 * kap
    lane = lax.broadcasted_iota(jnp.int32, (256, 128), 1)
    shift = 128 - 2 * k
    window = jnp.where(
        lane < shift,
        pltpu.roll(signal[0:256, 0:128], shift, 1),
        pltpu.roll(signal[0:256, 128:256], shift, 1),
    )
    high, low = split(window)

    def embedded(part):
        re, im = part[:128], part[128:]
        return jnp.concatenate([jnp.concatenate([re, im], 1), jnp.concatenate([-im, re], 1)], 0)

    high, low = embedded(high), embedded(low)
    m_high, m_low = left_high[k], left_low[k]
    stage[kap] = dot(jnp.concatenate([m_high, m_low, m_high], 1), jnp.concatenate([high, high, low], 0))


def combine(stage, total, row, power_ref=None, pace=None):
    rows = pl.ds(row, 8)
    re = [stage[kap, rows, 0:128] for kap in range(8)]
    im = [stage[kap, rows, 128:256] for kap in range(8)]
    out = dft8(re, im)
    for t in range(8):
        a, b = out[t]
        c, d = total[t, rows, 0:128], total[t, rows, 128:256]
        if t:
            cos, sin = math.cos(math.pi * t / 32), math.sin(math.pi * t / 32)
            c, d = c * cos - d * sin, c * sin + d * cos
        a, b = a + c, b + d
        if power_ref is None:
            total[t, rows, 0:128] = a
            total[t, rows, 128:256] = b
        else:
            power_ref[t, rows, :] = (a * a + b * b) * (1.0 / N)
    if pace is not None:
        signal, spare = pace
        signal[pl.ds(spare, 8), 0:128] = a


def main_part(signal, left_high, left_low, even, odd, total, power_ref):
    def both(lam, fill, drain):
        spare = pl.multiple_of(256 + 8 * (lam % 2), 8)
        for kap in range(8):
            products(lam, signal, left_high, left_low, fill, kap)
            for g in range(6):
                combine(drain, total, kap * 48 + g * 8, pace=(signal, spare))

    for kap in range(8):
        products(7, signal, left_high, left_low, odd, kap)

    def step(i, _):
        @pl.when(i % 2 == 0)
        def _():
            both(6 - i, even, odd)

        @pl.when(i % 2 == 1)
        def _():
            both(6 - i, odd, even)

        return 0

    lax.fori_loop(0, 7, step, 0)

    def last(c, _):
        combine(even, total, pl.multiple_of(c * 8, 8), power_ref)
        return 0

    lax.fori_loop(0, SATS * 16, last, 0, unroll=2)


def compute_kernel(centers_ref, samples_ref, chips_hbm, *refs):
    count = len(NAMES)
    hbm = dict(zip(NAMES, refs[:count]))
    power_ref, mean_ref = refs[count : count + 2]
    refs = refs[count + 2 :]
    table = dict(zip(NAMES, refs[:count]))
    (gathered, chips, chip_rows, spectrum, code, left_high, left_low, signal, even, odd, total,
     own_sem, table_sem, send_sem, recv_sem) = refs[count:]
    sat = lax.axis_index("sat")
    dop = lax.axis_index("dop")
    x, z = sat // 4, sat % 4
    me = sat * 8 + dop
    barrier = pltpu.get_barrier_semaphore()
    peers = [{"sat": sat, "dop": (dop + step) % 8} for step in range(1, 8)]
    for step in range(1, 16):
        peers.append({"sat": (x + step // 4) % 4 * 4 + (z + step % 4) % 4, "dop": dop})
    for peer in peers:
        pl.semaphore_signal(barrier, inc=1, device_id=peer, device_id_type=MESH)
    own = pltpu.make_async_copy(samples_ref, gathered.at[me], own_sem)
    own.start()
    loads = {"chips": pltpu.make_async_copy(chips_hbm, chips, table_sem.at[count])}
    loads["chips"].start()
    for i, name in enumerate(NAMES):
        loads[name] = pltpu.make_async_copy(hbm[name], table[name], table_sem.at[i])
        loads[name].start()

    def exchange(first, size, start, targets, source):
        copies = []
        for i, peer in enumerate(targets):
            copies.append(
                pltpu.make_async_remote_copy(
                    src_ref=source,
                    dst_ref=gathered.at[pl.ds(start, size)],
                    send_sem=send_sem.at[first + i],
                    recv_sem=recv_sem.at[first + i],
                    device_id=peer,
                    device_id_type=MESH,
                )
            )
            copies[-1].start()
        return copies

    for name in ("chips", "code_first", "code_twiddle", "right"):
        loads[name].wait()
    code_part(centers_ref, chips, dop, table["code_first"], table["code_twiddle"], table["right"], chip_rows, spectrum, code)
    own.wait()
    pl.semaphore_wait(barrier, 22)
    copies = exchange(0, 1, me, peers[:7], gathered.at[pl.ds(me, 1)])
    total[...] = jnp.zeros_like(total)
    for name in ("inverse", "step", "left", "signal_first", "signal_twiddle", "window"):
        loads[name].wait()
    table_part(code, table["inverse"], table["step"], left_high, left_low, 0, 3)
    for copy in copies:
        copy.wait()
    copies = exchange(7, 8, sat * 8, peers[7:], gathered.at[pl.ds(sat * 8, 8)])
    table_part(code, table["inverse"], table["step"], left_high, left_low, 3, 8)
    for copy in copies:
        copy.wait()
    rows = jnp.concatenate([gathered[:, 0, :], gathered[:, 1, :]], 1)
    signal[0:256, :] = signal_part(rows, table["left"], table["signal_first"], table["signal_twiddle"])
    mean_part(signal, table["window"], code, mean_ref)
    main_part(signal, left_high, left_low, even, odd, total, power_ref)


def vmem():
    return pl.BlockSpec(memory_space=pltpu.VMEM)


def computed(samples, chips, centers, tables):
    return pl.pallas_call(
        compute_kernel,
        out_shape=[
            jax.ShapeDtypeStruct((THI, SATS * 128, DOP), F32),
            jax.ShapeDtypeStruct((SATS, 8, 128), F32),
        ],
        in_specs=[pl.BlockSpec(memory_space=pltpu.SMEM)] + [pl.BlockSpec(memory_space=pltpu.HBM)] * (2 + len(tables)),
        out_specs=[vmem(), vmem()],
        scratch_shapes=[pltpu.VMEM(t.shape, t.dtype) for t in tables]
        + [
            pltpu.VMEM((128, 2, 64), F32),
            pltpu.VMEM((SATS, CHIPS), jnp.int32),
            pltpu.VMEM((96, 128), F32),
            pltpu.VMEM((SATS, 128, 256), F32),
            pltpu.VMEM((SATS, 2, KLO, 128), F32),
            pltpu.VMEM((KLO, SATS * 128, 256), BF16),
            pltpu.VMEM((KLO, SATS * 128, 256), BF16),
            pltpu.VMEM((272, 256), F32),
            pltpu.VMEM((8, SATS * 128, 256), F32),
            pltpu.VMEM((8, SATS * 128, 256), F32),
            pltpu.VMEM((THI, SATS * 128, 256), F32),
            pltpu.SemaphoreType.DMA,
            pltpu.SemaphoreType.DMA((len(tables) + 1,)),
            pltpu.SemaphoreType.DMA((22,)),
            pltpu.SemaphoreType.DMA((22,)),
        ],
        compiler_params=pltpu.CompilerParams(vmem_limit_bytes=44 << 20, collective_id=0, has_side_effects=True),
        name="compute",
    )(centers, samples, chips, *tables)


def finish_kernel(widths_ref, power_ref, mean_ref, out_ref, ratios, sem):
    r = lax.broadcasted_iota(jnp.int32, (DOP, DOP), 0)
    q = lax.broadcasted_iota(jnp.int32, (DOP, DOP), 1)
    gap = jnp.abs(r - q)
    copies = []
    for s in range(SATS):
        band = ((gap >= 2) & (gap <= 1 + widths_ref[s])).astype(F32)
        scale = 1.0 / jnp.sum(band, axis=0, keepdims=True)
        band = band.astype(BF16)
        band = jnp.concatenate([band, band], 0)
        floor = mean_ref[s, 0:1, :] * 0.25 + 1e-6
        for t in range(THI):
            power = power_ref[t, s * 128 : s * 128 + 128, :]
            high, low = split(power)
            around = dot(jnp.concatenate([high, low], 1), band)
            ratio = power / (around * scale + floor)
            ratios[s, :, t * 128 : t * 128 + 128] = ratio.T
        copies.append(pltpu.make_async_copy(ratios.at[s], out_ref.at[s], sem.at[s]))
        copies[-1].start()
    for copy in copies:
        copy.wait()


def finished(power, mean, widths):
    return pl.pallas_call(
        finish_kernel,
        out_shape=jax.ShapeDtypeStruct((SATS, DOP, THI * 128), F32),
        in_specs=[pl.BlockSpec(memory_space=pltpu.SMEM), vmem(), vmem()],
        out_specs=pl.BlockSpec(memory_space=pl.ANY),
        scratch_shapes=[pltpu.VMEM((SATS, DOP, THI * 128), F32), pltpu.SemaphoreType.DMA((SATS,))],
        compiler_params=pltpu.CompilerParams(vmem_limit_bytes=16 << 20),
        name="finish",
    )(widths, power, mean)


def on_device(samples, code_chips, centers, widths):
    tables = build_tables()
    places = [samples, code_chips] + [jnp.asarray(tables[n]) for n in NAMES]
    places = [pltpu.with_memory_space_constraint(a, pltpu.HBM) for a in places]
    power, mean = computed(places[0], places[1], centers, places[2:])
    return finished(power, mean, widths)


def solution(mesh):
    both = ("sat", "dop")
    return jax.shard_map(
        on_device,
        mesh=mesh,
        in_specs=(P(None, both), P("sat", None), P("sat"), P("sat")),
        out_specs=P("sat", None, "dop"),
        check_vma=False,
    )
```

```python
import math

import jax
import jax.numpy as jnp
import numpy as np
from jax import lax
from jax.experimental import pallas as pl
from jax.experimental.pallas import tpu as pltpu
from jax.sharding import PartitionSpec as P

N = 8192
CHIPS = 4092
DOP = 128
SATS = 3
KLO = 64
KHI = 128
THI = 8
F32 = jnp.float32
BF16 = jnp.bfloat16
MESH = pl.DeviceIdType.MESH


def split_np(table):
    table = np.asarray(table, np.float32)
    high = table.astype(jnp.bfloat16)
    low = (table - high.astype(np.float32)).astype(jnp.bfloat16)
    return high, low


def split(value):
    high = value.astype(BF16)
    low = (value - high.astype(F32)).astype(BF16)
    return high, low


def dot(left, right):
    return jnp.dot(left, right, preferred_element_type=F32)


def phase(turns):
    return np.cos(2 * np.pi * turns), np.sin(2 * np.pi * turns)


def build_tables():
    out = {}
    kappa = np.arange(-32, 96)
    order = np.concatenate([np.arange(0, 64, 2), np.arange(1, 64, 2)])
    cos, sin = phase(-(kappa[:, None] * order[None, :] % 64) / 64)
    high, low = split_np(np.concatenate([cos, sin], 0))
    out["code_first"] = np.concatenate([high, low], 1)
    lanes = np.arange(128)
    out["code_twiddle"] = np.stack(phase(-(kappa[:, None] * lanes[None, :] % N) / N)).astype(np.float32)
    cos, sin = phase((lanes[:, None] * lanes[None, :] % 128) / 128)
    high, low = split_np(np.block([[cos, -sin], [sin, cos]]))
    out["right"] = np.stack([high, low])
    high, low = split_np(np.block([[cos, sin], [-sin, cos]]))
    out["left"] = np.stack([high, low])
    rho = np.arange(-64, 192)
    device = np.arange(128)
    cos, sin = phase(-((device[:, None] // 2) * rho[None, :] % 128) / 128)
    columns = []
    for parity in range(2):
        keep = (device % 2 == parity)[:, None]
        columns += [cos * keep, sin * keep]
    high, low = split_np(np.concatenate(columns, 1))
    out["signal_first"] = np.stack([high, low])
    out["signal_twiddle"] = np.stack(phase(-(lanes[:, None] * rho[None, :] % (2 * N)) / (2 * N))).astype(np.float32)
    out["inverse"] = np.stack(phase((lanes[:, None] * lanes[None, :] % 128) / 128)).astype(np.float32)
    step = phase(np.broadcast_to(lanes[:, None], (128, 128)) / N)
    out["step"] = np.stack(step).astype(np.float32)
    first = np.arange(256)[None, :] - 2 * np.arange(KLO)[:, None]
    out["window"] = ((first >= 0) & (first < 128)).astype(jnp.bfloat16)
    return out


NAMES = ["code_first", "code_twiddle", "right", "left", "signal_first", "signal_twiddle", "inverse", "step", "window"]


def eighth_turns(turns):
    half = jnp.where(turns >= 4, -1.0, 1.0)
    part = turns & 3
    cos = jnp.where(part == 0, 1.0, jnp.where(part == 1, EIGHTH, jnp.where(part == 2, 0.0, -EIGHTH)))
    sin = jnp.where(part == 0, 0.0, jnp.where(part == 2, 1.0, EIGHTH))
    return cos * half, sin * half


def code_part(centers_ref, chips_ref, dop, code_first, code_twiddle, right, chip_rows, spectrum, code):
    chip_rows[...] = jnp.zeros_like(chip_rows)
    for s in range(SATS):
        for a in range(32):
            width = 128 if a < 31 else CHIPS - 31 * 128
            chip_rows[pl.ds(s * 32 + a, 1), 0:width] = chips_ref[s : s + 1, a * 128 : a * 128 + width].astype(F32)
    rows = chip_rows[...]
    lane = lax.broadcasted_iota(jnp.int32, (96, 128), 1)
    index = lax.broadcasted_iota(jnp.int32, (96, 128), 0)
    turned = pltpu.roll(rows, 64, 1)
    above = pltpu.roll(turned, 1, 0)
    odd = jnp.where(lane < 64, above, turned)
    both = jnp.concatenate([odd, rows], 0).astype(BF16)
    sample = lax.broadcasted_iota(jnp.int32, (128, 128), 1)
    chip = lax.broadcasted_iota(jnp.int32, (128, 128), 0)
    kind = lax.broadcasted_iota(jnp.int32, (192, 128), 0) % 32 // 4
    replica = jnp.zeros((192, 128), F32)
    for i in range(8):
        shifted = sample + (7 - i)
        hit = chip == 60 + (shifted >> 1)
        sign = 1.0 - 2.0 * (shifted & 1).astype(F32)
        select = jnp.where(hit, sign, 0.0).astype(BF16)
        replica = jnp.where(kind == i, dot(both, select), replica)
    start = (lax.broadcasted_iota(jnp.int32, (192, 128), 0) < 96) & (
        lax.broadcasted_iota(jnp.int32, (192, 128), 0) % 4 == 0
    ) & (lax.broadcasted_iota(jnp.int32, (192, 128), 1) == 0)
    replica = jnp.where(start, pltpu.roll(replica, 127, 1), replica).astype(BF16)
    for s in range(SATS):
        part = jnp.concatenate([replica[s * 32 : s * 32 + 32], replica[96 + s * 32 : 128 + s * 32]], 0)
        stage = dot(code_first[...], jnp.concatenate([part, part], 0))
        re, im = stage[:128], stage[128:]
        cos, sin = code_twiddle[0], code_twiddle[1]
        turned = jnp.concatenate([re * cos - im * sin, im * cos + re * sin], 1)
        high, low = split(turned)
        spectrum[s] = dot(
            jnp.concatenate([high, low, high], 1),
            jnp.concatenate([right[0], right[0], right[1]], 0),
        )
    cos, sin = eighth_turns(lax.broadcasted_iota(jnp.int32, (KLO, 128), 0) * dop & 7)
    cos, sin = cos * (1.0 / N), sin * (1.0 / N)
    for s in range(SATS):
        shifted = pltpu.roll(spectrum[s], 96 + centers_ref[s], 0)[:KLO]
        re, im = shifted[:, :128], shifted[:, 128:]
        code[s, 0] = re * cos + im * sin
        code[s, 1] = re * sin - im * cos


def table_part(code, inverse, step, left_high, left_low, first, last):
    def group(g, _):
        at = pl.multiple_of(g * 16, 16)
        rows = pl.ds(at, 16)
        step_re, step_im = step[0, rows, :], step[1, rows, :]

        def one(k, carry):
            e_re, e_im = carry
            for s in range(SATS):
                c_re = code[s, 0, pl.ds(k, 1), :]
                c_im = code[s, 1, pl.ds(k, 1), :]
                m_re = e_re * c_re - e_im * c_im
                m_im = e_re * c_im + e_im * c_re
                into = pl.ds(pl.multiple_of(s * 128 + at, 16), 16)
                high, low = split(m_re)
                left_high[k, into, 0:128] = high
                left_low[k, into, 0:128] = low
                high, low = split(m_im)
                left_high[k, into, 128:256] = high
                left_low[k, into, 128:256] = low
            return e_re * step_re - e_im * step_im, e_re * step_im + e_im * step_re

        lax.fori_loop(0, KLO, one, (inverse[0, rows, :], inverse[1, rows, :]), unroll=4)
        return 0

    lax.fori_loop(first, last, group, 0)


def signal_part(rows, left, signal_first, signal_twiddle):
    turned = rows.T
    high, low = split(turned)
    stage = dot(
        jnp.concatenate([high, low, high], 1),
        jnp.concatenate([signal_first[0], signal_first[0], signal_first[1]], 0),
    )
    re, im = [], []
    for parity in range(2):
        cos = stage[:, parity * 512 : parity * 512 + 256]
        sin = stage[:, parity * 512 + 256 : parity * 512 + 512]
        re.append(cos[:64] - sin[64:])
        im.append(sin[:64] + cos[64:])
    re, im = jnp.concatenate(re, 0), jnp.concatenate(im, 0)
    cos, sin = signal_twiddle[0], signal_twiddle[1]
    both = jnp.concatenate([re * cos - im * sin, im * cos + re * sin], 0)
    high, low = split(both)
    return dot(
        jnp.concatenate([left[0], left[1], left[0]], 1),
        jnp.concatenate([high, high, low], 0),
    )


def mean_part(signal, window, code, mean_ref):
    size = signal[0:128, :] * signal[0:128, :] + signal[128:256, :] * signal[128:256, :]
    high, low = split(size)
    under = lax.dot_general(
        jnp.concatenate([window[...], window[...]], 1),
        jnp.concatenate([high, low], 1),
        (((1,), (1,)), ((), ())),
        preferred_element_type=F32,
    )
    for s in range(SATS):
        re, im = code[s, 0], code[s, 1]
        total = jnp.sum(under * (re * re + im * im), axis=(0, 1), keepdims=True)
        mean_ref[s] = jnp.broadcast_to(total * (1.0 / (DOP * N)), (8, 128))


EIGHTH = math.sqrt(0.5)


def dft8(re, im):
    def add(a, b):
        return (a[0] + b[0], a[1] + b[1])

    def sub(a, b):
        return (a[0] - b[0], a[1] - b[1])

    def turn(a):
        return (-a[1], a[0])

    v = list(zip(re, im))

    def dft4(a, b, c, d):
        p, m = add(a, c), sub(a, c)
        q, n = add(b, d), turn(sub(b, d))
        return add(p, q), add(m, n), sub(p, q), sub(m, n)

    e = dft4(v[0], v[2], v[4], v[6])
    o = dft4(v[1], v[3], v[5], v[7])
    w1 = ((o[1][0] - o[1][1]) * EIGHTH, (o[1][0] + o[1][1]) * EIGHTH)
    w2 = turn(o[2])
    w3 = ((-o[3][0] - o[3][1]) * EIGHTH, (o[3][0] - o[3][1]) * EIGHTH)
    w = [o[0], w1, w2, w3]
    return [add(e[i], w[i]) for i in range(4)] + [sub(e[i], w[i]) for i in range(4)]


def products(lam, signal, left_high, left_low, stage, kap):
    k = lam + 8 * kap
    lane = lax.broadcasted_iota(jnp.int32, (256, 128), 1)
    shift = 128 - 2 * k
    window = jnp.where(
        lane < shift,
        pltpu.roll(signal[0:256, 0:128], shift, 1),
        pltpu.roll(signal[0:256, 128:256], shift, 1),
    )
    high, low = split(window)

    def embedded(part):
        re, im = part[:128], part[128:]
        return jnp.concatenate([jnp.concatenate([re, im], 1), jnp.concatenate([-im, re], 1)], 0)

    high, low = embedded(high), embedded(low)
    m_high, m_low = left_high[k], left_low[k]
    stage[kap] = dot(jnp.concatenate([m_high, m_low, m_high], 1), jnp.concatenate([high, high, low], 0))


def combine(stage, total, row, power_ref=None, pace=None):
    rows = pl.ds(row, 8)
    re = [stage[kap, rows, 0:128] for kap in range(8)]
    im = [stage[kap, rows, 128:256] for kap in range(8)]
    out = dft8(re, im)
    for t in range(8):
        a, b = out[t]
        c, d = total[t, rows, 0:128], total[t, rows, 128:256]
        if t:
            cos, sin = math.cos(math.pi * t / 32), math.sin(math.pi * t / 32)
            c, d = c * cos - d * sin, c * sin + d * cos
        a, b = a + c, b + d
        if power_ref is None:
            total[t, rows, 0:128] = a
            total[t, rows, 128:256] = b
        else:
            power_ref[t, rows, :] = (a * a + b * b) * (1.0 / N)
    if pace is not None:
        signal, spare = pace
        signal[pl.ds(spare, 8), 0:128] = a


def main_part(signal, left_high, left_low, even, odd, total, power_ref):
    def both(lam, fill, drain):
        spare = pl.multiple_of(256 + 8 * (lam % 2), 8)
        for kap in range(8):
            products(lam, signal, left_high, left_low, fill, kap)
            for g in range(6):
                combine(drain, total, kap * 48 + g * 8, pace=(signal, spare))

    for kap in range(8):
        products(7, signal, left_high, left_low, odd, kap)

    def step(i, _):
        @pl.when(i % 2 == 0)
        def _():
            both(6 - i, even, odd)

        @pl.when(i % 2 == 1)
        def _():
            both(6 - i, odd, even)

        return 0

    lax.fori_loop(0, 7, step, 0)

    def last(c, _):
        combine(even, total, pl.multiple_of(c * 8, 8), power_ref)
        return 0

    lax.fori_loop(0, SATS * 16, last, 0, unroll=2)


def compute_kernel(centers_ref, samples_ref, chips_hbm, *refs):
    count = len(NAMES)
    hbm = dict(zip(NAMES, refs[:count]))
    power_ref, mean_ref = refs[count : count + 2]
    refs = refs[count + 2 :]
    table = dict(zip(NAMES, refs[:count]))
    (gathered, chips, chip_rows, spectrum, code, left_high, left_low, signal, even, odd, total,
     own_sem, table_sem, send_sem, recv_sem) = refs[count:]
    sat = lax.axis_index("sat")
    dop = lax.axis_index("dop")
    x, z = sat // 4, sat % 4
    me = sat * 8 + dop
    barrier = pltpu.get_barrier_semaphore()
    peers = [{"sat": sat, "dop": (dop + step) % 8} for step in range(1, 8)]
    for step in range(1, 16):
        peers.append({"sat": (x + step // 4) % 4 * 4 + (z + step % 4) % 4, "dop": dop})
    for peer in peers:
        pl.semaphore_signal(barrier, inc=1, device_id=peer, device_id_type=MESH)
    own = pltpu.make_async_copy(samples_ref, gathered.at[me], own_sem)
    own.start()
    loads = {"chips": pltpu.make_async_copy(chips_hbm, chips, table_sem.at[count])}
    loads["chips"].start()
    for i, name in enumerate(NAMES):
        loads[name] = pltpu.make_async_copy(hbm[name], table[name], table_sem.at[i])
        loads[name].start()

    def exchange(first, size, start, targets, source):
        copies = []
        for i, peer in enumerate(targets):
            copies.append(
                pltpu.make_async_remote_copy(
                    src_ref=source,
                    dst_ref=gathered.at[pl.ds(start, size)],
                    send_sem=send_sem.at[first + i],
                    recv_sem=recv_sem.at[first + i],
                    device_id=peer,
                    device_id_type=MESH,
                )
            )
            copies[-1].start()
        return copies

    own.wait()
    pl.semaphore_wait(barrier, 22)
    copies = exchange(0, 1, me, peers[:7], gathered.at[pl.ds(me, 1)])
    for name in ("chips", "code_first", "code_twiddle", "right"):
        loads[name].wait()
    code_part(centers_ref, chips, dop, table["code_first"], table["code_twiddle"], table["right"], chip_rows, spectrum, code)
    for name in ("inverse", "step", "left", "signal_first", "signal_twiddle", "window"):
        loads[name].wait()
    table_part(code, table["inverse"], table["step"], left_high, left_low, 0, 1)
    for copy in copies:
        copy.wait()
    copies = exchange(7, 8, sat * 8, peers[7:], gathered.at[pl.ds(sat * 8, 8)])
    total[...] = jnp.zeros_like(total)
    table_part(code, table["inverse"], table["step"], left_high, left_low, 1, 8)
    for copy in copies:
        copy.wait()
    rows = jnp.concatenate([gathered[:, 0, :], gathered[:, 1, :]], 1)
    signal[0:256, :] = signal_part(rows, table["left"], table["signal_first"], table["signal_twiddle"])
    mean_part(signal, table["window"], code, mean_ref)
    main_part(signal, left_high, left_low, even, odd, total, power_ref)


def vmem():
    return pl.BlockSpec(memory_space=pltpu.VMEM)


def computed(samples, chips, centers, tables):
    return pl.pallas_call(
        compute_kernel,
        out_shape=[
            jax.ShapeDtypeStruct((THI, SATS * 128, DOP), F32),
            jax.ShapeDtypeStruct((SATS, 8, 128), F32),
        ],
        in_specs=[pl.BlockSpec(memory_space=pltpu.SMEM)] + [pl.BlockSpec(memory_space=pltpu.HBM)] * (2 + len(tables)),
        out_specs=[vmem(), vmem()],
        scratch_shapes=[pltpu.VMEM(t.shape, t.dtype) for t in tables]
        + [
            pltpu.VMEM((128, 2, 64), F32),
            pltpu.VMEM((SATS, CHIPS), jnp.int32),
            pltpu.VMEM((96, 128), F32),
            pltpu.VMEM((SATS, 128, 256), F32),
            pltpu.VMEM((SATS, 2, KLO, 128), F32),
            pltpu.VMEM((KLO, SATS * 128, 256), BF16),
            pltpu.VMEM((KLO, SATS * 128, 256), BF16),
            pltpu.VMEM((272, 256), F32),
            pltpu.VMEM((8, SATS * 128, 256), F32),
            pltpu.VMEM((8, SATS * 128, 256), F32),
            pltpu.VMEM((THI, SATS * 128, 256), F32),
            pltpu.SemaphoreType.DMA,
            pltpu.SemaphoreType.DMA((len(tables) + 1,)),
            pltpu.SemaphoreType.DMA((22,)),
            pltpu.SemaphoreType.DMA((22,)),
        ],
        compiler_params=pltpu.CompilerParams(vmem_limit_bytes=44 << 20, collective_id=0, has_side_effects=True),
        name="compute",
    )(centers, samples, chips, *tables)


def finish_kernel(widths_ref, power_ref, mean_ref, out_ref, ratios, sem):
    r = lax.broadcasted_iota(jnp.int32, (DOP, DOP), 0)
    q = lax.broadcasted_iota(jnp.int32, (DOP, DOP), 1)
    gap = jnp.abs(r - q)
    copies = []
    for s in range(SATS):
        band = ((gap >= 2) & (gap <= 1 + widths_ref[s])).astype(F32)
        scale = 1.0 / jnp.sum(band, axis=0, keepdims=True)
        band = band.astype(BF16)
        band = jnp.concatenate([band, band], 0)
        floor = mean_ref[s, 0:1, :] * 0.25 + 1e-6
        for t in range(THI):
            power = power_ref[t, s * 128 : s * 128 + 128, :]
            high, low = split(power)
            around = dot(jnp.concatenate([high, low], 1), band)
            ratio = power / (around * scale + floor)
            ratios[s, :, t * 128 : t * 128 + 128] = ratio.T
        copies.append(pltpu.make_async_copy(ratios.at[s], out_ref.at[s], sem.at[s]))
        copies[-1].start()
    for copy in copies:
        copy.wait()


def finished(power, mean, widths):
    return pl.pallas_call(
        finish_kernel,
        out_shape=jax.ShapeDtypeStruct((SATS, DOP, THI * 128), F32),
        in_specs=[pl.BlockSpec(memory_space=pltpu.SMEM), vmem(), vmem()],
        out_specs=pl.BlockSpec(memory_space=pl.ANY),
        scratch_shapes=[pltpu.VMEM((SATS, DOP, THI * 128), F32), pltpu.SemaphoreType.DMA((SATS,))],
        compiler_params=pltpu.CompilerParams(vmem_limit_bytes=16 << 20),
        name="finish",
    )(widths, power, mean)


def on_device(samples, code_chips, centers, widths):
    tables = build_tables()
    places = [samples, code_chips] + [jnp.asarray(tables[n]) for n in NAMES]
    places = [pltpu.with_memory_space_constraint(a, pltpu.HBM) for a in places]
    power, mean = computed(places[0], places[1], centers, places[2:])
    return finished(power, mean, widths)


def solution(mesh):
    both = ("sat", "dop")
    return jax.shard_map(
        on_device,
        mesh=mesh,
        in_specs=(P(None, both), P("sat", None), P("sat"), P("sat")),
        out_specs=P("sat", None, "dop"),
        check_vma=False,
    )
```

```python
import math

import jax
import jax.numpy as jnp
import numpy as np
from jax import lax
from jax.experimental import pallas as pl
from jax.experimental.pallas import tpu as pltpu
from jax.sharding import PartitionSpec as P

N = 8192
CHIPS = 4092
DOP = 128
SATS = 3
KLO = 64
KHI = 128
THI = 8
F32 = jnp.float32
BF16 = jnp.bfloat16
MESH = pl.DeviceIdType.MESH


def split_np(table):
    table = np.asarray(table, np.float32)
    high = table.astype(jnp.bfloat16)
    low = (table - high.astype(np.float32)).astype(jnp.bfloat16)
    return high, low


def split(value):
    high = value.astype(BF16)
    low = (value - high.astype(F32)).astype(BF16)
    return high, low


def dot(left, right):
    return jnp.dot(left, right, preferred_element_type=F32)


def phase(turns):
    return np.cos(2 * np.pi * turns), np.sin(2 * np.pi * turns)


def build_tables():
    out = {}
    kappa = np.arange(-32, 96)
    order = np.concatenate([np.arange(0, 64, 2), np.arange(1, 64, 2)])
    cos, sin = phase(-(kappa[:, None] * order[None, :] % 64) / 64)
    high, low = split_np(np.concatenate([cos, sin], 0))
    out["code_first"] = np.concatenate([high, low], 1)
    lanes = np.arange(128)
    out["code_twiddle"] = np.stack(phase(-(kappa[:, None] * lanes[None, :] % N) / N)).astype(np.float32)
    cos, sin = phase((lanes[:, None] * lanes[None, :] % 128) / 128)
    high, low = split_np(np.block([[cos, -sin], [sin, cos]]))
    out["right"] = np.stack([high, low])
    high, low = split_np(np.block([[cos, sin], [-sin, cos]]))
    out["left"] = np.stack([high, low])
    rho = np.arange(-64, 192)
    device = np.arange(128)
    cos, sin = phase(-((device[:, None] // 2) * rho[None, :] % 128) / 128)
    columns = []
    for parity in range(2):
        keep = (device % 2 == parity)[:, None]
        columns += [cos * keep, sin * keep]
    high, low = split_np(np.concatenate(columns, 1))
    out["signal_first"] = np.stack([high, low])
    out["signal_twiddle"] = np.stack(phase(-(lanes[:, None] * rho[None, :] % (2 * N)) / (2 * N))).astype(np.float32)
    out["inverse"] = np.stack(phase((lanes[:, None] * lanes[None, :] % 128) / 128)).astype(np.float32)
    step = phase(np.broadcast_to(lanes[:, None], (128, 128)) / N)
    out["step"] = np.stack(step).astype(np.float32)
    first = np.arange(256)[None, :] - 2 * np.arange(KLO)[:, None]
    out["window"] = ((first >= 0) & (first < 128)).astype(jnp.bfloat16)
    return out


NAMES = ["code_first", "code_twiddle", "right", "left", "signal_first", "signal_twiddle", "inverse", "step", "window"]


def eighth_turns(turns):
    half = jnp.where(turns >= 4, -1.0, 1.0)
    part = turns & 3
    cos = jnp.where(part == 0, 1.0, jnp.where(part == 1, EIGHTH, jnp.where(part == 2, 0.0, -EIGHTH)))
    sin = jnp.where(part == 0, 0.0, jnp.where(part == 2, 1.0, EIGHTH))
    return cos * half, sin * half


def code_part(centers_ref, chips_ref, dop, code_first, code_twiddle, right, chip_rows, spectrum, code):
    chip_rows[...] = jnp.zeros_like(chip_rows)
    for s in range(SATS):
        for a in range(32):
            width = 128 if a < 31 else CHIPS - 31 * 128
            chip_rows[pl.ds(s * 32 + a, 1), 0:width] = chips_ref[s : s + 1, a * 128 : a * 128 + width].astype(F32)
    rows = chip_rows[...]
    lane = lax.broadcasted_iota(jnp.int32, (96, 128), 1)
    index = lax.broadcasted_iota(jnp.int32, (96, 128), 0)
    turned = pltpu.roll(rows, 64, 1)
    above = pltpu.roll(turned, 1, 0)
    odd = jnp.where(lane < 64, above, turned)
    both = jnp.concatenate([odd, rows], 0).astype(BF16)
    sample = lax.broadcasted_iota(jnp.int32, (128, 128), 1)
    chip = lax.broadcasted_iota(jnp.int32, (128, 128), 0)
    kind = lax.broadcasted_iota(jnp.int32, (192, 128), 0) % 32 // 4
    replica = jnp.zeros((192, 128), F32)
    for i in range(8):
        shifted = sample + (7 - i)
        hit = chip == 60 + (shifted >> 1)
        sign = 1.0 - 2.0 * (shifted & 1).astype(F32)
        select = jnp.where(hit, sign, 0.0).astype(BF16)
        replica = jnp.where(kind == i, dot(both, select), replica)
    start = (lax.broadcasted_iota(jnp.int32, (192, 128), 0) < 96) & (
        lax.broadcasted_iota(jnp.int32, (192, 128), 0) % 4 == 0
    ) & (lax.broadcasted_iota(jnp.int32, (192, 128), 1) == 0)
    replica = jnp.where(start, pltpu.roll(replica, 127, 1), replica).astype(BF16)
    for s in range(SATS):
        part = jnp.concatenate([replica[s * 32 : s * 32 + 32], replica[96 + s * 32 : 128 + s * 32]], 0)
        stage = dot(code_first[...], jnp.concatenate([part, part], 0))
        re, im = stage[:128], stage[128:]
        cos, sin = code_twiddle[0], code_twiddle[1]
        turned = jnp.concatenate([re * cos - im * sin, im * cos + re * sin], 1)
        high, low = split(turned)
        spectrum[s] = dot(
            jnp.concatenate([high, low, high], 1),
            jnp.concatenate([right[0], right[0], right[1]], 0),
        )
    row = lax.broadcasted_iota(jnp.int32, (KLO, 128), 0)
    for s in range(SATS):
        block = dop if s == 2 else dop // 2 * 2
        cos, sin = eighth_turns(row * block & 7)
        cos, sin = cos * (1.0 / N), sin * (1.0 / N)
        shifted = pltpu.roll(spectrum[s], 96 + centers_ref[s], 0)[:KLO]
        re, im = shifted[:, :128], shifted[:, 128:256]
        code[s, 0] = re * cos + im * sin
        code[s, 1] = re * sin - im * cos


def table_part(code, own, inverse, step, left_high, left_low, first, last):
    def group(g, _):
        at = pl.multiple_of(g * 16, 16)
        rows = pl.ds(at, 16)
        step_re, step_im = step[0, rows, :], step[1, rows, :]

        def one(k, carry):
            e_re, e_im = carry
            for slot, s in ((0, own), (1, 2)):
                c_re = code[s, 0, pl.ds(k, 1), :]
                c_im = code[s, 1, pl.ds(k, 1), :]
                m_re = e_re * c_re - e_im * c_im
                m_im = e_re * c_im + e_im * c_re
                into = pl.ds(pl.multiple_of(slot * 128 + at, 16), 16)
                high, low = split(m_re)
                left_high[k, into, 0:128] = high
                left_low[k, into, 0:128] = low
                high, low = split(m_im)
                left_high[k, into, 128:256] = high
                left_low[k, into, 128:256] = low
            return e_re * step_re - e_im * step_im, e_re * step_im + e_im * step_re

        lax.fori_loop(0, KLO, one, (inverse[0, rows, :], inverse[1, rows, :]), unroll=4)
        return 0

    lax.fori_loop(first, last, group, 0)


def signal_part(rows, left, signal_first, signal_twiddle):
    turned = rows.T
    high, low = split(turned)
    stage = dot(
        jnp.concatenate([high, low, high], 1),
        jnp.concatenate([signal_first[0], signal_first[0], signal_first[1]], 0),
    )
    re, im = [], []
    for parity in range(2):
        cos = stage[:, parity * 512 : parity * 512 + 256]
        sin = stage[:, parity * 512 + 256 : parity * 512 + 512]
        re.append(cos[:64] - sin[64:])
        im.append(sin[:64] + cos[64:])
    re, im = jnp.concatenate(re, 0), jnp.concatenate(im, 0)
    cos, sin = signal_twiddle[0], signal_twiddle[1]
    both = jnp.concatenate([re * cos - im * sin, im * cos + re * sin], 0)
    high, low = split(both)
    return dot(
        jnp.concatenate([left[0], left[1], left[0]], 1),
        jnp.concatenate([high, high, low], 0),
    )


def mean_part(signal, window, code, mean_ref):
    size = signal[0:128, :] * signal[0:128, :] + signal[128:256, :] * signal[128:256, :]
    high, low = split(size)
    under = lax.dot_general(
        jnp.concatenate([window[...], window[...]], 1),
        jnp.concatenate([high, low], 1),
        (((1,), (1,)), ((), ())),
        preferred_element_type=F32,
    )
    for s in range(SATS):
        re, im = code[s, 0], code[s, 1]
        total = jnp.sum(under * (re * re + im * im), axis=(0, 1), keepdims=True)
        mean_ref[s] = jnp.broadcast_to(total * (1.0 / (DOP * N)), (8, 128))


EIGHTH = math.sqrt(0.5)


def dft8(re, im):
    def add(a, b):
        return (a[0] + b[0], a[1] + b[1])

    def sub(a, b):
        return (a[0] - b[0], a[1] - b[1])

    def turn(a):
        return (-a[1], a[0])

    v = list(zip(re, im))

    def dft4(a, b, c, d):
        p, m = add(a, c), sub(a, c)
        q, n = add(b, d), turn(sub(b, d))
        return add(p, q), add(m, n), sub(p, q), sub(m, n)

    e = dft4(v[0], v[2], v[4], v[6])
    o = dft4(v[1], v[3], v[5], v[7])
    w1 = ((o[1][0] - o[1][1]) * EIGHTH, (o[1][0] + o[1][1]) * EIGHTH)
    w2 = turn(o[2])
    w3 = ((-o[3][0] - o[3][1]) * EIGHTH, (o[3][0] - o[3][1]) * EIGHTH)
    w = [o[0], w1, w2, w3]
    return [add(e[i], w[i]) for i in range(4)] + [sub(e[i], w[i]) for i in range(4)]


def products(lam, signal, left_high, left_low, stage, kap):
    k = lam + 8 * kap
    lane = lax.broadcasted_iota(jnp.int32, (256, 128), 1)
    shift = 128 - 2 * k
    window = jnp.where(
        lane < shift,
        pltpu.roll(signal[0:256, 0:128], shift, 1),
        pltpu.roll(signal[0:256, 128:256], shift, 1),
    )
    high, low = split(window)

    def embedded(part):
        re, im = part[:128], part[128:]
        return jnp.concatenate([jnp.concatenate([re, im], 1), jnp.concatenate([-im, re], 1)], 0)

    high, low = embedded(high), embedded(low)
    m_high, m_low = left_high[k], left_low[k]
    stage[kap] = dot(jnp.concatenate([m_high, m_low, m_high], 1), jnp.concatenate([high, high, low], 0))


def combine(stage, total, slot, row, store=None):
    rows = pl.ds(row, 8)
    from_rows = pl.ds(slot * 128 + row, 8)
    re = [stage[kap, from_rows, 0:128] for kap in range(8)]
    im = [stage[kap, from_rows, 128:256] for kap in range(8)]
    out = dft8(re, im)
    for t in range(total.shape[0]):
        a, b = out[t % 8]
        c, d = total[t, rows, 0:128], total[t, rows, 128:256]
        if t:
            cos, sin = math.cos(math.pi * t / 32), math.sin(math.pi * t / 32)
            c, d = c * cos - d * sin, c * sin + d * cos
        a, b = a + c, b + d
        if store is None:
            total[t, rows, 0:128] = a
            total[t, rows, 128:256] = b
        else:
            store(t, rows, (a * a + b * b) * (1.0 / N))


def main_part(signal, left_high, left_low, even, odd, wide, narrow, power_ref, own, send):
    def both(lam, fill, drain):
        for kap in range(8):
            products(lam, signal, left_high, left_low, fill, kap)
            for g in range(2):
                combine(drain, wide, 0, kap * 16 + g * 8)
                combine(drain, narrow, 1, kap * 16 + g * 8)

    for kap in range(8):
        products(7, signal, left_high, left_low, odd, kap)

    def step(i, _):
        @pl.when(i % 2 == 0)
        def _():
            both(6 - i, even, odd)

        @pl.when(i % 2 == 1)
        def _():
            both(6 - i, odd, even)

        return 0

    lax.fori_loop(0, 7, step, 0)
    places = [jnp.where(own == half, own, 3) for half in range(2)]

    def keep_wide(t, rows, value):
        power_ref[places[t // 8], t % 8, rows, :] = value

    def keep_narrow(t, rows, value):
        power_ref[2, t, rows, :] = value

    def finish_wide(first, last):
        def one(c, _):
            combine(even, wide, 0, pl.multiple_of(c * 8, 8), keep_wide)
            return 0

        lax.fori_loop(first, last, one, 0)

    def finish_narrow(first, last):
        def one(c, _):
            combine(even, narrow, 1, pl.multiple_of(c * 8, 8), keep_narrow)
            return 0

        lax.fori_loop(first, last, one, 0, unroll=2)

    finish_wide(0, 8)
    finish_narrow(0, 4)
    copies = [send(0)]
    finish_wide(8, 16)
    finish_narrow(4, 8)
    copies.append(send(1))
    finish_narrow(8, 16)
    for copy in copies:
        copy.wait()


def compute_kernel(centers_ref, samples_ref, chips_hbm, *refs):
    count = len(NAMES)
    hbm = dict(zip(NAMES, refs[:count]))
    power_ref, mean_ref = refs[count : count + 2]
    refs = refs[count + 2 :]
    table = dict(zip(NAMES, refs[:count]))
    (gathered, chips, chip_rows, spectrum, code, left_high, left_low, signal, even, odd, wide, narrow,
     own_sem, table_sem, send_sem, recv_sem) = refs[count:]
    sat = lax.axis_index("sat")
    dop = lax.axis_index("dop")
    x, z = sat // 4, sat % 4
    me = sat * 8 + dop
    own_sat = dop % 2
    barrier = pltpu.get_barrier_semaphore()
    peers = [{"sat": sat, "dop": (dop + step) % 8} for step in range(1, 8)]
    for step in range(1, 16):
        peers.append({"sat": (x + step // 4) % 4 * 4 + (z + step % 4) % 4, "dop": dop})
    for peer in peers:
        pl.semaphore_signal(barrier, inc=1, device_id=peer, device_id_type=MESH)
    own = pltpu.make_async_copy(samples_ref, gathered.at[me], own_sem)
    own.start()
    loads = {"chips": pltpu.make_async_copy(chips_hbm, chips, table_sem.at[count])}
    loads["chips"].start()
    for i, name in enumerate(NAMES):
        loads[name] = pltpu.make_async_copy(hbm[name], table[name], table_sem.at[i])
        loads[name].start()

    def exchange(first, size, start, targets, source):
        copies = []
        for i, peer in enumerate(targets):
            copies.append(
                pltpu.make_async_remote_copy(
                    src_ref=source,
                    dst_ref=gathered.at[pl.ds(start, size)],
                    send_sem=send_sem.at[first + i],
                    recv_sem=recv_sem.at[first + i],
                    device_id=peer,
                    device_id_type=MESH,
                )
            )
            copies[-1].start()
        return copies

    for name in ("chips", "code_first", "code_twiddle", "right"):
        loads[name].wait()
    code_part(centers_ref, chips, dop, table["code_first"], table["code_twiddle"], table["right"], chip_rows, spectrum, code)
    own.wait()
    pl.semaphore_wait(barrier, 22)
    copies = exchange(0, 1, me, peers[:7], gathered.at[pl.ds(me, 1)])
    wide[...] = jnp.zeros_like(wide)
    narrow[...] = jnp.zeros_like(narrow)
    for name in ("inverse", "step", "left", "signal_first", "signal_twiddle", "window"):
        loads[name].wait()
    table_part(code, own_sat, table["inverse"], table["step"], left_high, left_low, 0, 3)
    for copy in copies:
        copy.wait()
    copies = exchange(7, 8, sat * 8, peers[7:], gathered.at[pl.ds(sat * 8, 8)])
    table_part(code, own_sat, table["inverse"], table["step"], left_high, left_low, 3, 8)
    for copy in copies:
        copy.wait()
    rows = jnp.concatenate([gathered[:, 0, :], gathered[:, 1, :]], 1)
    signal[...] = signal_part(rows, table["left"], table["signal_first"], table["signal_twiddle"])
    mean_part(signal, table["window"], code, mean_ref)

    def send(half):
        rows = pl.ds(half * 64, 64)
        copy = pltpu.make_async_remote_copy(
            src_ref=power_ref.at[3, :, rows],
            dst_ref=power_ref.at[own_sat, :, rows],
            send_sem=send_sem.at[22 + half],
            recv_sem=recv_sem.at[22 + half],
            device_id={"sat": sat, "dop": dop + 1 - 2 * own_sat},
            device_id_type=MESH,
        )
        copy.start()
        return copy

    main_part(signal, left_high, left_low, even, odd, wide, narrow, power_ref, own_sat, send)


def vmem():
    return pl.BlockSpec(memory_space=pltpu.VMEM)


def computed(samples, chips, centers, tables):
    return pl.pallas_call(
        compute_kernel,
        out_shape=[
            jax.ShapeDtypeStruct((SATS + 1, THI, 128, DOP), F32),
            jax.ShapeDtypeStruct((SATS, 8, 128), F32),
        ],
        in_specs=[pl.BlockSpec(memory_space=pltpu.SMEM)] + [pl.BlockSpec(memory_space=pltpu.HBM)] * (2 + len(tables)),
        out_specs=[vmem(), vmem()],
        scratch_shapes=[pltpu.VMEM(t.shape, t.dtype) for t in tables]
        + [
            pltpu.VMEM((128, 2, 64), F32),
            pltpu.VMEM((SATS, CHIPS), jnp.int32),
            pltpu.VMEM((96, 128), F32),
            pltpu.VMEM((SATS, 128, 256), F32),
            pltpu.VMEM((SATS, 2, KLO, 128), F32),
            pltpu.VMEM((KLO, 256, 256), BF16),
            pltpu.VMEM((KLO, 256, 256), BF16),
            pltpu.VMEM((256, 256), F32),
            pltpu.VMEM((8, 256, 256), F32),
            pltpu.VMEM((8, 256, 256), F32),
            pltpu.VMEM((2 * THI, 128, 256), F32),
            pltpu.VMEM((THI, 128, 256), F32),
            pltpu.SemaphoreType.DMA,
            pltpu.SemaphoreType.DMA((len(tables) + 1,)),
            pltpu.SemaphoreType.DMA((24,)),
            pltpu.SemaphoreType.DMA((24,)),
        ],
        compiler_params=pltpu.CompilerParams(vmem_limit_bytes=40 << 20, collective_id=0, has_side_effects=True),
        name="compute",
    )(centers, samples, chips, *tables)


def finish_kernel(widths_ref, power_ref, mean_ref, out_ref, ratios, sem):
    r = lax.broadcasted_iota(jnp.int32, (DOP, DOP), 0)
    q = lax.broadcasted_iota(jnp.int32, (DOP, DOP), 1)
    gap = jnp.abs(r - q)
    copies = []
    for s in range(SATS):
        band = ((gap >= 2) & (gap <= 1 + widths_ref[s])).astype(F32)
        scale = 1.0 / jnp.sum(band, axis=0, keepdims=True)
        band = band.astype(BF16)
        band = jnp.concatenate([band, band], 0)
        floor = mean_ref[s, 0:1, :] * 0.25 + 1e-6
        for t in range(THI):
            power = power_ref[s, t]
            high, low = split(power)
            around = dot(jnp.concatenate([high, low], 1), band)
            ratio = power / (around * scale + floor)
            ratios[s, :, t * 128 : t * 128 + 128] = ratio.T
        copies.append(pltpu.make_async_copy(ratios.at[s], out_ref.at[s], sem.at[s]))
        copies[-1].start()
    for copy in copies:
        copy.wait()


def finished(power, mean, widths):
    return pl.pallas_call(
        finish_kernel,
        out_shape=jax.ShapeDtypeStruct((SATS, DOP, THI * 128), F32),
        in_specs=[pl.BlockSpec(memory_space=pltpu.SMEM), vmem(), vmem()],
        out_specs=pl.BlockSpec(memory_space=pl.ANY),
        scratch_shapes=[pltpu.VMEM((SATS, DOP, THI * 128), F32), pltpu.SemaphoreType.DMA((SATS,))],
        compiler_params=pltpu.CompilerParams(vmem_limit_bytes=16 << 20),
        name="finish",
    )(widths, power, mean)


def on_device(samples, code_chips, centers, widths):
    tables = build_tables()
    places = [samples, code_chips] + [jnp.asarray(tables[n]) for n in NAMES]
    places = [pltpu.with_memory_space_constraint(a, pltpu.HBM) for a in places]
    power, mean = computed(places[0], places[1], centers, places[2:])
    return finished(power, mean, widths)


def solution(mesh):
    both = ("sat", "dop")
    return jax.shard_map(
        on_device,
        mesh=mesh,
        in_specs=(P(None, both), P("sat", None), P("sat"), P("sat")),
        out_specs=P("sat", None, "dop"),
        check_vma=False,
    )
```

```python
import math

import jax
import jax.numpy as jnp
import numpy as np
from jax import lax
from jax.experimental import pallas as pl
from jax.experimental.pallas import tpu as pltpu
from jax.sharding import PartitionSpec as P

N = 8192
CHIPS = 4092
DOP = 128
SATS = 3
KLO = 64
KHI = 128
THI = 8
F32 = jnp.float32
BF16 = jnp.bfloat16
MESH = pl.DeviceIdType.MESH


def split_np(table):
    table = np.asarray(table, np.float32)
    high = table.astype(jnp.bfloat16)
    low = (table - high.astype(np.float32)).astype(jnp.bfloat16)
    return high, low


def split(value):
    high = value.astype(BF16)
    low = (value - high.astype(F32)).astype(BF16)
    return high, low


def dot(left, right):
    return jnp.dot(left, right, preferred_element_type=F32)


def phase(turns):
    return np.cos(2 * np.pi * turns), np.sin(2 * np.pi * turns)


def build_tables():
    out = {}
    kappa = np.arange(-32, 96)
    order = np.concatenate([np.arange(0, 64, 2), np.arange(1, 64, 2)])
    cos, sin = phase(-(kappa[:, None] * order[None, :] % 64) / 64)
    high, low = split_np(np.concatenate([cos, sin], 0))
    out["code_first"] = np.concatenate([high, low], 1)
    lanes = np.arange(128)
    out["code_twiddle"] = np.stack(phase(-(kappa[:, None] * lanes[None, :] % N) / N)).astype(np.float32)
    cos, sin = phase((lanes[:, None] * lanes[None, :] % 128) / 128)
    high, low = split_np(np.block([[cos, -sin], [sin, cos]]))
    out["right"] = np.stack([high, low])
    high, low = split_np(np.block([[cos, sin], [-sin, cos]]))
    out["left"] = np.stack([high, low])
    rho = np.arange(-64, 192)
    device = np.arange(128)
    cos, sin = phase(-((device[:, None] // 2) * rho[None, :] % 128) / 128)
    columns = []
    for parity in range(2):
        keep = (device % 2 == parity)[:, None]
        columns += [cos * keep, sin * keep]
    high, low = split_np(np.concatenate(columns, 1))
    out["signal_first"] = np.stack([high, low])
    out["signal_twiddle"] = np.stack(phase(-(lanes[:, None] * rho[None, :] % (2 * N)) / (2 * N))).astype(np.float32)
    out["inverse"] = np.stack(phase((lanes[:, None] * lanes[None, :] % 128) / 128)).astype(np.float32)
    step = phase(np.broadcast_to(lanes[:, None], (128, 128)) / N)
    out["step"] = np.stack(step).astype(np.float32)
    first = np.arange(256)[None, :] - 2 * np.arange(KLO)[:, None]
    out["window"] = ((first >= 0) & (first < 128)).astype(jnp.bfloat16)
    return out


NAMES = ["code_first", "code_twiddle", "right", "left", "signal_first", "signal_twiddle", "inverse", "step", "window"]


def eighth_turns(turns):
    half = jnp.where(turns >= 4, -1.0, 1.0)
    part = turns & 3
    cos = jnp.where(part == 0, 1.0, jnp.where(part == 1, EIGHTH, jnp.where(part == 2, 0.0, -EIGHTH)))
    sin = jnp.where(part == 0, 0.0, jnp.where(part == 2, 1.0, EIGHTH))
    return cos * half, sin * half


def code_part(centers_ref, chips_ref, dop, code_first, code_twiddle, right, chip_rows, spectrum, code):
    chip_rows[...] = jnp.zeros_like(chip_rows)
    for s in range(SATS):
        for a in range(32):
            width = 128 if a < 31 else CHIPS - 31 * 128
            chip_rows[pl.ds(s * 32 + a, 1), 0:width] = chips_ref[s : s + 1, a * 128 : a * 128 + width].astype(F32)
    rows = chip_rows[...]
    lane = lax.broadcasted_iota(jnp.int32, (96, 128), 1)
    index = lax.broadcasted_iota(jnp.int32, (96, 128), 0)
    turned = pltpu.roll(rows, 64, 1)
    above = pltpu.roll(turned, 1, 0)
    odd = jnp.where(lane < 64, above, turned)
    both = jnp.concatenate([odd, rows], 0).astype(BF16)
    sample = lax.broadcasted_iota(jnp.int32, (128, 128), 1)
    chip = lax.broadcasted_iota(jnp.int32, (128, 128), 0)
    kind = lax.broadcasted_iota(jnp.int32, (192, 128), 0) % 32 // 4
    replica = jnp.zeros((192, 128), F32)
    for i in range(8):
        shifted = sample + (7 - i)
        hit = chip == 60 + (shifted >> 1)
        sign = 1.0 - 2.0 * (shifted & 1).astype(F32)
        select = jnp.where(hit, sign, 0.0).astype(BF16)
        replica = jnp.where(kind == i, dot(both, select), replica)
    start = (lax.broadcasted_iota(jnp.int32, (192, 128), 0) < 96) & (
        lax.broadcasted_iota(jnp.int32, (192, 128), 0) % 4 == 0
    ) & (lax.broadcasted_iota(jnp.int32, (192, 128), 1) == 0)
    replica = jnp.where(start, pltpu.roll(replica, 127, 1), replica).astype(BF16)
    for s in range(SATS):
        part = jnp.concatenate([replica[s * 32 : s * 32 + 32], replica[96 + s * 32 : 128 + s * 32]], 0)
        stage = dot(code_first[...], jnp.concatenate([part, part], 0))
        re, im = stage[:128], stage[128:]
        cos, sin = code_twiddle[0], code_twiddle[1]
        turned = jnp.concatenate([re * cos - im * sin, im * cos + re * sin], 1)
        high, low = split(turned)
        spectrum[s] = dot(
            jnp.concatenate([high, low, high], 1),
            jnp.concatenate([right[0], right[0], right[1]], 0),
        )
    row = lax.broadcasted_iota(jnp.int32, (KLO, 128), 0)
    for s in range(SATS):
        block = dop if s == 2 else dop // 2 * 2
        cos, sin = eighth_turns(row * block & 7)
        cos, sin = cos * (1.0 / N), sin * (1.0 / N)
        shifted = pltpu.roll(spectrum[s], 96 + centers_ref[s], 0)[:KLO]
        re, im = shifted[:, :128], shifted[:, 128:256]
        code[s, 0] = re * cos + im * sin
        code[s, 1] = re * sin - im * cos


def table_part(code, own, inverse, step, left_high, left_low, first, last):
    def group(g, _):
        at = pl.multiple_of(g * 16, 16)
        rows = pl.ds(at, 16)
        step_re, step_im = step[0, rows, :], step[1, rows, :]

        def one(k, carry):
            e_re, e_im = carry
            for slot, s in ((0, own), (1, 2)):
                c_re = code[s, 0, pl.ds(k, 1), :]
                c_im = code[s, 1, pl.ds(k, 1), :]
                m_re = e_re * c_re - e_im * c_im
                m_im = e_re * c_im + e_im * c_re
                into = pl.ds(pl.multiple_of(slot * 128 + at, 16), 16)
                high, low = split(m_re)
                left_high[k, into, 0:128] = high
                left_low[k, into, 0:128] = low
                high, low = split(m_im)
                left_high[k, into, 128:256] = high
                left_low[k, into, 128:256] = low
            return e_re * step_re - e_im * step_im, e_re * step_im + e_im * step_re

        lax.fori_loop(0, KLO, one, (inverse[0, rows, :], inverse[1, rows, :]), unroll=4)
        return 0

    lax.fori_loop(first, last, group, 0)


def signal_part(rows, left, signal_first, signal_twiddle):
    turned = rows.T
    high, low = split(turned)
    stage = dot(
        jnp.concatenate([high, low, high], 1),
        jnp.concatenate([signal_first[0], signal_first[0], signal_first[1]], 0),
    )
    re, im = [], []
    for parity in range(2):
        cos = stage[:, parity * 512 : parity * 512 + 256]
        sin = stage[:, parity * 512 + 256 : parity * 512 + 512]
        re.append(cos[:64] - sin[64:])
        im.append(sin[:64] + cos[64:])
    re, im = jnp.concatenate(re, 0), jnp.concatenate(im, 0)
    cos, sin = signal_twiddle[0], signal_twiddle[1]
    both = jnp.concatenate([re * cos - im * sin, im * cos + re * sin], 0)
    high, low = split(both)
    return dot(
        jnp.concatenate([left[0], left[1], left[0]], 1),
        jnp.concatenate([high, high, low], 0),
    )


def mean_part(signal, window, code, widths, mean_ref):
    size = signal[0:128, :] * signal[0:128, :] + signal[128:256, :] * signal[128:256, :]
    high, low = split(size)
    under = lax.dot_general(
        jnp.concatenate([window[...], window[...]], 1),
        jnp.concatenate([high, low], 1),
        (((1,), (1,)), ((), ())),
        preferred_element_type=F32,
    )
    for s in range(SATS):
        re, im = code[s, 0], code[s, 1]
        total = jnp.sum(under * (re * re + im * im), axis=(0, 1), keepdims=True)
        mean = jnp.broadcast_to(total * (1.0 / (DOP * N)), (8, 128))
        width = jnp.full((8, 128), widths[s].astype(F32))
        mean_ref[s] = jnp.where(lax.broadcasted_iota(jnp.int32, (8, 128), 0) == 0, mean, width)


EIGHTH = math.sqrt(0.5)


def dft8(re, im):
    def add(a, b):
        return (a[0] + b[0], a[1] + b[1])

    def sub(a, b):
        return (a[0] - b[0], a[1] - b[1])

    def turn(a):
        return (-a[1], a[0])

    v = list(zip(re, im))

    def dft4(a, b, c, d):
        p, m = add(a, c), sub(a, c)
        q, n = add(b, d), turn(sub(b, d))
        return add(p, q), add(m, n), sub(p, q), sub(m, n)

    e = dft4(v[0], v[2], v[4], v[6])
    o = dft4(v[1], v[3], v[5], v[7])
    w1 = ((o[1][0] - o[1][1]) * EIGHTH, (o[1][0] + o[1][1]) * EIGHTH)
    w2 = turn(o[2])
    w3 = ((-o[3][0] - o[3][1]) * EIGHTH, (o[3][0] - o[3][1]) * EIGHTH)
    w = [o[0], w1, w2, w3]
    return [add(e[i], w[i]) for i in range(4)] + [sub(e[i], w[i]) for i in range(4)]


def products(lam, signal, left_high, left_low, stage, kap):
    k = lam + 8 * kap
    lane = lax.broadcasted_iota(jnp.int32, (256, 128), 1)
    shift = 128 - 2 * k
    window = jnp.where(
        lane < shift,
        pltpu.roll(signal[0:256, 0:128], shift, 1),
        pltpu.roll(signal[0:256, 128:256], shift, 1),
    )
    high, low = split(window)

    def embedded(part):
        re, im = part[:128], part[128:]
        return jnp.concatenate([jnp.concatenate([re, im], 1), jnp.concatenate([-im, re], 1)], 0)

    high, low = embedded(high), embedded(low)
    m_high, m_low = left_high[k], left_low[k]
    stage[kap] = dot(jnp.concatenate([m_high, m_low, m_high], 1), jnp.concatenate([high, high, low], 0))


def combine(stage, total, slot, row, store=None):
    rows = pl.ds(row, 8)
    from_rows = pl.ds(slot * 128 + row, 8)
    re = [stage[kap, from_rows, 0:128] for kap in range(8)]
    im = [stage[kap, from_rows, 128:256] for kap in range(8)]
    out = dft8(re, im)
    for t in range(total.shape[0]):
        a, b = out[t % 8]
        c, d = total[t, rows, 0:128], total[t, rows, 128:256]
        if t:
            cos, sin = math.cos(math.pi * t / 32), math.sin(math.pi * t / 32)
            c, d = c * cos - d * sin, c * sin + d * cos
        a, b = a + c, b + d
        if store is None:
            total[t, rows, 0:128] = a
            total[t, rows, 128:256] = b
        else:
            store(t, rows, (a * a + b * b) * (1.0 / N))


def main_part(signal, left_high, left_low, even, odd, wide, narrow, power_ref, own, send, meanwhile):
    def both(lam, fill, drain):
        for kap in range(8):
            products(lam, signal, left_high, left_low, fill, kap)
            for g in range(2):
                combine(drain, wide, 0, kap * 16 + g * 8)
                combine(drain, narrow, 1, kap * 16 + g * 8)

    for kap in range(8):
        products(7, signal, left_high, left_low, odd, kap)

    def step(i, _):
        @pl.when(i % 2 == 0)
        def _():
            both(6 - i, even, odd)

        @pl.when(i % 2 == 1)
        def _():
            both(6 - i, odd, even)

        return 0

    lax.fori_loop(0, 7, step, 0)
    places = [jnp.where(own == half, own, 3) for half in range(2)]

    def keep_wide(t, rows, value):
        power_ref[places[t // 8], t % 8, rows, :] = value

    def keep_narrow(t, rows, value):
        power_ref[2, t, rows, :] = value

    def finish_wide(first, last):
        def one(c, _):
            combine(even, wide, 0, pl.multiple_of(c * 8, 8), keep_wide)
            return 0

        lax.fori_loop(first, last, one, 0)

    def finish_narrow(first, last):
        def one(c, _):
            combine(even, narrow, 1, pl.multiple_of(c * 8, 8), keep_narrow)
            return 0

        lax.fori_loop(first, last, one, 0, unroll=2)

    finish_wide(0, 8)
    finish_narrow(0, 2)
    copies = [send(0)]
    finish_wide(8, 16)
    finish_narrow(2, 4)
    copies.append(send(1))
    meanwhile()
    finish_narrow(4, 16)
    for copy in copies:
        copy.wait()


def compute_kernel(centers_hbm, widths_hbm, samples_ref, chips_hbm, *refs):
    count = len(NAMES)
    hbm = dict(zip(NAMES, refs[:count]))
    power_ref, mean_ref = refs[count : count + 2]
    refs = refs[count + 2 :]
    table = dict(zip(NAMES, refs[:count]))
    (centers, widths, gathered, chips, chip_rows, spectrum, code, left_high, left_low, signal, even, odd, wide, narrow,
     own_sem, table_sem, send_sem, recv_sem) = refs[count:]
    sat = lax.axis_index("sat")
    dop = lax.axis_index("dop")
    x, z = sat // 4, sat % 4
    me = sat * 8 + dop
    own_sat = dop % 2
    barrier = pltpu.get_barrier_semaphore()
    peers = [{"sat": sat, "dop": (dop + step) % 8} for step in range(1, 8)]
    for step in range(1, 16):
        peers.append({"sat": (x + step // 4) % 4 * 4 + (z + step % 4) % 4, "dop": dop})
    for peer in peers:
        pl.semaphore_signal(barrier, inc=1, device_id=peer, device_id_type=MESH)
    own = pltpu.make_async_copy(samples_ref, gathered.at[me], own_sem)
    own.start()
    loads = {"chips": pltpu.make_async_copy(chips_hbm, chips, table_sem.at[count])}
    loads["chips"].start()
    loads["centers"] = pltpu.make_async_copy(centers_hbm, centers, table_sem.at[count + 1])
    loads["centers"].start()
    loads["widths"] = pltpu.make_async_copy(widths_hbm, widths, table_sem.at[count + 2])
    loads["widths"].start()
    for i, name in enumerate(NAMES):
        loads[name] = pltpu.make_async_copy(hbm[name], table[name], table_sem.at[i])
        loads[name].start()

    def exchange(first, size, start, targets, source):
        copies = []
        for i, peer in enumerate(targets):
            copies.append(
                pltpu.make_async_remote_copy(
                    src_ref=source,
                    dst_ref=gathered.at[pl.ds(start, size)],
                    send_sem=send_sem.at[first + i],
                    recv_sem=recv_sem.at[first + i],
                    device_id=peer,
                    device_id_type=MESH,
                )
            )
            copies[-1].start()
        return copies

    for name in ("chips", "centers", "code_first", "code_twiddle", "right"):
        loads[name].wait()
    code_part(centers, chips, dop, table["code_first"], table["code_twiddle"], table["right"], chip_rows, spectrum, code)
    own.wait()
    pl.semaphore_wait(barrier, 22)
    copies = exchange(0, 1, me, peers[:7], gathered.at[pl.ds(me, 1)])
    wide[...] = jnp.zeros_like(wide)
    narrow[...] = jnp.zeros_like(narrow)
    for name in ("widths", "inverse", "step", "left", "signal_first", "signal_twiddle", "window"):
        loads[name].wait()
    table_part(code, own_sat, table["inverse"], table["step"], left_high, left_low, 0, 3)
    for copy in copies:
        copy.wait()
    copies = exchange(7, 8, sat * 8, peers[7:], gathered.at[pl.ds(sat * 8, 8)])
    table_part(code, own_sat, table["inverse"], table["step"], left_high, left_low, 3, 8)
    for copy in copies:
        copy.wait()
    rows = jnp.concatenate([gathered[:, 0, :], gathered[:, 1, :]], 1)
    signal[...] = signal_part(rows, table["left"], table["signal_first"], table["signal_twiddle"])

    def send(half):
        rows = pl.ds(half * 64, 64)
        copy = pltpu.make_async_remote_copy(
            src_ref=power_ref.at[3, :, rows],
            dst_ref=power_ref.at[own_sat, :, rows],
            send_sem=send_sem.at[22 + half],
            recv_sem=recv_sem.at[22 + half],
            device_id={"sat": sat, "dop": dop + 1 - 2 * own_sat},
            device_id_type=MESH,
        )
        copy.start()
        return copy

    main_part(signal, left_high, left_low, even, odd, wide, narrow, power_ref, own_sat, send,
              lambda: mean_part(signal, table["window"], code, widths, mean_ref))


def vmem():
    return pl.BlockSpec(memory_space=pltpu.VMEM)


def computed(centers, widths, samples, chips, tables):
    return pl.pallas_call(
        compute_kernel,
        out_shape=[
            jax.ShapeDtypeStruct((SATS + 1, THI, 128, DOP), F32),
            jax.ShapeDtypeStruct((SATS, 8, 128), F32),
        ],
        in_specs=[pl.BlockSpec(memory_space=pltpu.HBM)] * (4 + len(tables)),
        out_specs=[vmem(), vmem()],
        scratch_shapes=[pltpu.VMEM(t.shape, t.dtype) for t in tables]
        + [
            pltpu.SMEM((SATS,), jnp.int32),
            pltpu.SMEM((SATS,), jnp.int32),
            pltpu.VMEM((128, 2, 64), F32),
            pltpu.VMEM((SATS, CHIPS), jnp.int32),
            pltpu.VMEM((96, 128), F32),
            pltpu.VMEM((SATS, 128, 256), F32),
            pltpu.VMEM((SATS, 2, KLO, 128), F32),
            pltpu.VMEM((KLO, 256, 256), BF16),
            pltpu.VMEM((KLO, 256, 256), BF16),
            pltpu.VMEM((256, 256), F32),
            pltpu.VMEM((8, 256, 256), F32),
            pltpu.VMEM((8, 256, 256), F32),
            pltpu.VMEM((2 * THI, 128, 256), F32),
            pltpu.VMEM((THI, 128, 256), F32),
            pltpu.SemaphoreType.DMA,
            pltpu.SemaphoreType.DMA((len(tables) + 3,)),
            pltpu.SemaphoreType.DMA((24,)),
            pltpu.SemaphoreType.DMA((24,)),
        ],
        compiler_params=pltpu.CompilerParams(vmem_limit_bytes=40 << 20, collective_id=0, has_side_effects=True),
        name="compute",
    )(centers, widths, samples, chips, *tables)


def finish_kernel(power_ref, mean_ref, out_ref, ratios, sem):
    r = lax.broadcasted_iota(jnp.int32, (DOP, DOP), 0)
    q = lax.broadcasted_iota(jnp.int32, (DOP, DOP), 1)
    gap = jnp.abs(r - q)
    copies = []
    for s in range(SATS):
        band = ((gap >= 2) & (gap.astype(F32) <= 1.0 + mean_ref[s, 1:2, :])).astype(F32)
        scale = 1.0 / jnp.sum(band, axis=0, keepdims=True)
        band = band.astype(BF16)
        band = jnp.concatenate([band, band], 0)
        floor = mean_ref[s, 0:1, :] * 0.25 + 1e-6
        for t in range(THI):
            power = power_ref[s, t]
            high, low = split(power)
            around = dot(jnp.concatenate([high, low], 1), band)
            ratio = power / (around * scale + floor)
            ratios[s, :, t * 128 : t * 128 + 128] = ratio.T
        copies.append(pltpu.make_async_copy(ratios.at[s], out_ref.at[s], sem.at[s]))
        copies[-1].start()
    for copy in copies:
        copy.wait()


def finished(power, mean):
    return pl.pallas_call(
        finish_kernel,
        out_shape=jax.ShapeDtypeStruct((SATS, DOP, THI * 128), F32),
        in_specs=[vmem(), vmem()],
        out_specs=pl.BlockSpec(memory_space=pl.ANY),
        scratch_shapes=[pltpu.VMEM((SATS, DOP, THI * 128), F32), pltpu.SemaphoreType.DMA((SATS,))],
        compiler_params=pltpu.CompilerParams(vmem_limit_bytes=16 << 20),
        name="finish",
    )(power, mean)


def on_device(samples, code_chips, centers, widths):
    tables = build_tables()
    places = [centers, widths, samples, code_chips] + [jnp.asarray(tables[n]) for n in NAMES]
    places = [pltpu.with_memory_space_constraint(a, pltpu.HBM) for a in places]
    power, mean = computed(*places[:4], places[4:])
    return finished(power, mean)


def solution(mesh):
    both = ("sat", "dop")
    return jax.shard_map(
        on_device,
        mesh=mesh,
        in_specs=(P(None, both), P("sat", None), P("sat"), P("sat")),
        out_specs=P("sat", None, "dop"),
        check_vma=False,
    )
```

```python
import math

import jax
import jax.numpy as jnp
import numpy as np
from jax import lax
from jax.experimental import pallas as pl
from jax.experimental.pallas import tpu as pltpu
from jax.sharding import PartitionSpec as P

N = 8192
CHIPS = 4092
DOP = 128
SATS = 3
KLO = 64
KHI = 128
THI = 8
F32 = jnp.float32
BF16 = jnp.bfloat16
MESH = pl.DeviceIdType.MESH


def split_np(table):
    table = np.asarray(table, np.float32)
    high = table.astype(jnp.bfloat16)
    low = (table - high.astype(np.float32)).astype(jnp.bfloat16)
    return high, low


def split(value):
    high = value.astype(BF16)
    low = (value - high.astype(F32)).astype(BF16)
    return high, low


def dot(left, right):
    return jnp.dot(left, right, preferred_element_type=F32)


def phase(turns):
    return np.cos(2 * np.pi * turns), np.sin(2 * np.pi * turns)


def build_tables():
    out = {}
    kappa = np.arange(-32, 96)
    order = np.concatenate([np.arange(0, 64, 2), np.arange(1, 64, 2)])
    cos, sin = phase(-(kappa[:, None] * order[None, :] % 64) / 64)
    high, low = split_np(np.concatenate([cos, sin], 0))
    out["code_first"] = np.concatenate([high, low], 1)
    lanes = np.arange(128)
    out["code_twiddle"] = np.stack(phase(-(kappa[:, None] * lanes[None, :] % N) / N)).astype(np.float32)
    cos, sin = phase((lanes[:, None] * lanes[None, :] % 128) / 128)
    high, low = split_np(np.block([[cos, -sin], [sin, cos]]))
    out["right"] = np.stack([high, low])
    high, low = split_np(np.block([[cos, sin], [-sin, cos]]))
    out["left"] = np.stack([high, low])
    rho = np.arange(-64, 192)
    device = np.arange(128)
    cos, sin = phase(-((device[:, None] // 2) * rho[None, :] % 128) / 128)
    columns = []
    for parity in range(2):
        keep = (device % 2 == parity)[:, None]
        columns += [cos * keep, sin * keep]
    high, low = split_np(np.concatenate(columns, 1))
    out["signal_first"] = np.stack([high, low])
    out["signal_twiddle"] = np.stack(phase(-(lanes[:, None] * rho[None, :] % (2 * N)) / (2 * N))).astype(np.float32)
    out["inverse"] = np.stack(phase((lanes[:, None] * lanes[None, :] % 128) / 128)).astype(np.float32)
    step = phase(np.broadcast_to(lanes[:, None], (128, 128)) / N)
    out["step"] = np.stack(step).astype(np.float32)
    first = np.arange(256)[None, :] - 2 * np.arange(KLO)[:, None]
    out["window"] = ((first >= 0) & (first < 128)).astype(jnp.bfloat16)
    return out


NAMES = ["code_first", "code_twiddle", "right", "left", "signal_first", "signal_twiddle", "inverse", "step", "window"]


def eighth_turns(turns):
    half = jnp.where(turns >= 4, -1.0, 1.0)
    part = turns & 3
    cos = jnp.where(part == 0, 1.0, jnp.where(part == 1, EIGHTH, jnp.where(part == 2, 0.0, -EIGHTH)))
    sin = jnp.where(part == 0, 0.0, jnp.where(part == 2, 1.0, EIGHTH))
    return cos * half, sin * half


def code_part(centers_ref, chips_ref, dop, code_first, code_twiddle, right, chip_rows, spectrum, code):
    chip_rows[...] = jnp.zeros_like(chip_rows)
    for s in range(SATS):
        for a in range(32):
            width = 128 if a < 31 else CHIPS - 31 * 128
            chip_rows[pl.ds(s * 32 + a, 1), 0:width] = chips_ref[s : s + 1, a * 128 : a * 128 + width].astype(F32)
    rows = chip_rows[...]
    lane = lax.broadcasted_iota(jnp.int32, (96, 128), 1)
    index = lax.broadcasted_iota(jnp.int32, (96, 128), 0)
    turned = pltpu.roll(rows, 64, 1)
    above = pltpu.roll(turned, 1, 0)
    odd = jnp.where(lane < 64, above, turned)
    both = jnp.concatenate([odd, rows], 0).astype(BF16)
    sample = lax.broadcasted_iota(jnp.int32, (128, 128), 1)
    chip = lax.broadcasted_iota(jnp.int32, (128, 128), 0)
    kind = lax.broadcasted_iota(jnp.int32, (192, 128), 0) % 32 // 4
    replica = jnp.zeros((192, 128), F32)
    for i in range(8):
        shifted = sample + (7 - i)
        hit = chip == 60 + (shifted >> 1)
        sign = 1.0 - 2.0 * (shifted & 1).astype(F32)
        select = jnp.where(hit, sign, 0.0).astype(BF16)
        replica = jnp.where(kind == i, dot(both, select), replica)
    start = (lax.broadcasted_iota(jnp.int32, (192, 128), 0) < 96) & (
        lax.broadcasted_iota(jnp.int32, (192, 128), 0) % 4 == 0
    ) & (lax.broadcasted_iota(jnp.int32, (192, 128), 1) == 0)
    replica = jnp.where(start, pltpu.roll(replica, 127, 1), replica).astype(BF16)
    for s in range(SATS):
        part = jnp.concatenate([replica[s * 32 : s * 32 + 32], replica[96 + s * 32 : 128 + s * 32]], 0)
        stage = dot(code_first[...], jnp.concatenate([part, part], 0))
        re, im = stage[:128], stage[128:]
        cos, sin = code_twiddle[0], code_twiddle[1]
        turned = jnp.concatenate([re * cos - im * sin, im * cos + re * sin], 1)
        high, low = split(turned)
        spectrum[s] = dot(
            jnp.concatenate([high, low, high], 1),
            jnp.concatenate([right[0], right[0], right[1]], 0),
        )
    row = lax.broadcasted_iota(jnp.int32, (KLO, 128), 0)
    for s in range(SATS):
        block = dop if s == 2 else dop // 2 * 2
        cos, sin = eighth_turns(row * block & 7)
        cos, sin = cos * (1.0 / N), sin * (1.0 / N)
        shifted = pltpu.roll(spectrum[s], 96 + centers_ref[s], 0)[:KLO]
        re, im = shifted[:, :128], shifted[:, 128:256]
        code[s, 0] = re * cos + im * sin
        code[s, 1] = re * sin - im * cos


def table_part(code, own, inverse, step, left_high, left_low, first, last):
    def group(g, _):
        at = pl.multiple_of(g * 16, 16)
        rows = pl.ds(at, 16)
        step_re, step_im = step[0, rows, :], step[1, rows, :]

        def one(k, carry):
            e_re, e_im = carry
            for slot, s in ((0, own), (1, 2)):
                c_re = code[s, 0, pl.ds(k, 1), :]
                c_im = code[s, 1, pl.ds(k, 1), :]
                m_re = e_re * c_re - e_im * c_im
                m_im = e_re * c_im + e_im * c_re
                into = pl.ds(pl.multiple_of(slot * 128 + at, 16), 16)
                high, low = split(m_re)
                left_high[k, into, 0:128] = high
                left_low[k, into, 0:128] = low
                high, low = split(m_im)
                left_high[k, into, 128:256] = high
                left_low[k, into, 128:256] = low
            return e_re * step_re - e_im * step_im, e_re * step_im + e_im * step_re

        lax.fori_loop(0, KLO, one, (inverse[0, rows, :], inverse[1, rows, :]), unroll=4)
        return 0

    lax.fori_loop(first, last, group, 0)


def signal_part(rows, left, signal_first, signal_twiddle):
    turned = rows.T
    high, low = split(turned)
    stage = dot(
        jnp.concatenate([high, low, high], 1),
        jnp.concatenate([signal_first[0], signal_first[0], signal_first[1]], 0),
    )
    re, im = [], []
    for parity in range(2):
        cos = stage[:, parity * 512 : parity * 512 + 256]
        sin = stage[:, parity * 512 + 256 : parity * 512 + 512]
        re.append(cos[:64] - sin[64:])
        im.append(sin[:64] + cos[64:])
    re, im = jnp.concatenate(re, 0), jnp.concatenate(im, 0)
    cos, sin = signal_twiddle[0], signal_twiddle[1]
    both = jnp.concatenate([re * cos - im * sin, im * cos + re * sin], 0)
    high, low = split(both)
    return dot(
        jnp.concatenate([left[0], left[1], left[0]], 1),
        jnp.concatenate([high, high, low], 0),
    )


def mean_part(signal, window, code, widths, mean_ref):
    size = signal[0:128, :] * signal[0:128, :] + signal[128:256, :] * signal[128:256, :]
    high, low = split(size)
    under = lax.dot_general(
        jnp.concatenate([window[...], window[...]], 1),
        jnp.concatenate([high, low], 1),
        (((1,), (1,)), ((), ())),
        preferred_element_type=F32,
    )
    for s in range(SATS):
        re, im = code[s, 0], code[s, 1]
        total = jnp.sum(under * (re * re + im * im), axis=(0, 1), keepdims=True)
        mean = jnp.broadcast_to(total * (1.0 / (DOP * N)), (8, 128))
        width = jnp.full((8, 128), widths[s].astype(F32))
        mean_ref[s] = jnp.where(lax.broadcasted_iota(jnp.int32, (8, 128), 0) == 0, mean, width)


EIGHTH = math.sqrt(0.5)


def dft8(re, im):
    def add(a, b):
        return (a[0] + b[0], a[1] + b[1])

    def sub(a, b):
        return (a[0] - b[0], a[1] - b[1])

    def turn(a):
        return (-a[1], a[0])

    v = list(zip(re, im))

    def dft4(a, b, c, d):
        p, m = add(a, c), sub(a, c)
        q, n = add(b, d), turn(sub(b, d))
        return add(p, q), add(m, n), sub(p, q), sub(m, n)

    e = dft4(v[0], v[2], v[4], v[6])
    o = dft4(v[1], v[3], v[5], v[7])
    w1 = ((o[1][0] - o[1][1]) * EIGHTH, (o[1][0] + o[1][1]) * EIGHTH)
    w2 = turn(o[2])
    w3 = ((-o[3][0] - o[3][1]) * EIGHTH, (o[3][0] - o[3][1]) * EIGHTH)
    w = [o[0], w1, w2, w3]
    return [add(e[i], w[i]) for i in range(4)] + [sub(e[i], w[i]) for i in range(4)]


def windows(k, signal):
    lane = lax.broadcasted_iota(jnp.int32, (256, 128), 1)
    shift = 128 - 2 * k
    window = jnp.where(
        lane < shift,
        pltpu.roll(signal[:, 0:128], shift, 1),
        pltpu.roll(signal[:, 128:256], shift, 1),
    )
    high, low = split(window)

    def embedded(part):
        re, im = part[:128], part[128:]
        return jnp.concatenate([jnp.concatenate([re, im], 1), jnp.concatenate([-im, re], 1)], 0)

    return embedded(high), embedded(low)


def products(k, kap, factors, left_high, left_low, stage):
    high, low = factors
    m_high, m_low = left_high[k], left_low[k]
    stage[kap] = dot(jnp.concatenate([m_high, m_low, m_high], 1), jnp.concatenate([high, high, low], 0))


def combine(stage, total, slot, row, store=None):
    rows = pl.ds(row, 8)
    from_rows = pl.ds(slot * 128 + row, 8)
    re = [stage[kap, from_rows, 0:128] for kap in range(8)]
    im = [stage[kap, from_rows, 128:256] for kap in range(8)]
    out = dft8(re, im)
    for t in range(total.shape[0]):
        a, b = out[t % 8]
        c, d = total[t, rows, 0:128], total[t, rows, 128:256]
        if t:
            cos, sin = math.cos(math.pi * t / 32), math.sin(math.pi * t / 32)
            if t == 8:
                c, d = (c - d) * EIGHTH, (c + d) * EIGHTH
            else:
                c, d = c * cos - d * sin, c * sin + d * cos
        a, b = a + c, b + d
        if store is None:
            total[t, rows, 0:128] = a
            total[t, rows, 128:256] = b
        else:
            store(t, rows, (a * a + b * b) * (1.0 / N))


def main_part(signal, left_high, left_low, even, odd, wide, narrow, power_ref, own, send, meanwhile, ready):
    def both(lam, fill, drain):
        for kap in range(8):
            k = lam + 8 * kap
            factors = windows(k, signal) if kap else (ready[0], ready[1])
            products(k, kap, factors, left_high, left_low, fill)
            for g in range(2):
                combine(drain, wide, 0, kap * 16 + g * 8)
                combine(drain, narrow, 1, kap * 16 + g * 8)
        ready[0], ready[1] = windows(jnp.maximum(lam - 1, 0), signal)

    for kap in range(8):
        products(7 + 8 * kap, kap, windows(7 + 8 * kap, signal), left_high, left_low, odd)
    ready[0], ready[1] = windows(6, signal)

    def step(i, _):
        @pl.when(i % 2 == 0)
        def _():
            both(6 - i, even, odd)

        @pl.when(i % 2 == 1)
        def _():
            both(6 - i, odd, even)

        return 0

    lax.fori_loop(0, 7, step, 0)
    places = [jnp.where(own == half, own, 3) for half in range(2)]

    def keep_wide(t, rows, value):
        power_ref[places[t // 8], t % 8, rows, :] = value

    def keep_narrow(t, rows, value):
        power_ref[2, t, rows, :] = value

    def finish_wide(first, last):
        def one(c, _):
            combine(even, wide, 0, pl.multiple_of(c * 8, 8), keep_wide)
            return 0

        lax.fori_loop(first, last, one, 0)

    def finish_narrow(first, last):
        def one(c, _):
            combine(even, narrow, 1, pl.multiple_of(c * 8, 8), keep_narrow)
            return 0

        lax.fori_loop(first, last, one, 0, unroll=2)

    finish_wide(0, 8)
    finish_narrow(0, 2)
    copies = [send(0)]
    finish_wide(8, 16)
    finish_narrow(2, 4)
    copies.append(send(1))
    meanwhile()
    finish_narrow(4, 16)
    for copy in copies:
        copy.wait()


def compute_kernel(centers_hbm, widths_hbm, samples_ref, chips_hbm, *refs):
    count = len(NAMES)
    hbm = dict(zip(NAMES, refs[:count]))
    power_ref, mean_ref = refs[count : count + 2]
    refs = refs[count + 2 :]
    table = dict(zip(NAMES, refs[:count]))
    (centers, widths, gathered, chips, chip_rows, spectrum, code, left_high, left_low, signal, even, odd, wide, narrow, ready,
     own_sem, table_sem, send_sem, recv_sem) = refs[count:]
    sat = lax.axis_index("sat")
    dop = lax.axis_index("dop")
    x, z = sat // 4, sat % 4
    me = sat * 8 + dop
    own_sat = dop % 2
    barrier = pltpu.get_barrier_semaphore()
    peers = [{"sat": sat, "dop": (dop + step) % 8} for step in range(1, 8)]
    for step in range(1, 16):
        peers.append({"sat": (x + step // 4) % 4 * 4 + (z + step % 4) % 4, "dop": dop})
    for peer in peers:
        pl.semaphore_signal(barrier, inc=1, device_id=peer, device_id_type=MESH)
    own = pltpu.make_async_copy(samples_ref, gathered.at[me], own_sem)
    own.start()
    loads = {"chips": pltpu.make_async_copy(chips_hbm, chips, table_sem.at[count])}
    loads["chips"].start()
    loads["centers"] = pltpu.make_async_copy(centers_hbm, centers, table_sem.at[count + 1])
    loads["centers"].start()
    loads["widths"] = pltpu.make_async_copy(widths_hbm, widths, table_sem.at[count + 2])
    loads["widths"].start()
    for i, name in enumerate(NAMES):
        loads[name] = pltpu.make_async_copy(hbm[name], table[name], table_sem.at[i])
        loads[name].start()

    def exchange(first, size, start, targets, source):
        copies = []
        for i, peer in enumerate(targets):
            copies.append(
                pltpu.make_async_remote_copy(
                    src_ref=source,
                    dst_ref=gathered.at[pl.ds(start, size)],
                    send_sem=send_sem.at[first + i],
                    recv_sem=recv_sem.at[first + i],
                    device_id=peer,
                    device_id_type=MESH,
                )
            )
            copies[-1].start()
        return copies

    for name in ("chips", "centers", "code_first", "code_twiddle", "right"):
        loads[name].wait()
    code_part(centers, chips, dop, table["code_first"], table["code_twiddle"], table["right"], chip_rows, spectrum, code)
    own.wait()
    pl.semaphore_wait(barrier, 22)
    copies = exchange(0, 1, me, peers[:7], gathered.at[pl.ds(me, 1)])
    wide[...] = jnp.zeros_like(wide)
    narrow[...] = jnp.zeros_like(narrow)
    for name in ("widths", "inverse", "step", "left", "signal_first", "signal_twiddle", "window"):
        loads[name].wait()
    table_part(code, own_sat, table["inverse"], table["step"], left_high, left_low, 0, 3)
    for copy in copies:
        copy.wait()
    copies = exchange(7, 8, sat * 8, peers[7:], gathered.at[pl.ds(sat * 8, 8)])
    table_part(code, own_sat, table["inverse"], table["step"], left_high, left_low, 3, 8)
    for copy in copies:
        copy.wait()
    rows = jnp.concatenate([gathered[:, 0, :], gathered[:, 1, :]], 1)
    signal[...] = signal_part(rows, table["left"], table["signal_first"], table["signal_twiddle"])

    def send(half):
        rows = pl.ds(half * 64, 64)
        copy = pltpu.make_async_remote_copy(
            src_ref=power_ref.at[3, :, rows],
            dst_ref=power_ref.at[own_sat, :, rows],
            send_sem=send_sem.at[22 + half],
            recv_sem=recv_sem.at[22 + half],
            device_id={"sat": sat, "dop": dop + 1 - 2 * own_sat},
            device_id_type=MESH,
        )
        copy.start()
        return copy

    main_part(signal, left_high, left_low, even, odd, wide, narrow, power_ref, own_sat, send,
              lambda: mean_part(signal, table["window"], code, widths, mean_ref), ready)


def vmem():
    return pl.BlockSpec(memory_space=pltpu.VMEM)


def computed(centers, widths, samples, chips, tables):
    return pl.pallas_call(
        compute_kernel,
        out_shape=[
            jax.ShapeDtypeStruct((SATS + 1, THI, 128, DOP), F32),
            jax.ShapeDtypeStruct((SATS, 8, 128), F32),
        ],
        in_specs=[pl.BlockSpec(memory_space=pltpu.HBM)] * (4 + len(tables)),
        out_specs=[vmem(), vmem()],
        scratch_shapes=[pltpu.VMEM(t.shape, t.dtype) for t in tables]
        + [
            pltpu.SMEM((SATS,), jnp.int32),
            pltpu.SMEM((SATS,), jnp.int32),
            pltpu.VMEM((128, 2, 64), F32),
            pltpu.VMEM((SATS, CHIPS), jnp.int32),
            pltpu.VMEM((96, 128), F32),
            pltpu.VMEM((SATS, 128, 256), F32),
            pltpu.VMEM((SATS, 2, KLO, 128), F32),
            pltpu.VMEM((KLO, 256, 256), BF16),
            pltpu.VMEM((KLO, 256, 256), BF16),
            pltpu.VMEM((256, 256), F32),
            pltpu.VMEM((8, 256, 256), F32),
            pltpu.VMEM((8, 256, 256), F32),
            pltpu.VMEM((2 * THI, 128, 256), F32),
            pltpu.VMEM((THI, 128, 256), F32),
            pltpu.VMEM((2, 256, 256), BF16),
            pltpu.SemaphoreType.DMA,
            pltpu.SemaphoreType.DMA((len(tables) + 3,)),
            pltpu.SemaphoreType.DMA((24,)),
            pltpu.SemaphoreType.DMA((24,)),
        ],
        compiler_params=pltpu.CompilerParams(vmem_limit_bytes=40 << 20, collective_id=0, has_side_effects=True),
        name="compute",
    )(centers, widths, samples, chips, *tables)


def finish_kernel(power_ref, mean_ref, out_ref, ratios, sem):
    r = lax.broadcasted_iota(jnp.int32, (DOP, DOP), 0)
    q = lax.broadcasted_iota(jnp.int32, (DOP, DOP), 1)
    gap = jnp.abs(r - q)
    copies = []
    for s in range(SATS):
        band = ((gap >= 2) & (gap.astype(F32) <= 1.0 + mean_ref[s, 1:2, :])).astype(F32)
        scale = 1.0 / jnp.sum(band, axis=0, keepdims=True)
        band = band.astype(BF16)
        band = jnp.concatenate([band, band], 0)
        floor = mean_ref[s, 0:1, :] * 0.25 + 1e-6
        for t in range(THI):
            power = power_ref[s, t]
            high, low = split(power)
            around = dot(jnp.concatenate([high, low], 1), band)
            ratio = power / (around * scale + floor)
            ratios[s, :, t * 128 : t * 128 + 128] = ratio.T
        copies.append(pltpu.make_async_copy(ratios.at[s], out_ref.at[s], sem.at[s]))
        copies[-1].start()
    for copy in copies:
        copy.wait()


def finished(power, mean):
    return pl.pallas_call(
        finish_kernel,
        out_shape=jax.ShapeDtypeStruct((SATS, DOP, THI * 128), F32),
        in_specs=[vmem(), vmem()],
        out_specs=pl.BlockSpec(memory_space=pl.ANY),
        scratch_shapes=[pltpu.VMEM((SATS, DOP, THI * 128), F32), pltpu.SemaphoreType.DMA((SATS,))],
        compiler_params=pltpu.CompilerParams(vmem_limit_bytes=16 << 20),
        name="finish",
    )(power, mean)


def on_device(samples, code_chips, centers, widths):
    tables = build_tables()
    places = [centers, widths, samples, code_chips] + [jnp.asarray(tables[n]) for n in NAMES]
    places = [pltpu.with_memory_space_constraint(a, pltpu.HBM) for a in places]
    power, mean = computed(*places[:4], places[4:])
    return finished(power, mean)


def solution(mesh):
    both = ("sat", "dop")
    return jax.shard_map(
        on_device,
        mesh=mesh,
        in_specs=(P(None, both), P("sat", None), P("sat"), P("sat")),
        out_specs=P("sat", None, "dop"),
        check_vma=False,
    )
```

```python
import math

import jax
import jax.numpy as jnp
import numpy as np
from jax import lax
from jax.experimental import pallas as pl
from jax.experimental.pallas import tpu as pltpu
from jax.sharding import PartitionSpec as P

N = 8192
CHIPS = 4092
DOP = 128
SATS = 3
KLO = 64
KHI = 128
THI = 8
F32 = jnp.float32
BF16 = jnp.bfloat16
MESH = pl.DeviceIdType.MESH


def split_np(table):
    table = np.asarray(table, np.float32)
    high = table.astype(jnp.bfloat16)
    low = (table - high.astype(np.float32)).astype(jnp.bfloat16)
    return high, low


def split(value):
    high = value.astype(BF16)
    low = (value - high.astype(F32)).astype(BF16)
    return high, low


def dot(left, right):
    return jnp.dot(left, right, preferred_element_type=F32)


def phase(turns):
    return np.cos(2 * np.pi * turns), np.sin(2 * np.pi * turns)


def build_tables():
    out = {}
    kappa = np.arange(-32, 96)
    order = np.concatenate([np.arange(0, 64, 2), np.arange(1, 64, 2)])
    cos, sin = phase(-(kappa[:, None] * order[None, :] % 64) / 64)
    high, low = split_np(np.concatenate([cos, sin], 0))
    out["code_first"] = np.concatenate([high, low], 1)
    lanes = np.arange(128)
    out["code_twiddle"] = np.stack(phase(-(kappa[:, None] * lanes[None, :] % N) / N)).astype(np.float32)
    cos, sin = phase((lanes[:, None] * lanes[None, :] % 128) / 128)
    high, low = split_np(np.block([[cos, -sin], [sin, cos]]))
    out["right"] = np.stack([high, low])
    high, low = split_np(np.block([[cos, sin], [-sin, cos]]))
    out["left"] = np.stack([high, low])
    rho = np.arange(-64, 192)
    device = np.arange(128)
    cos, sin = phase(-((device[:, None] // 2) * rho[None, :] % 128) / 128)
    columns = []
    for parity in range(2):
        keep = (device % 2 == parity)[:, None]
        columns += [cos * keep, sin * keep]
    high, low = split_np(np.concatenate(columns, 1))
    out["signal_first"] = np.stack([high, low])
    out["signal_twiddle"] = np.stack(phase(-(lanes[:, None] * rho[None, :] % (2 * N)) / (2 * N))).astype(np.float32)
    out["inverse"] = np.stack(phase((lanes[:, None] * lanes[None, :] % 128) / 128)).astype(np.float32)
    step = phase(np.broadcast_to(lanes[:, None], (128, 128)) / N)
    out["step"] = np.stack(step).astype(np.float32)
    first = np.arange(256)[None, :] - 2 * np.arange(KLO)[:, None]
    out["window"] = ((first >= 0) & (first < 128)).astype(jnp.bfloat16)
    return out


NAMES = ["code_first", "code_twiddle", "right", "left", "signal_first", "signal_twiddle", "inverse", "step", "window"]


def eighth_turns(turns):
    half = jnp.where(turns >= 4, -1.0, 1.0)
    part = turns & 3
    cos = jnp.where(part == 0, 1.0, jnp.where(part == 1, EIGHTH, jnp.where(part == 2, 0.0, -EIGHTH)))
    sin = jnp.where(part == 0, 0.0, jnp.where(part == 2, 1.0, EIGHTH))
    return cos * half, sin * half


def code_part(centers_ref, chips_ref, dop, code_first, code_twiddle, right, chip_rows, spectrum, code):
    chip_rows[...] = jnp.zeros_like(chip_rows)
    for s in range(SATS):
        for a in range(32):
            width = 128 if a < 31 else CHIPS - 31 * 128
            chip_rows[pl.ds(s * 32 + a, 1), 0:width] = chips_ref[s : s + 1, a * 128 : a * 128 + width].astype(F32)
    rows = chip_rows[...]
    lane = lax.broadcasted_iota(jnp.int32, (96, 128), 1)
    index = lax.broadcasted_iota(jnp.int32, (96, 128), 0)
    turned = pltpu.roll(rows, 64, 1)
    above = pltpu.roll(turned, 1, 0)
    odd = jnp.where(lane < 64, above, turned)
    both = jnp.concatenate([odd, rows], 0).astype(BF16)
    sample = lax.broadcasted_iota(jnp.int32, (128, 128), 1)
    chip = lax.broadcasted_iota(jnp.int32, (128, 128), 0)
    kind = lax.broadcasted_iota(jnp.int32, (192, 128), 0) % 32 // 4
    replica = jnp.zeros((192, 128), F32)
    for i in range(8):
        shifted = sample + (7 - i)
        hit = chip == 60 + (shifted >> 1)
        sign = 1.0 - 2.0 * (shifted & 1).astype(F32)
        select = jnp.where(hit, sign, 0.0).astype(BF16)
        replica = jnp.where(kind == i, dot(both, select), replica)
    start = (lax.broadcasted_iota(jnp.int32, (192, 128), 0) < 96) & (
        lax.broadcasted_iota(jnp.int32, (192, 128), 0) % 4 == 0
    ) & (lax.broadcasted_iota(jnp.int32, (192, 128), 1) == 0)
    replica = jnp.where(start, pltpu.roll(replica, 127, 1), replica).astype(BF16)
    for s in range(SATS):
        part = jnp.concatenate([replica[s * 32 : s * 32 + 32], replica[96 + s * 32 : 128 + s * 32]], 0)
        stage = dot(code_first[...], jnp.concatenate([part, part], 0))
        re, im = stage[:128], stage[128:]
        cos, sin = code_twiddle[0], code_twiddle[1]
        turned = jnp.concatenate([re * cos - im * sin, im * cos + re * sin], 1)
        high, low = split(turned)
        spectrum[s] = dot(
            jnp.concatenate([high, low, high], 1),
            jnp.concatenate([right[0], right[0], right[1]], 0),
        )
    row = lax.broadcasted_iota(jnp.int32, (KLO, 128), 0)
    for s in range(SATS):
        block = dop if s == 2 else dop // 2 * 2
        cos, sin = eighth_turns(row * block & 7)
        cos, sin = cos * (1.0 / N), sin * (1.0 / N)
        shifted = pltpu.roll(spectrum[s], 96 + centers_ref[s], 0)[:KLO]
        re, im = shifted[:, :128], shifted[:, 128:256]
        code[s, 0] = re * cos + im * sin
        code[s, 1] = re * sin - im * cos


def table_part(code, own, inverse, step, left_high, left_low, first, last):
    def group(g, _):
        at = pl.multiple_of(g * 16, 16)
        rows = pl.ds(at, 16)
        step_re, step_im = step[0, rows, :], step[1, rows, :]

        def one(k, carry):
            e_re, e_im = carry
            for slot, s in ((0, own), (1, 2)):
                c_re = code[s, 0, pl.ds(k, 1), :]
                c_im = code[s, 1, pl.ds(k, 1), :]
                m_re = e_re * c_re - e_im * c_im
                m_im = e_re * c_im + e_im * c_re
                into = pl.ds(pl.multiple_of(slot * 128 + at, 16), 16)
                high, low = split(m_re)
                left_high[k, into, 0:128] = high
                left_low[k, into, 0:128] = low
                high, low = split(m_im)
                left_high[k, into, 128:256] = high
                left_low[k, into, 128:256] = low
            return e_re * step_re - e_im * step_im, e_re * step_im + e_im * step_re

        lax.fori_loop(0, KLO, one, (inverse[0, rows, :], inverse[1, rows, :]), unroll=4)
        return 0

    lax.fori_loop(first, last, group, 0)


def signal_part(rows, left, signal_first, signal_twiddle):
    turned = rows.T
    high, low = split(turned)
    stage = dot(
        jnp.concatenate([high, low, high], 1),
        jnp.concatenate([signal_first[0], signal_first[0], signal_first[1]], 0),
    )
    re, im = [], []
    for parity in range(2):
        cos = stage[:, parity * 512 : parity * 512 + 256]
        sin = stage[:, parity * 512 + 256 : parity * 512 + 512]
        re.append(cos[:64] - sin[64:])
        im.append(sin[:64] + cos[64:])
    re, im = jnp.concatenate(re, 0), jnp.concatenate(im, 0)
    cos, sin = signal_twiddle[0], signal_twiddle[1]
    both = jnp.concatenate([re * cos - im * sin, im * cos + re * sin], 0)
    high, low = split(both)
    return dot(
        jnp.concatenate([left[0], left[1], left[0]], 1),
        jnp.concatenate([high, high, low], 0),
    )


def mean_part(signal, window, code, widths, mean_ref):
    size = signal[0:128, :] * signal[0:128, :] + signal[128:256, :] * signal[128:256, :]
    high, low = split(size)
    under = lax.dot_general(
        jnp.concatenate([window[...], window[...]], 1),
        jnp.concatenate([high, low], 1),
        (((1,), (1,)), ((), ())),
        preferred_element_type=F32,
    )
    for s in range(SATS):
        re, im = code[s, 0], code[s, 1]
        total = jnp.sum(under * (re * re + im * im), axis=(0, 1), keepdims=True)
        mean = jnp.broadcast_to(total * (1.0 / (DOP * N)), (8, 128))
        width = jnp.full((8, 128), widths[s].astype(F32))
        mean_ref[s] = jnp.where(lax.broadcasted_iota(jnp.int32, (8, 128), 0) == 0, mean, width)


EIGHTH = math.sqrt(0.5)


def dft8(re, im):
    def add(a, b):
        return (a[0] + b[0], a[1] + b[1])

    def sub(a, b):
        return (a[0] - b[0], a[1] - b[1])

    def turn(a):
        return (-a[1], a[0])

    v = list(zip(re, im))

    def dft4(a, b, c, d):
        p, m = add(a, c), sub(a, c)
        q, n = add(b, d), turn(sub(b, d))
        return add(p, q), add(m, n), sub(p, q), sub(m, n)

    e = dft4(v[0], v[2], v[4], v[6])
    o = dft4(v[1], v[3], v[5], v[7])
    w1 = ((o[1][0] - o[1][1]) * EIGHTH, (o[1][0] + o[1][1]) * EIGHTH)
    w2 = turn(o[2])
    w3 = ((-o[3][0] - o[3][1]) * EIGHTH, (o[3][0] - o[3][1]) * EIGHTH)
    w = [o[0], w1, w2, w3]
    return [add(e[i], w[i]) for i in range(4)] + [sub(e[i], w[i]) for i in range(4)]


def windows(k, signal):
    lane = lax.broadcasted_iota(jnp.int32, (256, 128), 1)
    shift = 128 - 2 * k

    def embedded(i):
        part = jnp.where(
            lane < shift,
            pltpu.roll(signal[i, :, 0:128], shift, 1),
            pltpu.roll(signal[i, :, 128:256], shift, 1),
        )
        re, im = part[:128], part[128:]
        return jnp.concatenate([jnp.concatenate([re, im], 1), jnp.concatenate([-im, re], 1)], 0)

    return embedded(0), embedded(1)


def products(k, kap, factors, left_high, left_low, stage):
    high, low = factors
    m_high, m_low = left_high[k], left_low[k]
    stage[kap] = dot(jnp.concatenate([m_high, m_low, m_high], 1), jnp.concatenate([high, high, low], 0))


def combine(stage, total, slot, row, store=None, first=False):
    rows = pl.ds(row, 8)
    from_rows = pl.ds(slot * 128 + row, 8)
    re = [stage[kap, from_rows, 0:128] for kap in range(8)]
    im = [stage[kap, from_rows, 128:256] for kap in range(8)]
    out = dft8(re, im)
    for t in range(total.shape[0]):
        a, b = out[t % 8]
        if not first:
            c, d = total[t, rows, 0:128], total[t, rows, 128:256]
            cos, sin = math.cos(math.pi * t / 32), math.sin(math.pi * t / 32)
            if t == 8:
                c, d = (c - d) * EIGHTH, (c + d) * EIGHTH
            elif t:
                c, d = c * cos - d * sin, c * sin + d * cos
            a, b = a + c, b + d
        if store is None:
            total[t, rows, 0:128] = a
            total[t, rows, 128:256] = b
        else:
            store(t, rows, (a * a + b * b) * (1.0 / N))


def main_part(signal_full, left_high, left_low, even, odd, wide, narrow, power_ref, own, send, meanwhile, ready, pieces):
    def both(lam, fill, drain, first=False):
        for kap in range(8):
            k = lam + 8 * kap
            factors = windows(k, signal) if kap else (ready[0], ready[1])
            products(k, kap, factors, left_high, left_low, fill)
            for g in range(2):
                combine(drain, wide, 0, kap * 16 + g * 8, first=first)
                combine(drain, narrow, 1, kap * 16 + g * 8, first=first)
        ready[0], ready[1] = windows(jnp.maximum(lam - 1, 0), signal)

    signal = pieces
    signal[0], signal[1] = split(signal_full[...])
    for kap in range(8):
        products(7 + 8 * kap, kap, windows(7 + 8 * kap, signal), left_high, left_low, odd)
    ready[0], ready[1] = windows(6, signal)

    def step(i, _):
        @pl.when(i % 2 == 0)
        def _():
            both(6 - i, even, odd)

        @pl.when(i % 2 == 1)
        def _():
            both(6 - i, odd, even)

        return 0

    both(6, even, odd, first=True)
    lax.fori_loop(1, 7, step, 0)
    places = [jnp.where(own == half, own, 3) for half in range(2)]

    def keep_wide(t, rows, value):
        power_ref[places[t // 8], t % 8, rows, :] = value

    def keep_narrow(t, rows, value):
        power_ref[2, t, rows, :] = value

    def finish_wide(first, last):
        def one(c, _):
            combine(even, wide, 0, pl.multiple_of(c * 8, 8), keep_wide)
            return 0

        lax.fori_loop(first, last, one, 0)

    def finish_narrow(first, last):
        def one(c, _):
            combine(even, narrow, 1, pl.multiple_of(c * 8, 8), keep_narrow)
            return 0

        lax.fori_loop(first, last, one, 0, unroll=2)

    finish_wide(0, 8)
    finish_narrow(0, 2)
    copies = [send(0)]
    finish_wide(8, 16)
    finish_narrow(2, 4)
    copies.append(send(1))
    meanwhile()
    finish_narrow(4, 16)
    for copy in copies:
        copy.wait()


def compute_kernel(centers_hbm, widths_hbm, samples_ref, chips_hbm, *refs):
    count = len(NAMES)
    hbm = dict(zip(NAMES, refs[:count]))
    power_ref, mean_ref = refs[count : count + 2]
    refs = refs[count + 2 :]
    table = dict(zip(NAMES, refs[:count]))
    (centers, widths, gathered, chips, chip_rows, spectrum, code, left_high, left_low, signal, even, odd, wide, narrow, ready, pieces,
     own_sem, table_sem, send_sem, recv_sem) = refs[count:]
    sat = lax.axis_index("sat")
    dop = lax.axis_index("dop")
    x, z = sat // 4, sat % 4
    me = sat * 8 + dop
    own_sat = dop % 2
    barrier = pltpu.get_barrier_semaphore()
    peers = [{"sat": sat, "dop": (dop + step) % 8} for step in range(1, 8)]
    for step in range(1, 16):
        peers.append({"sat": (x + step // 4) % 4 * 4 + (z + step % 4) % 4, "dop": dop})
    for peer in peers:
        pl.semaphore_signal(barrier, inc=1, device_id=peer, device_id_type=MESH)
    own = pltpu.make_async_copy(samples_ref, gathered.at[me], own_sem)
    own.start()
    loads = {"chips": pltpu.make_async_copy(chips_hbm, chips, table_sem.at[count])}
    loads["chips"].start()
    loads["centers"] = pltpu.make_async_copy(centers_hbm, centers, table_sem.at[count + 1])
    loads["centers"].start()
    loads["widths"] = pltpu.make_async_copy(widths_hbm, widths, table_sem.at[count + 2])
    loads["widths"].start()
    for i, name in enumerate(NAMES):
        loads[name] = pltpu.make_async_copy(hbm[name], table[name], table_sem.at[i])
        loads[name].start()

    def exchange(first, size, start, targets, source):
        copies = []
        for i, peer in enumerate(targets):
            copies.append(
                pltpu.make_async_remote_copy(
                    src_ref=source,
                    dst_ref=gathered.at[pl.ds(start, size)],
                    send_sem=send_sem.at[first + i],
                    recv_sem=recv_sem.at[first + i],
                    device_id=peer,
                    device_id_type=MESH,
                )
            )
            copies[-1].start()
        return copies

    for name in ("chips", "centers", "code_first", "code_twiddle", "right"):
        loads[name].wait()
    code_part(centers, chips, dop, table["code_first"], table["code_twiddle"], table["right"], chip_rows, spectrum, code)
    own.wait()
    pl.semaphore_wait(barrier, 22)
    copies = exchange(0, 1, me, peers[:7], gathered.at[pl.ds(me, 1)])
    for name in ("widths", "inverse", "step", "left", "signal_first", "signal_twiddle", "window"):
        loads[name].wait()
    table_part(code, own_sat, table["inverse"], table["step"], left_high, left_low, 0, 3)
    for copy in copies:
        copy.wait()
    copies = exchange(7, 8, sat * 8, peers[7:], gathered.at[pl.ds(sat * 8, 8)])
    table_part(code, own_sat, table["inverse"], table["step"], left_high, left_low, 3, 8)
    for copy in copies:
        copy.wait()
    rows = jnp.concatenate([gathered[:, 0, :], gathered[:, 1, :]], 1)
    signal[...] = signal_part(rows, table["left"], table["signal_first"], table["signal_twiddle"])

    def send(half):
        rows = pl.ds(half * 64, 64)
        copy = pltpu.make_async_remote_copy(
            src_ref=power_ref.at[3, :, rows],
            dst_ref=power_ref.at[own_sat, :, rows],
            send_sem=send_sem.at[22 + half],
            recv_sem=recv_sem.at[22 + half],
            device_id={"sat": sat, "dop": dop + 1 - 2 * own_sat},
            device_id_type=MESH,
        )
        copy.start()
        return copy

    main_part(signal, left_high, left_low, even, odd, wide, narrow, power_ref, own_sat, send,
              lambda: mean_part(signal, table["window"], code, widths, mean_ref), ready, pieces)


def vmem():
    return pl.BlockSpec(memory_space=pltpu.VMEM)


def computed(centers, widths, samples, chips, tables):
    return pl.pallas_call(
        compute_kernel,
        out_shape=[
            jax.ShapeDtypeStruct((SATS + 1, THI, 128, DOP), F32),
            jax.ShapeDtypeStruct((SATS, 8, 128), F32),
        ],
        in_specs=[pl.BlockSpec(memory_space=pltpu.HBM)] * (4 + len(tables)),
        out_specs=[vmem(), vmem()],
        scratch_shapes=[pltpu.VMEM(t.shape, t.dtype) for t in tables]
        + [
            pltpu.SMEM((SATS,), jnp.int32),
            pltpu.SMEM((SATS,), jnp.int32),
            pltpu.VMEM((128, 2, 64), F32),
            pltpu.VMEM((SATS, CHIPS), jnp.int32),
            pltpu.VMEM((96, 128), F32),
            pltpu.VMEM((SATS, 128, 256), F32),
            pltpu.VMEM((SATS, 2, KLO, 128), F32),
            pltpu.VMEM((KLO, 256, 256), BF16),
            pltpu.VMEM((KLO, 256, 256), BF16),
            pltpu.VMEM((256, 256), F32),
            pltpu.VMEM((8, 256, 256), F32),
            pltpu.VMEM((8, 256, 256), F32),
            pltpu.VMEM((2 * THI, 128, 256), F32),
            pltpu.VMEM((THI, 128, 256), F32),
            pltpu.VMEM((2, 256, 256), BF16),
            pltpu.VMEM((2, 256, 256), BF16),
            pltpu.SemaphoreType.DMA,
            pltpu.SemaphoreType.DMA((len(tables) + 3,)),
            pltpu.SemaphoreType.DMA((24,)),
            pltpu.SemaphoreType.DMA((24,)),
        ],
        compiler_params=pltpu.CompilerParams(vmem_limit_bytes=40 << 20, collective_id=0, has_side_effects=True),
        name="compute",
    )(centers, widths, samples, chips, *tables)


def finish_kernel(power_ref, mean_ref, out_ref, ratios, sem):
    r = lax.broadcasted_iota(jnp.int32, (DOP, DOP), 0)
    q = lax.broadcasted_iota(jnp.int32, (DOP, DOP), 1)
    gap = jnp.abs(r - q)
    copies = []
    for s in range(SATS):
        band = ((gap >= 2) & (gap.astype(F32) <= 1.0 + mean_ref[s, 1:2, :])).astype(F32)
        scale = 1.0 / jnp.sum(band, axis=0, keepdims=True)
        band = band.astype(BF16)
        band = jnp.concatenate([band, band], 0)
        floor = mean_ref[s, 0:1, :] * 0.25 + 1e-6
        for t in range(THI):
            power = power_ref[s, t]
            high, low = split(power)
            around = dot(jnp.concatenate([high, low], 1), band)
            ratio = power / (around * scale + floor)
            ratios[s, :, t * 128 : t * 128 + 128] = ratio.T
        copies.append(pltpu.make_async_copy(ratios.at[s], out_ref.at[s], sem.at[s]))
        copies[-1].start()
    for copy in copies:
        copy.wait()


def finished(power, mean):
    return pl.pallas_call(
        finish_kernel,
        out_shape=jax.ShapeDtypeStruct((SATS, DOP, THI * 128), F32),
        in_specs=[vmem(), vmem()],
        out_specs=pl.BlockSpec(memory_space=pl.ANY),
        scratch_shapes=[pltpu.VMEM((SATS, DOP, THI * 128), F32), pltpu.SemaphoreType.DMA((SATS,))],
        compiler_params=pltpu.CompilerParams(vmem_limit_bytes=16 << 20),
        name="finish",
    )(power, mean)


def on_device(samples, code_chips, centers, widths):
    tables = build_tables()
    places = [centers, widths, samples, code_chips] + [jnp.asarray(tables[n]) for n in NAMES]
    places = [pltpu.with_memory_space_constraint(a, pltpu.HBM) for a in places]
    power, mean = computed(*places[:4], places[4:])
    return finished(power, mean)


def solution(mesh):
    both = ("sat", "dop")
    return jax.shard_map(
        on_device,
        mesh=mesh,
        in_specs=(P(None, both), P("sat", None), P("sat"), P("sat")),
        out_specs=P("sat", None, "dop"),
        check_vma=False,
    )
```

```python
import math

import jax
import jax.numpy as jnp
import numpy as np
from jax import lax
from jax.experimental import pallas as pl
from jax.experimental.pallas import tpu as pltpu
from jax.sharding import PartitionSpec as P

N = 8192
CHIPS = 4092
DOP = 128
SATS = 3
KLO = 64
KHI = 128
THI = 8
F32 = jnp.float32
BF16 = jnp.bfloat16
MESH = pl.DeviceIdType.MESH


def split_np(table):
    table = np.asarray(table, np.float32)
    high = table.astype(jnp.bfloat16)
    low = (table - high.astype(np.float32)).astype(jnp.bfloat16)
    return high, low


def split(value):
    high = value.astype(BF16)
    low = (value - high.astype(F32)).astype(BF16)
    return high, low


def dot(left, right):
    return jnp.dot(left, right, preferred_element_type=F32)


def phase(turns):
    return np.cos(2 * np.pi * turns), np.sin(2 * np.pi * turns)


def build_tables():
    out = {}
    kappa = np.arange(-32, 96)
    order = np.concatenate([np.arange(0, 64, 2), np.arange(1, 64, 2)])
    cos, sin = phase(-(kappa[:, None] * order[None, :] % 64) / 64)
    high, low = split_np(np.concatenate([cos, sin], 0))
    out["code_first"] = np.concatenate([high, low], 1)
    lanes = np.arange(128)
    out["code_twiddle"] = np.stack(phase(-(kappa[:, None] * lanes[None, :] % N) / N)).astype(np.float32)
    cos, sin = phase((lanes[:, None] * lanes[None, :] % 128) / 128)
    high, low = split_np(np.block([[cos, -sin], [sin, cos]]))
    out["right"] = np.stack([high, low])
    high, low = split_np(np.block([[cos, sin], [-sin, cos]]))
    out["left"] = np.stack([high, low])
    rho = np.arange(-64, 192)
    device = np.arange(128)
    cos, sin = phase(-((device[:, None] // 2) * rho[None, :] % 128) / 128)
    columns = []
    for parity in range(2):
        keep = (device % 2 == parity)[:, None]
        columns += [cos * keep, sin * keep]
    high, low = split_np(np.concatenate(columns, 1))
    out["signal_first"] = np.stack([high, low])
    out["signal_twiddle"] = np.stack(phase(-(lanes[:, None] * rho[None, :] % (2 * N)) / (2 * N))).astype(np.float32)
    out["inverse"] = np.stack(phase((lanes[:, None] * lanes[None, :] % 128) / 128)).astype(np.float32)
    step = phase(np.broadcast_to(lanes[:, None], (128, 128)) / N)
    out["step"] = np.stack(step).astype(np.float32)
    first = np.arange(256)[None, :] - 2 * np.arange(KLO)[:, None]
    out["window"] = ((first >= 0) & (first < 128)).astype(jnp.bfloat16)
    return out


NAMES = ["code_first", "code_twiddle", "right", "left", "signal_first", "signal_twiddle", "inverse", "step", "window"]


def eighth_turns(turns):
    half = jnp.where(turns >= 4, -1.0, 1.0)
    part = turns & 3
    cos = jnp.where(part == 0, 1.0, jnp.where(part == 1, EIGHTH, jnp.where(part == 2, 0.0, -EIGHTH)))
    sin = jnp.where(part == 0, 0.0, jnp.where(part == 2, 1.0, EIGHTH))
    return cos * half, sin * half


def code_part(centers_ref, chips_ref, dop, code_first, code_twiddle, right, chip_rows, spectrum, code):
    chip_rows[...] = jnp.zeros_like(chip_rows)
    for s in range(SATS):
        for a in range(32):
            width = 128 if a < 31 else CHIPS - 31 * 128
            chip_rows[pl.ds(s * 32 + a, 1), 0:width] = chips_ref[s : s + 1, a * 128 : a * 128 + width].astype(F32)
    rows = chip_rows[...]
    lane = lax.broadcasted_iota(jnp.int32, (96, 128), 1)
    index = lax.broadcasted_iota(jnp.int32, (96, 128), 0)
    turned = pltpu.roll(rows, 64, 1)
    above = pltpu.roll(turned, 1, 0)
    odd = jnp.where(lane < 64, above, turned)
    both = jnp.concatenate([odd, rows], 0).astype(BF16)
    sample = lax.broadcasted_iota(jnp.int32, (128, 128), 1)
    chip = lax.broadcasted_iota(jnp.int32, (128, 128), 0)
    kind = lax.broadcasted_iota(jnp.int32, (192, 128), 0) % 32 // 4
    replica = jnp.zeros((192, 128), F32)
    for i in range(8):
        shifted = sample + (7 - i)
        hit = chip == 60 + (shifted >> 1)
        sign = 1.0 - 2.0 * (shifted & 1).astype(F32)
        select = jnp.where(hit, sign, 0.0).astype(BF16)
        replica = jnp.where(kind == i, dot(both, select), replica)
    start = (lax.broadcasted_iota(jnp.int32, (192, 128), 0) < 96) & (
        lax.broadcasted_iota(jnp.int32, (192, 128), 0) % 4 == 0
    ) & (lax.broadcasted_iota(jnp.int32, (192, 128), 1) == 0)
    replica = jnp.where(start, pltpu.roll(replica, 127, 1), replica).astype(BF16)
    for s in range(SATS):
        part = jnp.concatenate([replica[s * 32 : s * 32 + 32], replica[96 + s * 32 : 128 + s * 32]], 0)
        stage = dot(code_first[...], jnp.concatenate([part, part], 0))
        re, im = stage[:128], stage[128:]
        cos, sin = code_twiddle[0], code_twiddle[1]
        turned = jnp.concatenate([re * cos - im * sin, im * cos + re * sin], 1)
        high, low = split(turned)
        spectrum[s] = dot(
            jnp.concatenate([high, low, high], 1),
            jnp.concatenate([right[0], right[0], right[1]], 0),
        )
    row = lax.broadcasted_iota(jnp.int32, (KLO, 128), 0)
    for s in range(SATS):
        block = dop if s == 2 else dop // 2 * 2
        cos, sin = eighth_turns(row * block & 7)
        cos, sin = cos * (1.0 / N), sin * (1.0 / N)
        shifted = pltpu.roll(spectrum[s], 96 + centers_ref[s], 0)[:KLO]
        re, im = shifted[:, :128], shifted[:, 128:256]
        code[s, 0] = re * cos + im * sin
        code[s, 1] = re * sin - im * cos


def table_part(code, own, inverse, step, left_high, left_low, first, last):
    def group(g, _):
        at = pl.multiple_of(g * 16, 16)
        rows = pl.ds(at, 16)
        step_re, step_im = step[0, rows, :], step[1, rows, :]

        def one(k, carry):
            e_re, e_im = carry
            for slot, s in ((0, own), (1, 2)):
                c_re = code[s, 0, pl.ds(k, 1), :]
                c_im = code[s, 1, pl.ds(k, 1), :]
                m_re = e_re * c_re - e_im * c_im
                m_im = e_re * c_im + e_im * c_re
                into = pl.ds(pl.multiple_of(slot * 128 + at, 16), 16)
                high, low = split(m_re)
                left_high[k, into, 0:128] = high
                left_low[k, into, 0:128] = low
                high, low = split(m_im)
                left_high[k, into, 128:256] = high
                left_low[k, into, 128:256] = low
            return e_re * step_re - e_im * step_im, e_re * step_im + e_im * step_re

        lax.fori_loop(0, KLO, one, (inverse[0, rows, :], inverse[1, rows, :]), unroll=4)
        return 0

    lax.fori_loop(first, last, group, 0)


def signal_part(rows, left, signal_first, signal_twiddle):
    turned = rows.T
    high, low = split(turned)
    stage = dot(
        jnp.concatenate([high, low, high], 1),
        jnp.concatenate([signal_first[0], signal_first[0], signal_first[1]], 0),
    )
    re, im = [], []
    for parity in range(2):
        cos = stage[:, parity * 512 : parity * 512 + 256]
        sin = stage[:, parity * 512 + 256 : parity * 512 + 512]
        re.append(cos[:64] - sin[64:])
        im.append(sin[:64] + cos[64:])
    re, im = jnp.concatenate(re, 0), jnp.concatenate(im, 0)
    cos, sin = signal_twiddle[0], signal_twiddle[1]
    both = jnp.concatenate([re * cos - im * sin, im * cos + re * sin], 0)
    high, low = split(both)
    return dot(
        jnp.concatenate([left[0], left[1], left[0]], 1),
        jnp.concatenate([high, high, low], 0),
    )


def mean_part(signal, window, code, widths, mean_ref):
    size = signal[0:128, :] * signal[0:128, :] + signal[128:256, :] * signal[128:256, :]
    high, low = split(size)
    under = lax.dot_general(
        jnp.concatenate([window[...], window[...]], 1),
        jnp.concatenate([high, low], 1),
        (((1,), (1,)), ((), ())),
        preferred_element_type=F32,
    )
    for s in range(SATS):
        re, im = code[s, 0], code[s, 1]
        total = jnp.sum(under * (re * re + im * im), axis=(0, 1), keepdims=True)
        mean = jnp.broadcast_to(total * (1.0 / (DOP * N)), (8, 128))
        width = jnp.full((8, 128), widths[s].astype(F32))
        mean_ref[s] = jnp.where(lax.broadcasted_iota(jnp.int32, (8, 128), 0) == 0, mean, width)


EIGHTH = math.sqrt(0.5)


def dft8(re, im):
    def add(a, b):
        return (a[0] + b[0], a[1] + b[1])

    def sub(a, b):
        return (a[0] - b[0], a[1] - b[1])

    def turn(a):
        return (-a[1], a[0])

    v = list(zip(re, im))

    def dft4(a, b, c, d):
        p, m = add(a, c), sub(a, c)
        q, n = add(b, d), turn(sub(b, d))
        return add(p, q), add(m, n), sub(p, q), sub(m, n)

    e = dft4(v[0], v[2], v[4], v[6])
    o = dft4(v[1], v[3], v[5], v[7])
    w1 = ((o[1][0] - o[1][1]) * EIGHTH, (o[1][0] + o[1][1]) * EIGHTH)
    w2 = turn(o[2])
    w3 = ((-o[3][0] - o[3][1]) * EIGHTH, (o[3][0] - o[3][1]) * EIGHTH)
    w = [o[0], w1, w2, w3]
    return [add(e[i], w[i]) for i in range(4)] + [sub(e[i], w[i]) for i in range(4)]


def windows(k, signal):
    lane = lax.broadcasted_iota(jnp.int32, (256, 128), 1)
    shift = 128 - 2 * k

    def embedded(i):
        part = jnp.where(
            lane < shift,
            pltpu.roll(signal[i, :, 0:128], shift, 1),
            pltpu.roll(signal[i, :, 128:256], shift, 1),
        )
        re, im = part[:128], part[128:]
        return jnp.concatenate([jnp.concatenate([re, im], 1), jnp.concatenate([-im, re], 1)], 0)

    return embedded(0), embedded(1)


def products(k, kap, factors, left_high, left_low, stage):
    high, low = factors
    m_high, m_low = left_high[k], left_low[k]
    stage[kap] = dot(jnp.concatenate([m_high, m_low, m_high], 1), jnp.concatenate([high, high, low], 0))


def combine(stage, total, slot, row, store=None, first=False):
    rows = pl.ds(row, 8)
    from_rows = pl.ds(slot * 128 + row, 8)
    re = [stage[kap, from_rows, 0:128] for kap in range(8)]
    im = [stage[kap, from_rows, 128:256] for kap in range(8)]
    out = dft8(re, im)
    for t in range(total.shape[0]):
        a, b = out[t % 8]
        if not first:
            c, d = total[t, rows, 0:128], total[t, rows, 128:256]
            cos, sin = math.cos(math.pi * t / 32), math.sin(math.pi * t / 32)
            if t == 8:
                c, d = (c - d) * EIGHTH, (c + d) * EIGHTH
            elif t:
                c, d = c * cos - d * sin, c * sin + d * cos
            a, b = a + c, b + d
        if store is None:
            total[t, rows, 0:128] = a
            total[t, rows, 128:256] = b
        else:
            store(t, rows, (a * a + b * b) * (1.0 / N))


def main_part(signal_full, left_high, left_low, even, odd, wide, narrow, power_ref, own, send, meanwhile, ready, pieces):
    def both(lam, fill, drain, first=False):
        for kap in range(8):
            k = lam + 8 * kap
            factors = windows(k, signal) if kap else (ready[0], ready[1])
            products(k, kap, factors, left_high, left_low, fill)
            for g in range(2):
                combine(drain, wide, 0, kap * 16 + g * 8, first=first)
                combine(drain, narrow, 1, kap * 16 + g * 8, first=first)
        ready[0], ready[1] = windows(jnp.maximum(lam - 1, 0), signal)

    signal = pieces
    signal[0], signal[1] = split(signal_full[...])
    for kap in range(8):
        products(7 + 8 * kap, kap, windows(7 + 8 * kap, signal), left_high, left_low, odd)
    ready[0], ready[1] = windows(6, signal)

    def step(i, _):
        @pl.when(i % 2 == 0)
        def _():
            both(6 - i, even, odd)

        @pl.when(i % 2 == 1)
        def _():
            both(6 - i, odd, even)

        return 0

    both(6, even, odd, first=True)
    lax.fori_loop(1, 7, step, 0)
    places = [jnp.where(own == half, own, 3) for half in range(2)]

    def keep_wide(t, rows, value):
        power_ref[places[t // 8], t % 8, rows, :] = value

    def keep_narrow(t, rows, value):
        power_ref[2, t, rows, :] = value

    def finish_wide(first, last):
        def one(c, _):
            combine(even, wide, 0, pl.multiple_of(c * 8, 8), keep_wide)
            return 0

        lax.fori_loop(first, last, one, 0)

    def finish_narrow(first, last):
        def one(c, _):
            combine(even, narrow, 1, pl.multiple_of(c * 8, 8), keep_narrow)
            return 0

        lax.fori_loop(first, last, one, 0, unroll=2)

    finish_wide(0, 8)
    finish_narrow(0, 2)
    copies = [send(0)]
    finish_wide(8, 16)
    finish_narrow(2, 4)
    copies.append(send(1))
    meanwhile()
    finish_narrow(4, 16)
    for copy in copies:
        copy.wait()


def compute_kernel(centers_hbm, widths_hbm, samples_ref, chips_hbm, *refs):
    count = len(NAMES)
    hbm = dict(zip(NAMES, refs[:count]))
    power_ref, mean_ref = refs[count : count + 2]
    refs = refs[count + 2 :]
    table = dict(zip(NAMES, refs[:count]))
    (centers, widths, gathered, chips, chip_rows, spectrum, code, left_high, left_low, signal, even, odd, wide, narrow, ready, pieces,
     own_sem, table_sem, send_sem, recv_sem) = refs[count:]
    sat = lax.axis_index("sat")
    dop = lax.axis_index("dop")
    x, z = sat // 4, sat % 4
    me = sat * 8 + dop
    own_sat = dop % 2
    barrier = pltpu.get_barrier_semaphore()
    y, core = dop // 2, dop % 2
    peers = []
    for step, other in ((2, 1), (2, 0), (1, 1), (1, 0), (3, 1), (3, 0), (0, 1)):
        peers.append({"sat": sat, "dop": (y + step) % 4 * 2 + (core + other) % 2})
    hops = (0, 1, 2, 1)
    steps = sorted(range(1, 16), key=lambda step: -(hops[step // 4] + hops[step % 4]))
    for step in steps:
        peers.append({"sat": (x + step // 4) % 4 * 4 + (z + step % 4) % 4, "dop": dop})
    for peer in peers[7:] + peers[:7]:
        pl.semaphore_signal(barrier, inc=1, device_id=peer, device_id_type=MESH)
    own = pltpu.make_async_copy(samples_ref, gathered.at[me], own_sem)
    own.start()
    loads = {"chips": pltpu.make_async_copy(chips_hbm, chips, table_sem.at[count])}
    loads["chips"].start()
    loads["centers"] = pltpu.make_async_copy(centers_hbm, centers, table_sem.at[count + 1])
    loads["centers"].start()
    loads["widths"] = pltpu.make_async_copy(widths_hbm, widths, table_sem.at[count + 2])
    loads["widths"].start()
    for i, name in enumerate(NAMES):
        loads[name] = pltpu.make_async_copy(hbm[name], table[name], table_sem.at[i])
        loads[name].start()

    def exchange(first, size, start, targets, source):
        copies = []
        for i, peer in enumerate(targets):
            copies.append(
                pltpu.make_async_remote_copy(
                    src_ref=source,
                    dst_ref=gathered.at[pl.ds(start, size)],
                    send_sem=send_sem.at[first + i],
                    recv_sem=recv_sem.at[first + i],
                    device_id=peer,
                    device_id_type=MESH,
                )
            )
            copies[-1].start()
        return copies

    for name in ("chips", "centers", "code_first", "code_twiddle", "right"):
        loads[name].wait()
    code_part(centers, chips, dop, table["code_first"], table["code_twiddle"], table["right"], chip_rows, spectrum, code)
    own.wait()
    pl.semaphore_wait(barrier, 22)
    copies = exchange(0, 1, me, peers[:7], gathered.at[pl.ds(me, 1)])
    for name in ("widths", "inverse", "step", "left", "signal_first", "signal_twiddle", "window"):
        loads[name].wait()
    table_part(code, own_sat, table["inverse"], table["step"], left_high, left_low, 0, 3)
    for copy in copies:
        copy.wait()
    copies = exchange(7, 8, sat * 8, peers[7:], gathered.at[pl.ds(sat * 8, 8)])
    table_part(code, own_sat, table["inverse"], table["step"], left_high, left_low, 3, 8)
    for copy in copies:
        copy.wait()
    rows = jnp.concatenate([gathered[:, 0, :], gathered[:, 1, :]], 1)
    signal[...] = signal_part(rows, table["left"], table["signal_first"], table["signal_twiddle"])

    def send(half):
        rows = pl.ds(half * 64, 64)
        copy = pltpu.make_async_remote_copy(
            src_ref=power_ref.at[3, :, rows],
            dst_ref=power_ref.at[own_sat, :, rows],
            send_sem=send_sem.at[22 + half],
            recv_sem=recv_sem.at[22 + half],
            device_id={"sat": sat, "dop": dop + 1 - 2 * own_sat},
            device_id_type=MESH,
        )
        copy.start()
        return copy

    main_part(signal, left_high, left_low, even, odd, wide, narrow, power_ref, own_sat, send,
              lambda: mean_part(signal, table["window"], code, widths, mean_ref), ready, pieces)


def vmem():
    return pl.BlockSpec(memory_space=pltpu.VMEM)


def computed(centers, widths, samples, chips, tables):
    return pl.pallas_call(
        compute_kernel,
        out_shape=[
            jax.ShapeDtypeStruct((SATS + 1, THI, 128, DOP), F32),
            jax.ShapeDtypeStruct((SATS, 8, 128), F32),
        ],
        in_specs=[pl.BlockSpec(memory_space=pltpu.HBM)] * (4 + len(tables)),
        out_specs=[vmem(), vmem()],
        scratch_shapes=[pltpu.VMEM(t.shape, t.dtype) for t in tables]
        + [
            pltpu.SMEM((SATS,), jnp.int32),
            pltpu.SMEM((SATS,), jnp.int32),
            pltpu.VMEM((128, 2, 64), F32),
            pltpu.VMEM((SATS, CHIPS), jnp.int32),
            pltpu.VMEM((96, 128), F32),
            pltpu.VMEM((SATS, 128, 256), F32),
            pltpu.VMEM((SATS, 2, KLO, 128), F32),
            pltpu.VMEM((KLO, 256, 256), BF16),
            pltpu.VMEM((KLO, 256, 256), BF16),
            pltpu.VMEM((256, 256), F32),
            pltpu.VMEM((8, 256, 256), F32),
            pltpu.VMEM((8, 256, 256), F32),
            pltpu.VMEM((2 * THI, 128, 256), F32),
            pltpu.VMEM((THI, 128, 256), F32),
            pltpu.VMEM((2, 256, 256), BF16),
            pltpu.VMEM((2, 256, 256), BF16),
            pltpu.SemaphoreType.DMA,
            pltpu.SemaphoreType.DMA((len(tables) + 3,)),
            pltpu.SemaphoreType.DMA((24,)),
            pltpu.SemaphoreType.DMA((24,)),
        ],
        compiler_params=pltpu.CompilerParams(vmem_limit_bytes=40 << 20, collective_id=0, has_side_effects=True,
        ),
        name="compute",
    )(centers, widths, samples, chips, *tables)


def finish_kernel(power_ref, mean_ref, out_ref, ratios, sem):
    r = lax.broadcasted_iota(jnp.int32, (DOP, DOP), 0)
    q = lax.broadcasted_iota(jnp.int32, (DOP, DOP), 1)
    gap = jnp.abs(r - q)
    copies = []
    for s in range(SATS):
        band = ((gap >= 2) & (gap.astype(F32) <= 1.0 + mean_ref[s, 1:2, :])).astype(F32)
        scale = 1.0 / jnp.sum(band, axis=0, keepdims=True)
        band = band.astype(BF16)
        band = jnp.concatenate([band, band], 0)
        floor = mean_ref[s, 0:1, :] * 0.25 + 1e-6
        for t in range(THI):
            power = power_ref[s, t]
            high, low = split(power)
            around = dot(jnp.concatenate([high, low], 1), band)
            ratio = power / (around * scale + floor)
            ratios[s, :, t * 128 : t * 128 + 128] = ratio.T
            if t % 4 == 3:
                part = pl.ds((t - 3) * 128, 512)
                copies.append(
                    pltpu.make_async_copy(
                        ratios.at[s, :, part], out_ref.at[s, :, part], sem.at[2 * s + t // 4]
                    )
                )
                copies[-1].start()
    for copy in copies:
        copy.wait()


def finished(power, mean):
    return pl.pallas_call(
        finish_kernel,
        out_shape=jax.ShapeDtypeStruct((SATS, DOP, THI * 128), F32),
        in_specs=[vmem(), vmem()],
        out_specs=pl.BlockSpec(memory_space=pl.ANY),
        scratch_shapes=[pltpu.VMEM((SATS, DOP, THI * 128), F32), pltpu.SemaphoreType.DMA((2 * SATS,))],
        compiler_params=pltpu.CompilerParams(vmem_limit_bytes=16 << 20),
        name="finish",
    )(power, mean)


def on_device(samples, code_chips, centers, widths):
    tables = build_tables()
    places = [centers, widths, samples, code_chips] + [jnp.asarray(tables[n]) for n in NAMES]
    places = [pltpu.with_memory_space_constraint(a, pltpu.HBM) for a in places]
    power, mean = computed(*places[:4], places[4:])
    return finished(power, mean)


def solution(mesh):
    both = ("sat", "dop")
    return jax.shard_map(
        on_device,
        mesh=mesh,
        in_specs=(P(None, both), P("sat", None), P("sat"), P("sat")),
        out_specs=P("sat", None, "dop"),
        check_vma=False,
    )
```

```python
import math

import jax
import jax.numpy as jnp
import numpy as np
from jax import lax
from jax.experimental import pallas as pl
from jax.experimental.pallas import tpu as pltpu
from jax.sharding import PartitionSpec as P

N = 8192
CHIPS = 4092
DOP = 128
SATS = 3
KLO = 64
KHI = 128
THI = 8
F32 = jnp.float32
BF16 = jnp.bfloat16
MESH = pl.DeviceIdType.MESH


def split_np(table):
    table = np.asarray(table, np.float32)
    high = table.astype(jnp.bfloat16)
    low = (table - high.astype(np.float32)).astype(jnp.bfloat16)
    return high, low


def split(value):
    high = value.astype(BF16)
    low = (value - high.astype(F32)).astype(BF16)
    return high, low


def dot(left, right):
    return jnp.dot(left, right, preferred_element_type=F32)


def phase(turns):
    return np.cos(2 * np.pi * turns), np.sin(2 * np.pi * turns)


def build_tables():
    out = {}
    kappa = np.arange(-32, 96)
    order = np.concatenate([np.arange(0, 64, 2), np.arange(1, 64, 2)])
    cos, sin = phase(-(kappa[:, None] * order[None, :] % 64) / 64)
    high, low = split_np(np.concatenate([cos, sin], 0))
    out["code_first"] = np.concatenate([high, low], 1)
    lanes = np.arange(128)
    out["code_twiddle"] = np.stack(phase(-(kappa[:, None] * lanes[None, :] % N) / N)).astype(np.float32)
    cos, sin = phase((lanes[:, None] * lanes[None, :] % 128) / 128)
    high, low = split_np(np.block([[cos, -sin], [sin, cos]]))
    out["right"] = np.stack([high, low])
    high, low = split_np(np.block([[cos, sin], [-sin, cos]]))
    out["left"] = np.stack([high, low])
    rho = np.arange(-64, 192)
    device = np.arange(128)
    cos, sin = phase(-((device[:, None] // 2) * rho[None, :] % 128) / 128)
    columns = []
    for parity in range(2):
        keep = (device % 2 == parity)[:, None]
        columns += [cos * keep, sin * keep]
    high, low = split_np(np.concatenate(columns, 1))
    out["signal_first"] = np.stack([high, low])
    out["signal_twiddle"] = np.stack(phase(-(lanes[:, None] * rho[None, :] % (2 * N)) / (2 * N))).astype(np.float32)
    out["inverse"] = np.stack(phase((lanes[:, None] * lanes[None, :] % 128) / 128)).astype(np.float32)
    step = phase(np.broadcast_to(lanes[:, None], (128, 128)) / N)
    out["step"] = np.stack(step).astype(np.float32)
    first = np.arange(256)[None, :] - 2 * np.arange(KLO)[:, None]
    out["window"] = ((first >= 0) & (first < 128)).astype(jnp.bfloat16)
    return out


NAMES = ["code_first", "code_twiddle", "right", "left", "signal_first", "signal_twiddle", "inverse", "step", "window"]


def eighth_turns(turns):
    half = jnp.where(turns >= 4, -1.0, 1.0)
    part = turns & 3
    cos = jnp.where(part == 0, 1.0, jnp.where(part == 1, EIGHTH, jnp.where(part == 2, 0.0, -EIGHTH)))
    sin = jnp.where(part == 0, 0.0, jnp.where(part == 2, 1.0, EIGHTH))
    return cos * half, sin * half


def code_part(centers_ref, chips_ref, dop, code_first, code_twiddle, right, chip_rows, spectrum, code):
    chip_rows[...] = jnp.zeros_like(chip_rows)
    for s in range(SATS):
        for a in range(32):
            width = 128 if a < 31 else CHIPS - 31 * 128
            chip_rows[pl.ds(s * 32 + a, 1), 0:width] = chips_ref[s : s + 1, a * 128 : a * 128 + width].astype(F32)
    rows = chip_rows[...]
    lane = lax.broadcasted_iota(jnp.int32, (96, 128), 1)
    index = lax.broadcasted_iota(jnp.int32, (96, 128), 0)
    turned = pltpu.roll(rows, 64, 1)
    above = pltpu.roll(turned, 1, 0)
    odd = jnp.where(lane < 64, above, turned)
    both = jnp.concatenate([odd, rows], 0).astype(BF16)
    sample = lax.broadcasted_iota(jnp.int32, (128, 128), 1)
    chip = lax.broadcasted_iota(jnp.int32, (128, 128), 0)
    kind = lax.broadcasted_iota(jnp.int32, (192, 128), 0) % 32 // 4
    replica = jnp.zeros((192, 128), F32)
    for i in range(8):
        shifted = sample + (7 - i)
        hit = chip == 60 + (shifted >> 1)
        sign = 1.0 - 2.0 * (shifted & 1).astype(F32)
        select = jnp.where(hit, sign, 0.0).astype(BF16)
        replica = jnp.where(kind == i, dot(both, select), replica)
    start = (lax.broadcasted_iota(jnp.int32, (192, 128), 0) < 96) & (
        lax.broadcasted_iota(jnp.int32, (192, 128), 0) % 4 == 0
    ) & (lax.broadcasted_iota(jnp.int32, (192, 128), 1) == 0)
    replica = jnp.where(start, pltpu.roll(replica, 127, 1), replica).astype(BF16)
    for s in range(SATS):
        part = jnp.concatenate([replica[s * 32 : s * 32 + 32], replica[96 + s * 32 : 128 + s * 32]], 0)
        stage = dot(code_first[...], jnp.concatenate([part, part], 0))
        re, im = stage[:128], stage[128:]
        cos, sin = code_twiddle[0], code_twiddle[1]
        turned = jnp.concatenate([re * cos - im * sin, im * cos + re * sin], 1)
        high, low = split(turned)
        spectrum[s] = dot(
            jnp.concatenate([high, low, high], 1),
            jnp.concatenate([right[0], right[0], right[1]], 0),
        )
    row = lax.broadcasted_iota(jnp.int32, (KLO, 128), 0)
    for s in range(SATS):
        block = dop if s == 2 else dop // 2 * 2
        cos, sin = eighth_turns(row * block & 7)
        cos, sin = cos * (1.0 / N), sin * (1.0 / N)
        shifted = pltpu.roll(spectrum[s], 96 + centers_ref[s], 0)[:KLO]
        re, im = shifted[:, :128], shifted[:, 128:256]
        code[s, 0] = re * cos + im * sin
        code[s, 1] = re * sin - im * cos


def table_part(code, own, inverse, step, left_high, left_low, first, last):
    def group(g, _):
        at = pl.multiple_of(g * 16, 16)
        rows = pl.ds(at, 16)
        step_re, step_im = step[0, rows, :], step[1, rows, :]

        def one(k, carry):
            e_re, e_im = carry
            for slot, s in ((0, own), (1, 2)):
                c_re = code[s, 0, pl.ds(k, 1), :]
                c_im = code[s, 1, pl.ds(k, 1), :]
                m_re = e_re * c_re - e_im * c_im
                m_im = e_re * c_im + e_im * c_re
                into = pl.ds(pl.multiple_of(slot * 128 + at, 16), 16)
                high, low = split(m_re)
                left_high[k, into, 0:128] = high
                left_low[k, into, 0:128] = low
                high, low = split(m_im)
                left_high[k, into, 128:256] = high
                left_low[k, into, 128:256] = low
            return e_re * step_re - e_im * step_im, e_re * step_im + e_im * step_re

        lax.fori_loop(0, KLO, one, (inverse[0, rows, :], inverse[1, rows, :]), unroll=4)
        return 0

    lax.fori_loop(first, last, group, 0)


def signal_part(rows, left, signal_first, signal_twiddle):
    turned = rows.T
    high, low = split(turned)
    stage = dot(
        jnp.concatenate([high, low, high], 1),
        jnp.concatenate([signal_first[0], signal_first[0], signal_first[1]], 0),
    )
    re, im = [], []
    for parity in range(2):
        cos = stage[:, parity * 512 : parity * 512 + 256]
        sin = stage[:, parity * 512 + 256 : parity * 512 + 512]
        re.append(cos[:64] - sin[64:])
        im.append(sin[:64] + cos[64:])
    re, im = jnp.concatenate(re, 0), jnp.concatenate(im, 0)
    cos, sin = signal_twiddle[0], signal_twiddle[1]
    both = jnp.concatenate([re * cos - im * sin, im * cos + re * sin], 0)
    high, low = split(both)
    return dot(
        jnp.concatenate([left[0], left[1], left[0]], 1),
        jnp.concatenate([high, high, low], 0),
    )


def mean_part(signal, window, code, widths, mean_ref):
    size = signal[0:128, :] * signal[0:128, :] + signal[128:256, :] * signal[128:256, :]
    high, low = split(size)
    under = lax.dot_general(
        jnp.concatenate([window[...], window[...]], 1),
        jnp.concatenate([high, low], 1),
        (((1,), (1,)), ((), ())),
        preferred_element_type=F32,
    )
    for s in range(SATS):
        re, im = code[s, 0], code[s, 1]
        total = jnp.sum(under * (re * re + im * im), axis=(0, 1), keepdims=True)
        mean = jnp.broadcast_to(total * (1.0 / (DOP * N)), (8, 128))
        width = jnp.full((8, 128), widths[s].astype(F32))
        mean_ref[s] = jnp.where(lax.broadcasted_iota(jnp.int32, (8, 128), 0) == 0, mean, width)


EIGHTH = math.sqrt(0.5)


def dft8(re, im):
    def add(a, b):
        return (a[0] + b[0], a[1] + b[1])

    def sub(a, b):
        return (a[0] - b[0], a[1] - b[1])

    def turn(a):
        return (-a[1], a[0])

    v = list(zip(re, im))

    def dft4(a, b, c, d):
        p, m = add(a, c), sub(a, c)
        q, n = add(b, d), turn(sub(b, d))
        return add(p, q), add(m, n), sub(p, q), sub(m, n)

    e = dft4(v[0], v[2], v[4], v[6])
    o = dft4(v[1], v[3], v[5], v[7])
    w1 = ((o[1][0] - o[1][1]) * EIGHTH, (o[1][0] + o[1][1]) * EIGHTH)
    w2 = turn(o[2])
    w3 = ((-o[3][0] - o[3][1]) * EIGHTH, (o[3][0] - o[3][1]) * EIGHTH)
    w = [o[0], w1, w2, w3]
    return [add(e[i], w[i]) for i in range(4)] + [sub(e[i], w[i]) for i in range(4)]


def windows(k, signal):
    lane = lax.broadcasted_iota(jnp.int32, (256, 128), 1)
    shift = 128 - 2 * k

    def embedded(i):
        part = jnp.where(
            lane < shift,
            pltpu.roll(signal[i, :, 0:128], shift, 1),
            pltpu.roll(signal[i, :, 128:256], shift, 1),
        )
        re, im = part[:128], part[128:]
        return jnp.concatenate([jnp.concatenate([re, im], 1), jnp.concatenate([-im, re], 1)], 0)

    return embedded(0), embedded(1)


def products(k, kap, factors, left_high, left_low, stage):
    high, low = factors
    m_high, m_low = left_high[k], left_low[k]
    stage[kap] = dot(jnp.concatenate([m_high, m_low, m_high], 1), jnp.concatenate([high, high, low], 0))


def combine(stage, total, slot, row, store=None, first=False):
    rows = pl.ds(row, 8)
    from_rows = pl.ds(slot * 128 + row, 8)
    re = [stage[kap, from_rows, 0:128] for kap in range(8)]
    im = [stage[kap, from_rows, 128:256] for kap in range(8)]
    out = dft8(re, im)
    for t in range(total.shape[0]):
        a, b = out[t % 8]
        if not first:
            c, d = total[t, rows, 0:128], total[t, rows, 128:256]
            cos, sin = math.cos(math.pi * t / 32), math.sin(math.pi * t / 32)
            if t == 8:
                c, d = (c - d) * EIGHTH, (c + d) * EIGHTH
            elif t:
                c, d = c * cos - d * sin, c * sin + d * cos
            a, b = a + c, b + d
        if store is None:
            total[t, rows, 0:128] = a
            total[t, rows, 128:256] = b
        else:
            store(t, rows, (a * a + b * b) * (1.0 / N))


def main_part(signal_full, left_high, left_low, even, odd, wide, narrow, power_ref, own, send, meanwhile, ready, pieces):
    def both(lam, fill, drain, first=False):
        for kap in range(8):
            k = lam + 8 * kap
            factors = windows(k, signal) if kap else (ready[0], ready[1])
            products(k, kap, factors, left_high, left_low, fill)
            for g in range(2):
                combine(drain, wide, 0, kap * 16 + g * 8, first=first)
                combine(drain, narrow, 1, kap * 16 + g * 8, first=first)
        ready[0], ready[1] = windows(jnp.maximum(lam - 1, 0), signal)

    signal = pieces
    signal[0], signal[1] = split(signal_full[...])
    for kap in range(8):
        products(7 + 8 * kap, kap, windows(7 + 8 * kap, signal), left_high, left_low, odd)
    ready[0], ready[1] = windows(6, signal)

    def step(i, _):
        @pl.when(i % 2 == 0)
        def _():
            both(6 - i, even, odd)

        @pl.when(i % 2 == 1)
        def _():
            both(6 - i, odd, even)

        return 0

    both(6, even, odd, first=True)
    lax.fori_loop(1, 7, step, 0)
    places = [jnp.where(own == half, own, 3) for half in range(2)]

    def keep_wide(t, rows, value):
        power_ref[places[t // 8], t % 8, rows, :] = value

    def keep_narrow(t, rows, value):
        power_ref[2, t, rows, :] = value

    def finish_wide(first, last):
        def one(c, _):
            combine(even, wide, 0, pl.multiple_of(c * 8, 8), keep_wide)
            return 0

        lax.fori_loop(first, last, one, 0, unroll=2)

    def finish_narrow(first, last):
        def one(c, _):
            combine(even, narrow, 1, pl.multiple_of(c * 8, 8), keep_narrow)
            return 0

        lax.fori_loop(first, last, one, 0, unroll=2)

    finish_wide(0, 8)
    finish_narrow(0, 2)
    copies = [send(0)]
    finish_wide(8, 16)
    finish_narrow(2, 4)
    copies.append(send(1))
    meanwhile()
    finish_narrow(4, 16)
    for copy in copies:
        copy.wait()


def compute_kernel(centers_hbm, widths_hbm, samples_ref, chips_hbm, *refs):
    count = len(NAMES)
    hbm = dict(zip(NAMES, refs[:count]))
    power_ref, mean_ref = refs[count : count + 2]
    refs = refs[count + 2 :]
    table = dict(zip(NAMES, refs[:count]))
    (centers, widths, gathered, chips, chip_rows, spectrum, code, left_high, left_low, signal, even, odd, wide, narrow, ready, pieces,
     own_sem, table_sem, send_sem, recv_sem) = refs[count:]
    sat = lax.axis_index("sat")
    dop = lax.axis_index("dop")
    x, z = sat // 4, sat % 4
    me = sat * 8 + dop
    own_sat = dop % 2
    barrier = pltpu.get_barrier_semaphore()
    y, core = dop // 2, dop % 2
    peers = []
    for step, other in ((2, 1), (2, 0), (1, 1), (1, 0), (3, 1), (3, 0), (0, 1)):
        peers.append({"sat": sat, "dop": (y + step) % 4 * 2 + (core + other) % 2})
    hops = (0, 1, 2, 1)
    steps = sorted(range(1, 16), key=lambda step: -(hops[step // 4] + hops[step % 4]))
    for step in steps:
        peers.append({"sat": (x + step // 4) % 4 * 4 + (z + step % 4) % 4, "dop": dop})
    for peer in peers[7:] + peers[:7]:
        pl.semaphore_signal(barrier, inc=1, device_id=peer, device_id_type=MESH)
    own = pltpu.make_async_copy(samples_ref, gathered.at[me], own_sem)
    own.start()
    loads = {"chips": pltpu.make_async_copy(chips_hbm, chips, table_sem.at[count])}
    loads["chips"].start()
    loads["centers"] = pltpu.make_async_copy(centers_hbm, centers, table_sem.at[count + 1])
    loads["centers"].start()
    loads["widths"] = pltpu.make_async_copy(widths_hbm, widths, table_sem.at[count + 2])
    loads["widths"].start()
    for i, name in enumerate(NAMES):
        loads[name] = pltpu.make_async_copy(hbm[name], table[name], table_sem.at[i])
        loads[name].start()

    def exchange(first, size, start, targets, source):
        copies = []
        for i, peer in enumerate(targets):
            copies.append(
                pltpu.make_async_remote_copy(
                    src_ref=source,
                    dst_ref=gathered.at[pl.ds(start, size)],
                    send_sem=send_sem.at[first + i],
                    recv_sem=recv_sem.at[first + i],
                    device_id=peer,
                    device_id_type=MESH,
                )
            )
            copies[-1].start()
        return copies

    for name in ("chips", "centers", "code_first", "code_twiddle", "right"):
        loads[name].wait()
    code_part(centers, chips, dop, table["code_first"], table["code_twiddle"], table["right"], chip_rows, spectrum, code)
    own.wait()
    pl.semaphore_wait(barrier, 22)
    copies = exchange(0, 1, me, peers[:7], gathered.at[pl.ds(me, 1)])
    for name in ("widths", "inverse", "step", "left", "signal_first", "signal_twiddle", "window"):
        loads[name].wait()
    table_part(code, own_sat, table["inverse"], table["step"], left_high, left_low, 0, 3)
    for copy in copies:
        copy.wait()
    copies = exchange(7, 8, sat * 8, peers[7:], gathered.at[pl.ds(sat * 8, 8)])
    table_part(code, own_sat, table["inverse"], table["step"], left_high, left_low, 3, 8)
    for copy in copies:
        copy.wait()
    rows = jnp.concatenate([gathered[:, 0, :], gathered[:, 1, :]], 1)
    signal[...] = signal_part(rows, table["left"], table["signal_first"], table["signal_twiddle"])

    def send(half):
        rows = pl.ds(half * 64, 64)
        copy = pltpu.make_async_remote_copy(
            src_ref=power_ref.at[3, :, rows],
            dst_ref=power_ref.at[own_sat, :, rows],
            send_sem=send_sem.at[22 + half],
            recv_sem=recv_sem.at[22 + half],
            device_id={"sat": sat, "dop": dop + 1 - 2 * own_sat},
            device_id_type=MESH,
        )
        copy.start()
        return copy

    main_part(signal, left_high, left_low, even, odd, wide, narrow, power_ref, own_sat, send,
              lambda: mean_part(signal, table["window"], code, widths, mean_ref), ready, pieces)


def vmem():
    return pl.BlockSpec(memory_space=pltpu.VMEM)


def computed(centers, widths, samples, chips, tables):
    return pl.pallas_call(
        compute_kernel,
        out_shape=[
            jax.ShapeDtypeStruct((SATS + 1, THI, 128, DOP), F32),
            jax.ShapeDtypeStruct((SATS, 8, 128), F32),
        ],
        in_specs=[pl.BlockSpec(memory_space=pltpu.HBM)] * (4 + len(tables)),
        out_specs=[vmem(), vmem()],
        scratch_shapes=[pltpu.VMEM(t.shape, t.dtype) for t in tables]
        + [
            pltpu.SMEM((SATS,), jnp.int32),
            pltpu.SMEM((SATS,), jnp.int32),
            pltpu.VMEM((128, 2, 64), F32),
            pltpu.VMEM((SATS, CHIPS), jnp.int32),
            pltpu.VMEM((96, 128), F32),
            pltpu.VMEM((SATS, 128, 256), F32),
            pltpu.VMEM((SATS, 2, KLO, 128), F32),
            pltpu.VMEM((KLO, 256, 256), BF16),
            pltpu.VMEM((KLO, 256, 256), BF16),
            pltpu.VMEM((256, 256), F32),
            pltpu.VMEM((8, 256, 256), F32),
            pltpu.VMEM((8, 256, 256), F32),
            pltpu.VMEM((2 * THI, 128, 256), F32),
            pltpu.VMEM((THI, 128, 256), F32),
            pltpu.VMEM((2, 256, 256), BF16),
            pltpu.VMEM((2, 256, 256), BF16),
            pltpu.SemaphoreType.DMA,
            pltpu.SemaphoreType.DMA((len(tables) + 3,)),
            pltpu.SemaphoreType.DMA((24,)),
            pltpu.SemaphoreType.DMA((24,)),
        ],
        compiler_params=pltpu.CompilerParams(vmem_limit_bytes=40 << 20, collective_id=0, has_side_effects=True,
        ),
        name="compute",
    )(centers, widths, samples, chips, *tables)


def finish_kernel(power_ref, mean_ref, out_ref, ratios, sem):
    r = lax.broadcasted_iota(jnp.int32, (DOP, DOP), 0)
    q = lax.broadcasted_iota(jnp.int32, (DOP, DOP), 1)
    gap = jnp.abs(r - q)
    copies = []
    for s in range(SATS):
        band = ((gap >= 2) & (gap.astype(F32) <= 1.0 + mean_ref[s, 1:2, :])).astype(F32)
        scale = 1.0 / jnp.sum(band, axis=0, keepdims=True)
        band = band.astype(BF16)
        band = jnp.concatenate([band, band], 0)
        floor = mean_ref[s, 0:1, :] * 0.25 + 1e-6
        for t in range(THI):
            power = power_ref[s, t]
            high, low = split(power)
            around = dot(jnp.concatenate([high, low], 1), band)
            ratio = power / (around * scale + floor)
            ratios[s, :, t * 128 : t * 128 + 128] = ratio.T
            if t % 4 == 3:
                part = pl.ds((t - 3) * 128, 512)
                copies.append(
                    pltpu.make_async_copy(
                        ratios.at[s, :, part], out_ref.at[s, :, part], sem.at[2 * s + t // 4]
                    )
                )
                copies[-1].start()
    for copy in copies:
        copy.wait()


def finished(power, mean):
    return pl.pallas_call(
        finish_kernel,
        out_shape=jax.ShapeDtypeStruct((SATS, DOP, THI * 128), F32),
        in_specs=[vmem(), vmem()],
        out_specs=pl.BlockSpec(memory_space=pl.ANY),
        scratch_shapes=[pltpu.VMEM((SATS, DOP, THI * 128), F32), pltpu.SemaphoreType.DMA((2 * SATS,))],
        compiler_params=pltpu.CompilerParams(
            vmem_limit_bytes=16 << 20
        ),
        name="finish",
    )(power, mean)


def on_device(samples, code_chips, centers, widths):
    tables = build_tables()
    places = [centers, widths, samples, code_chips] + [jnp.asarray(tables[n]) for n in NAMES]
    places = [pltpu.with_memory_space_constraint(a, pltpu.HBM) for a in places]
    power, mean = computed(*places[:4], places[4:])
    return finished(power, mean)


def solution(mesh):
    both = ("sat", "dop")
    return jax.shard_map(
        on_device,
        mesh=mesh,
        in_specs=(P(None, both), P("sat", None), P("sat"), P("sat")),
        out_specs=P("sat", None, "dop"),
        check_vma=False,
    )
```
